256 devices in a mesh: own: 2 (over y_hi), space: 128 (over z, x, y_lo, core).
Axes of the slice: x: 4, y: 4 (y_hi: 2, y_lo: 2; y = y_hi * 2 + y_lo), z: 8, core: 2. Of those that a mesh axis runs over, the one named last changes fastest.
Arguments:
- density: bfloat16 [256, 4, 512, 128], P(None, 'own', 'space'), may hold values from -6 to 6
- cotangent: bfloat16 [256, 4, 512, 128], P(None, 'own', 'space'), may hold values from -6 to 6
- pw_one: bfloat16 [256, 256], P('own'), may hold values from -0.375 to 0.375
- pw_two: bfloat16 [256, 256], P('own'), may hold values from -0.375 to 0.375
- dw_one: bfloat16 [27, 256], P(None, 'own'), may hold values from -1.25 to 1.25
- dw_two: bfloat16 [27, 256], P(None, 'own'), may hold values from -1.25 to 1.25
Outputs:
- grad_input: bfloat16 [256, 4, 512, 128], P(None, 'own', 'space')
- grad_pw_one: float32 [256, 256], P('own')
- grad_pw_two: float32 [256, 256], P('own')
- grad_dw_one: float32 [27, 256], P(None, 'own')
- grad_dw_two: float32 [27, 256], P(None, 'own')
The draws below stay inside these ranges and needn't reach their ends.
All inputs are finite; a program needn't handle non-finite values.
Results may differ from the reference program's by a relative error of at most 0.01.
Values may be sent and summed in bfloat16 or wider, within the bound.
A program may use at most 192 MiB of HBM per device.

```python
import math
import jax
import jax.numpy as jnp
from jax import lax

C = 256
NX = 4
NY = 512
NZ = 128


def shard_levels(own_key, dims, split, smallest, top_value):
    level = 1.0
    for dim, shards_of in split:
        heights = jax.random.uniform(jax.random.fold_in(jax.random.fold_in(own_key, 6), dim), (shards_of,), jnp.float32, smallest / len(split), top_value / len(split))
        level = level * jnp.repeat(jnp.exp(heights), dims[dim] // shards_of).reshape((-1,) + (1,) * (len(dims) - 1 - dim))
    return level


def centred(stream_key, shape, deviation, most, split=(), held_as=jnp.bfloat16):
    loudness = shard_levels(stream_key, shape, split, -0.22, 0.18) if split else 1.0
    array = jax.random.normal(stream_key, shape, jnp.float32) * deviation * loudness
    return jnp.minimum(jnp.maximum(array, -most), most).astype(held_as)


def setup_inputs(seed: int = 0) -> dict:
    key_list = jax.random.split(jax.random.key(seed), 7)
    return {
        "density": centred(key_list[0], (C, NX, NY, NZ), 1.0, 6.0, ((1, 2), (2, 128))),
        "cotangent": centred(key_list[1], (C, NX, NY, NZ), 1.0, 6.0, ((1, 2), (2, 128))),
        "pw_one": centred(key_list[2], (C, C), C ** -0.5, 0.375, ((0, 2),)),
        "pw_two": centred(key_list[3], (C, C), C ** -0.5, 0.375, ((0, 2),)),
        "dw_one": centred(key_list[4], (27, C), 27 ** -0.5, 1.25, ((1, 2),)),
        "dw_two": centred(key_list[5], (27, C), 27 ** -0.5, 1.25, ((1, 2),)),
    }


TAP_LIST = [(9 * (a + 1) + 3 * (b + 1) + (d + 1), a, b, d) for a in (-1, 0, 1) for b in (-1, 0, 1) for d in (-1, 0, 1)]

def depthwise_ref(source, weights, direction):
    groups = C // 16

    def per_group(operands):
        channel_block, weight_block = operands
        running = jnp.zeros(channel_block.shape, jnp.float32)
        for k, a, b, d in TAP_LIST:
            shifted = jnp.roll(channel_block, (-direction * a, -direction * b, -direction * d), (1, 2, 3))
            running = running + weight_block[:, k].astype(jnp.float32)[:, None, None, None] * shifted.astype(jnp.float32)
        return running
    output = lax.map(per_group, (source.reshape(groups, 16, NX, NY, NZ), weights.T.reshape(groups, 16, 27)))
    return output.reshape(C, NX, NY, NZ)

def tap_ref(source, gradient):
    groups = C // 16

    def per_group(operands):
        channel_block, grad_block = operands
        grad_float = grad_block.astype(jnp.float32)
        columns = []
        for k, a, b, d in TAP_LIST:
            shifted = jnp.roll(channel_block, (-a, -b, -d), (1, 2, 3)).astype(jnp.float32)
            columns.append(lax.optimization_barrier(jnp.sum(shifted * grad_float, axis=(1, 2, 3))))
        return jnp.stack(columns, axis=1)
    output = lax.map(per_group, (source.reshape(groups, 16, NX, NY, NZ), gradient.reshape(groups, 16, NX, NY, NZ)))
    return output.reshape(C, 27).T

def contract_cells(left, right):
    return lax.dot_general(left.reshape(C, -1), right.reshape(C, -1), (((1,), (1,)), ((), ())), preferred_element_type=jnp.float32)

def reference(density, cotangent, pw_one, pw_two, dw_one, dw_two):
    grad_scale = 1.0 / math.sqrt(float(NX * NY * NZ))
    first = depthwise_ref(density, dw_one, 1).astype(jnp.bfloat16)
    pre = jnp.dot(pw_one.T, first.reshape(C, -1), preferred_element_type=jnp.float32).reshape(C, NX, NY, NZ)
    act = jax.nn.silu(pre).astype(jnp.bfloat16)
    second = depthwise_ref(act, dw_two, 1).astype(jnp.bfloat16)
    grad_second = jnp.dot(pw_two, cotangent.reshape(C, -1), preferred_element_type=jnp.float32).reshape(C, NX, NY, NZ).astype(jnp.bfloat16)
    sigma = jax.nn.sigmoid(pre)
    grad_pre = (depthwise_ref(grad_second, dw_two, -1) * (sigma * (1.0 + pre * (1.0 - sigma)))).astype(jnp.bfloat16)
    grad_first = jnp.dot(pw_one, grad_pre.reshape(C, -1), preferred_element_type=jnp.float32).reshape(C, NX, NY, NZ).astype(jnp.bfloat16)
    grad_input = (cotangent.astype(jnp.float32) + depthwise_ref(grad_first, dw_one, -1)).astype(jnp.bfloat16)
    grad_pw_two = contract_cells(second, cotangent) * grad_scale
    grad_pw_one = contract_cells(first, grad_pre) * grad_scale
    grad_dw_two = tap_ref(act, grad_second) * grad_scale
    grad_dw_one = tap_ref(density, grad_first) * grad_scale
    return (grad_input, grad_pw_one, grad_pw_two, grad_dw_one, grad_dw_two)
```

```python
import functools
import math

import jax
import jax.numpy as jnp
from jax import lax
from jax.experimental import pallas as pl
from jax.experimental.pallas import tpu as pltpu
from jax.sharding import PartitionSpec as P

MESH = pl.DeviceIdType.MESH
TILE = 8 * 128

TAP_LIST = [
    (9 * (a + 1) + 3 * (b + 1) + (d + 1), a, b, d)
    for a in (-1, 0, 1)
    for b in (-1, 0, 1)
    for d in (-1, 0, 1)
]


def extended(value, sides, width):
    for axis, dim in sides:
        size, length = (lax.axis_size(axis), value.shape[dim])
        up = [(i, (i + 1) % size) for i in range(size)]
        down = [(j, i) for i, j in up]
        last = lax.slice_in_dim(value, length - width, length, axis=dim)
        first = lax.slice_in_dim(value, 0, width, axis=dim)
        before = lax.ppermute(last, axis, up)
        after = lax.ppermute(first, axis, down)
        value = jnp.concatenate([before, value, after], axis=dim)
    return value


def depthwise(padded, weights, extent_x, extent_y, direction):
    running = jnp.zeros((padded.shape[0], extent_x, extent_y, padded.shape[3]), jnp.float32)
    for k, a, b, d in TAP_LIST:
        start_x = 1 + direction * a
        start_y = 1 + direction * b
        shifted = padded[:, start_x : start_x + extent_x, start_y : start_y + extent_y, :]
        shifted = jnp.roll(shifted, -direction * d, axis=3).astype(jnp.float32)
        running = running + weights[k].astype(jnp.float32)[:, None, None, None] * shifted
    return running


def tap_sums(padded, gradient):
    extent_x = gradient.shape[1]
    extent_y = gradient.shape[2]
    grad_float = gradient.astype(jnp.float32)
    columns = []
    for k, a, b, d in TAP_LIST:
        shifted = padded[:, 1 + a : 1 + a + extent_x, 1 + b : 1 + b + extent_y, :]
        shifted = jnp.roll(shifted, -d, axis=3).astype(jnp.float32)
        columns.append(jnp.sum(shifted * grad_float, axis=(1, 2, 3)))
    return jnp.stack(columns, axis=0)


def pointwise(weights, source):
    layout = source.shape
    flattened = source.reshape(layout[0], -1)
    return jnp.dot(weights.T, flattened, preferred_element_type=jnp.float32).reshape(layout)


def backmap(weights, source):
    layout = source.shape
    flattened = source.reshape(layout[0], -1)
    return jnp.dot(weights, flattened, preferred_element_type=jnp.float32).reshape(layout)


def contract_cells(left, right):
    channels = left.shape[0]
    return lax.dot_general(
        left.reshape(channels, -1),
        right.reshape(channels, -1),
        (((1,), (1,)), ((), ())),
        preferred_element_type=jnp.float32,
    )


def reduce_plan(space_size):
    if space_size == 128:
        scatter = (("own", 0, 2), ("space", 1, 2), ("space", 2, 2), ("space", 4, 4))
        return scatter, ("space", 16, 8)
    factors, stride, rest = [], 1, space_size
    while rest > 2:
        factors.append(("space", stride, 2))
        stride, rest = stride * 2, rest // 2
    return (("own", 0, 2),) + tuple(factors), ("space", stride, rest)


def reduce_kernel(plan, x_ref, o_ref, *refs):
    scatter, last = plan
    count = len(scatter)
    bufs = refs[:count]
    recvs = refs[count : 2 * count]
    recv_last, res, send_sem, recv_sem = refs[2 * count :]
    own = lax.axis_index("own")
    space = lax.axis_index("space")

    def coord(stage):
        axis, stride, size = stage
        return own if axis == "own" else (space // stride) % size

    def device(stage, target):
        axis, stride, size = stage
        if axis == "own":
            return (target, space)
        return (own, space + (target - coord(stage)) * stride)

    barrier = pltpu.get_barrier_semaphore()
    partners = 0
    for stage in scatter + (last,):
        size, me = stage[2], coord(stage)
        for d in range(1, size):
            pl.semaphore_signal(
                barrier, 1, device_id=device(stage, (me + d) % size), device_id_type=MESH
            )
            partners += 1
    pl.semaphore_wait(barrier, partners)

    base = 0
    source = x_ref
    for i, stage in enumerate(scatter):
        size, me = stage[2], coord(stage)
        piece = source.shape[0] // size
        sends = []
        for d in range(1, size):
            target = (me + d) % size
            copy = pltpu.make_async_remote_copy(
                src_ref=source.at[pl.ds(target * piece, piece)],
                dst_ref=recvs[i].at[me],
                send_sem=send_sem.at[base + target],
                recv_sem=recv_sem.at[base + me],
                device_id=device(stage, target),
                device_id_type=MESH,
            )
            copy.start()
            sends.append(copy)
        for d in range(1, size):
            sender = (me + d) % size
            pltpu.make_async_remote_copy(
                src_ref=source.at[pl.ds(0, piece)],
                dst_ref=recvs[i].at[sender],
                send_sem=send_sem.at[base + sender],
                recv_sem=recv_sem.at[base + sender],
                device_id=device(stage, sender),
                device_id_type=MESH,
            ).wait_recv()
        for copy in sends:
            copy.wait_send()
        total = source[pl.ds(me * piece, piece)]
        for d in range(1, size):
            total = total + recvs[i][(me + d) % size]
        bufs[i][...] = total
        source = bufs[i]
        base += size

    size, me = last[2], coord(last)
    piece = source.shape[0]
    sends = []
    for d in range(1, size):
        target = (me + d) % size
        copy = pltpu.make_async_remote_copy(
            src_ref=source,
            dst_ref=recv_last.at[me],
            send_sem=send_sem.at[base + target],
            recv_sem=recv_sem.at[base + me],
            device_id=device(last, target),
            device_id_type=MESH,
        )
        copy.start()
        sends.append(copy)
    recv_last[me] = source[...]
    for d in range(1, size):
        sender = (me + d) % size
        pltpu.make_async_remote_copy(
            src_ref=source,
            dst_ref=recv_last.at[sender],
            send_sem=send_sem.at[base + sender],
            recv_sem=recv_sem.at[base + sender],
            device_id=device(last, sender),
            device_id_type=MESH,
        ).wait_recv()
    for copy in sends:
        copy.wait_send()
    total = recv_last[0]
    for k in range(1, size):
        total = total + recv_last[k]
    block = 0
    for stage in scatter[1:]:
        block = block * stage[2] + coord(stage)
    res[pl.ds(block * piece, piece)] = total
    base += size

    span = piece
    for j in range(len(scatter) - 1, 0, -1):
        stage = scatter[j]
        size, me = stage[2], coord(stage)
        prefix = 0
        for earlier in scatter[1:j]:
            prefix = prefix * earlier[2] + coord(earlier)
        group = prefix * size * span
        sends = []
        for d in range(1, size):
            target = (me + d) % size
            mine = res.at[pl.ds(group + me * span, span)]
            copy = pltpu.make_async_remote_copy(
                src_ref=mine,
                dst_ref=mine,
                send_sem=send_sem.at[base + target],
                recv_sem=recv_sem.at[base + me],
                device_id=device(stage, target),
                device_id_type=MESH,
            )
            copy.start()
            sends.append(copy)
        for d in range(1, size):
            sender = (me + d) % size
            theirs = res.at[pl.ds(group + sender * span, span)]
            pltpu.make_async_remote_copy(
                src_ref=theirs,
                dst_ref=theirs,
                send_sem=send_sem.at[base + sender],
                recv_sem=recv_sem.at[base + sender],
                device_id=device(stage, sender),
                device_id_type=MESH,
            ).wait_recv()
        for copy in sends:
            copy.wait_send()
        span *= size
        base += size
    o_ref[...] = res[...]


def tree_reduce(packed):
    plan = reduce_plan(lax.axis_size("space"))
    scatter, last = plan
    half = packed.shape[0] // 2
    shapes, length = [], packed.shape[0]
    for stage in scatter:
        length //= stage[2]
        shapes.append((stage[2], length))
    semaphores = sum(stage[2] for stage in scatter) * 2 + last[2]
    scratch = [pltpu.VMEM((n, 8, 128), jnp.float32) for _, n in shapes]
    scratch += [pltpu.VMEM((size, n, 8, 128), jnp.float32) for size, n in shapes]
    scratch += [
        pltpu.VMEM((last[2], length, 8, 128), jnp.float32),
        pltpu.VMEM((half, 8, 128), jnp.float32),
        pltpu.SemaphoreType.DMA((semaphores,)),
        pltpu.SemaphoreType.DMA((semaphores,)),
    ]
    return pl.pallas_call(
        functools.partial(reduce_kernel, plan),
        out_shape=jax.ShapeDtypeStruct((half, 8, 128), jnp.float32),
        in_specs=[pl.BlockSpec(memory_space=pltpu.VMEM)],
        out_specs=pl.BlockSpec(memory_space=pltpu.VMEM),
        scratch_shapes=scratch,
        compiler_params=pltpu.CompilerParams(collective_id=0, has_side_effects=True),
    )(packed)


def pack_halves(parts, blocks):
    halves = []
    for h in range(2):
        pieces = []
        for p in parts[:2]:
            rows = p.shape[0] // 2
            pieces.append(p[h * rows : (h + 1) * rows].reshape(-1))
        for p in parts[2:]:
            cols = p.shape[1] // 2
            pieces.append(p[:, h * cols : (h + 1) * cols].reshape(-1))
        halves.append(jnp.concatenate(pieces))
    real = halves[0].shape[0]
    tiles = -(-real // (TILE * blocks)) * blocks
    flat = jnp.stack(halves)
    flat = jnp.pad(flat, ((0, 0), (0, tiles * TILE - real)))
    return flat.reshape(2 * tiles, 8, 128), real


def unpack_half(reduced, parts):
    flat = reduced.reshape(-1)
    out, offset = [], 0
    for p in parts[:2]:
        shape = (p.shape[0] // 2, p.shape[1])
        out.append(flat[offset : offset + shape[0] * shape[1]].reshape(shape))
        offset += shape[0] * shape[1]
    for p in parts[2:]:
        shape = (p.shape[0], p.shape[1] // 2)
        out.append(flat[offset : offset + shape[0] * shape[1]].reshape(shape))
        offset += shape[0] * shape[1]
    return out


def shards(density, cotangent, pw_one, pw_two, dw_one, dw_two):
    channels, extent_x, extent_y, extent_z = density.shape
    weight_one, weight_two, taps_one, taps_two = (
        lax.all_gather(pw_one, "own", axis=0, tiled=True),
        lax.all_gather(pw_two, "own", axis=0, tiled=True),
        lax.all_gather(dw_one, "own", axis=1, tiled=True),
        lax.all_gather(dw_two, "own", axis=1, tiled=True),
    )
    rim_width = 1
    wide_input = extended(density, (("own", 1), ("space", 2)), rim_width)
    first = depthwise(wide_input, taps_one, extent_x, extent_y, 1).astype(jnp.bfloat16)
    pre = pointwise(weight_one, first)
    act = jax.nn.silu(pre).astype(jnp.bfloat16)
    act_padded = extended(act, (("own", 1), ("space", 2)), 1)
    second = depthwise(act_padded, taps_two, extent_x, extent_y, 1).astype(jnp.bfloat16)
    grad_second = backmap(weight_two, cotangent).astype(jnp.bfloat16)
    second_padded = extended(grad_second, (("own", 1), ("space", 2)), 1)
    sigma = jax.nn.sigmoid(pre)
    grad_pre = (
        depthwise(second_padded, taps_two, extent_x, extent_y, -1)
        * (sigma * (1.0 + pre * (1.0 - sigma)))
    ).astype(jnp.bfloat16)
    grad_first = backmap(weight_one, grad_pre).astype(jnp.bfloat16)
    first_padded = extended(grad_first, (("own", 1), ("space", 2)), 1)
    grad_input = (
        cotangent.astype(jnp.float32) + depthwise(first_padded, taps_one, extent_x, extent_y, -1)
    ).astype(jnp.bfloat16)
    total_cells = extent_x * extent_y * extent_z * lax.axis_size("own") * lax.axis_size("space")
    grad_scale = 1.0 / math.sqrt(float(total_cells))
    local_pw_one = contract_cells(first, grad_pre) * grad_scale
    local_pw_two = contract_cells(second, cotangent) * grad_scale
    local_dw_one = tap_sums(wide_input, grad_first) * grad_scale
    local_dw_two = tap_sums(act_padded, grad_second) * grad_scale
    partials = (local_pw_one, local_pw_two, local_dw_one, local_dw_two)
    scatter, _ = reduce_plan(lax.axis_size("space"))
    blocks = 1
    for stage in scatter[1:]:
        blocks *= stage[2]
    packed, _ = pack_halves(partials, blocks)
    result = unpack_half(tree_reduce(packed), partials)
    return (grad_input, result[0], result[1], result[2], result[3])


def solution(mesh):
    in_specs = (
        P(None, "own", "space", None),
        P(None, "own", "space", None),
        P("own", None),
        P("own", None),
        P(None, "own"),
        P(None, "own"),
    )
    out_specs = (
        P(None, "own", "space", None),
        P("own", None),
        P("own", None),
        P(None, "own"),
        P(None, "own"),
    )
    return jax.shard_map(shards, mesh=mesh, in_specs=in_specs, out_specs=out_specs, check_vma=False)
```

```python
import functools
import math

import jax
import jax.numpy as jnp
from jax import lax
from jax.experimental import pallas as pl
from jax.experimental.pallas import tpu as pltpu
from jax.sharding import PartitionSpec as P

MESH = pl.DeviceIdType.MESH
TILE = 8 * 128

TAP_LIST = [
    (9 * (a + 1) + 3 * (b + 1) + (d + 1), a, b, d)
    for a in (-1, 0, 1)
    for b in (-1, 0, 1)
    for d in (-1, 0, 1)
]


def extended(value, sides, width):
    for axis, dim in sides:
        size, length = (lax.axis_size(axis), value.shape[dim])
        up = [(i, (i + 1) % size) for i in range(size)]
        down = [(j, i) for i, j in up]
        last = lax.slice_in_dim(value, length - width, length, axis=dim)
        first = lax.slice_in_dim(value, 0, width, axis=dim)
        if size == 2:
            theirs = lax.ppermute(jnp.concatenate([first, last], axis=dim), axis, up)
            after = lax.slice_in_dim(theirs, 0, width, axis=dim)
            before = lax.slice_in_dim(theirs, width, 2 * width, axis=dim)
        else:
            before = lax.ppermute(last, axis, up)
            after = lax.ppermute(first, axis, down)
        value = jnp.concatenate([before, value, after], axis=dim)
    return value


def gather_weights(pw_one, pw_two, dw_one, dw_two):
    mine = jnp.concatenate([pw_one.reshape(-1), pw_two.reshape(-1), dw_one.reshape(-1), dw_two.reshape(-1)])
    theirs = lax.ppermute(mine, "own", [(0, 1), (1, 0)])
    first_half = lax.axis_index("own") == 0
    low = jnp.where(first_half, mine, theirs)
    high = jnp.where(first_half, theirs, mine)
    out, offset = [], 0
    for w, dim in ((pw_one, 0), (pw_two, 0), (dw_one, 1), (dw_two, 1)):
        count = w.size
        parts = [h[offset : offset + count].reshape(w.shape) for h in (low, high)]
        out.append(jnp.concatenate(parts, axis=dim))
        offset += count
    return out


def depthwise(padded, weights, extent_x, extent_y, direction):
    running = jnp.zeros((padded.shape[0], extent_x, extent_y, padded.shape[3]), jnp.float32)
    for k, a, b, d in TAP_LIST:
        start_x = 1 + direction * a
        start_y = 1 + direction * b
        shifted = padded[:, start_x : start_x + extent_x, start_y : start_y + extent_y, :]
        shifted = jnp.roll(shifted, -direction * d, axis=3).astype(jnp.float32)
        running = running + weights[k].astype(jnp.float32)[:, None, None, None] * shifted
    return running


def tap_sums(padded, gradient):
    extent_x = gradient.shape[1]
    extent_y = gradient.shape[2]
    grad_float = gradient.astype(jnp.float32)
    columns = []
    for k, a, b, d in TAP_LIST:
        shifted = padded[:, 1 + a : 1 + a + extent_x, 1 + b : 1 + b + extent_y, :]
        shifted = jnp.roll(shifted, -d, axis=3).astype(jnp.float32)
        columns.append(jnp.sum(shifted * grad_float, axis=(1, 2, 3)))
    return jnp.stack(columns, axis=0)


def pointwise(weights, source):
    layout = source.shape
    flattened = source.reshape(layout[0], -1)
    return jnp.dot(weights.T, flattened, preferred_element_type=jnp.float32).reshape(layout)


def backmap(weights, source):
    layout = source.shape
    flattened = source.reshape(layout[0], -1)
    return jnp.dot(weights, flattened, preferred_element_type=jnp.float32).reshape(layout)


def contract_cells(left, right):
    channels = left.shape[0]
    return lax.dot_general(
        left.reshape(channels, -1),
        right.reshape(channels, -1),
        (((1,), (1,)), ((), ())),
        preferred_element_type=jnp.float32,
    )


def reduce_plan(space_size):
    if space_size == 128:
        scatter = (("own", 0, 2), ("space", 1, 2), ("space", 2, 2), ("space", 4, 4))
        return scatter, ("space", 16, 8)
    factors, stride, rest = [], 1, space_size
    while rest > 2:
        factors.append(("space", stride, 2))
        stride, rest = stride * 2, rest // 2
    return (("own", 0, 2),) + tuple(factors), ("space", stride, rest)


def reduce_kernel(plan, x_ref, o_ref, *refs):
    scatter, last = plan
    count = len(scatter)
    bufs = refs[:count]
    recvs = refs[count : 2 * count]
    recv_last, res, send_sem, recv_sem = refs[2 * count :]
    own = lax.axis_index("own")
    space = lax.axis_index("space")

    def coord(stage):
        axis, stride, size = stage
        return own if axis == "own" else (space // stride) % size

    def device(stage, target):
        axis, stride, size = stage
        if axis == "own":
            return (target, space)
        return (own, space + (target - coord(stage)) * stride)

    barrier = pltpu.get_barrier_semaphore()
    partners = 0
    for stage in scatter + (last,):
        size, me = stage[2], coord(stage)
        for d in range(1, size):
            pl.semaphore_signal(
                barrier, 1, device_id=device(stage, (me + d) % size), device_id_type=MESH
            )
            partners += 1
    pl.semaphore_wait(barrier, partners)

    base = 0
    source = x_ref
    for i, stage in enumerate(scatter):
        size, me = stage[2], coord(stage)
        piece = source.shape[0] // size
        sends = []
        for d in range(1, size):
            target = (me + d) % size
            copy = pltpu.make_async_remote_copy(
                src_ref=source.at[pl.ds(target * piece, piece)],
                dst_ref=recvs[i].at[me],
                send_sem=send_sem.at[base + target],
                recv_sem=recv_sem.at[base + me],
                device_id=device(stage, target),
                device_id_type=MESH,
            )
            copy.start()
            sends.append(copy)
        for d in range(1, size):
            sender = (me + d) % size
            pltpu.make_async_remote_copy(
                src_ref=source.at[pl.ds(0, piece)],
                dst_ref=recvs[i].at[sender],
                send_sem=send_sem.at[base + sender],
                recv_sem=recv_sem.at[base + sender],
                device_id=device(stage, sender),
                device_id_type=MESH,
            ).wait_recv()
        for copy in sends:
            copy.wait_send()
        total = source[pl.ds(me * piece, piece)]
        for d in range(1, size):
            total = total + recvs[i][(me + d) % size]
        bufs[i][...] = total
        source = bufs[i]
        base += size

    size, me = last[2], coord(last)
    piece = source.shape[0]
    sends = []
    for d in range(1, size):
        target = (me + d) % size
        copy = pltpu.make_async_remote_copy(
            src_ref=source,
            dst_ref=recv_last.at[me],
            send_sem=send_sem.at[base + target],
            recv_sem=recv_sem.at[base + me],
            device_id=device(last, target),
            device_id_type=MESH,
        )
        copy.start()
        sends.append(copy)
    recv_last[me] = source[...]
    for d in range(1, size):
        sender = (me + d) % size
        pltpu.make_async_remote_copy(
            src_ref=source,
            dst_ref=recv_last.at[sender],
            send_sem=send_sem.at[base + sender],
            recv_sem=recv_sem.at[base + sender],
            device_id=device(last, sender),
            device_id_type=MESH,
        ).wait_recv()
    for copy in sends:
        copy.wait_send()
    total = recv_last[0]
    for k in range(1, size):
        total = total + recv_last[k]
    block = 0
    for stage in scatter[1:]:
        block = block * stage[2] + coord(stage)
    res[pl.ds(block * piece, piece)] = total
    base += size

    span = piece
    for j in range(len(scatter) - 1, 0, -1):
        stage = scatter[j]
        size, me = stage[2], coord(stage)
        prefix = 0
        for earlier in scatter[1:j]:
            prefix = prefix * earlier[2] + coord(earlier)
        group = prefix * size * span
        sends = []
        for d in range(1, size):
            target = (me + d) % size
            mine = res.at[pl.ds(group + me * span, span)]
            copy = pltpu.make_async_remote_copy(
                src_ref=mine,
                dst_ref=mine,
                send_sem=send_sem.at[base + target],
                recv_sem=recv_sem.at[base + me],
                device_id=device(stage, target),
                device_id_type=MESH,
            )
            copy.start()
            sends.append(copy)
        for d in range(1, size):
            sender = (me + d) % size
            theirs = res.at[pl.ds(group + sender * span, span)]
            pltpu.make_async_remote_copy(
                src_ref=theirs,
                dst_ref=theirs,
                send_sem=send_sem.at[base + sender],
                recv_sem=recv_sem.at[base + sender],
                device_id=device(stage, sender),
                device_id_type=MESH,
            ).wait_recv()
        for copy in sends:
            copy.wait_send()
        span *= size
        base += size
    o_ref[...] = res[...]


def tree_reduce(packed):
    plan = reduce_plan(lax.axis_size("space"))
    scatter, last = plan
    half = packed.shape[0] // 2
    shapes, length = [], packed.shape[0]
    for stage in scatter:
        length //= stage[2]
        shapes.append((stage[2], length))
    semaphores = sum(stage[2] for stage in scatter) * 2 + last[2]
    scratch = [pltpu.VMEM((n, 8, 128), jnp.float32) for _, n in shapes]
    scratch += [pltpu.VMEM((size, n, 8, 128), jnp.float32) for size, n in shapes]
    scratch += [
        pltpu.VMEM((last[2], length, 8, 128), jnp.float32),
        pltpu.VMEM((half, 8, 128), jnp.float32),
        pltpu.SemaphoreType.DMA((semaphores,)),
        pltpu.SemaphoreType.DMA((semaphores,)),
    ]
    return pl.pallas_call(
        functools.partial(reduce_kernel, plan),
        out_shape=jax.ShapeDtypeStruct((half, 8, 128), jnp.float32),
        in_specs=[pl.BlockSpec(memory_space=pltpu.VMEM)],
        out_specs=pl.BlockSpec(memory_space=pltpu.VMEM),
        scratch_shapes=scratch,
        compiler_params=pltpu.CompilerParams(collective_id=0, has_side_effects=True),
    )(packed)


def pack_halves(parts, blocks):
    halves = []
    for h in range(2):
        pieces = []
        for p in parts[:2]:
            rows = p.shape[0] // 2
            pieces.append(p[h * rows : (h + 1) * rows].reshape(-1))
        for p in parts[2:]:
            cols = p.shape[1] // 2
            pieces.append(p[:, h * cols : (h + 1) * cols].reshape(-1))
        halves.append(jnp.concatenate(pieces))
    real = halves[0].shape[0]
    tiles = -(-real // (TILE * blocks)) * blocks
    flat = jnp.stack(halves)
    flat = jnp.pad(flat, ((0, 0), (0, tiles * TILE - real)))
    return flat.reshape(2 * tiles, 8, 128), real


def unpack_half(reduced, parts):
    flat = reduced.reshape(-1)
    out, offset = [], 0
    for p in parts[:2]:
        shape = (p.shape[0] // 2, p.shape[1])
        out.append(flat[offset : offset + shape[0] * shape[1]].reshape(shape))
        offset += shape[0] * shape[1]
    for p in parts[2:]:
        shape = (p.shape[0], p.shape[1] // 2)
        out.append(flat[offset : offset + shape[0] * shape[1]].reshape(shape))
        offset += shape[0] * shape[1]
    return out


def shards(density, cotangent, pw_one, pw_two, dw_one, dw_two):
    channels, extent_x, extent_y, extent_z = density.shape
    assert lax.axis_size("own") == 2
    weight_one, weight_two, taps_one, taps_two = gather_weights(pw_one, pw_two, dw_one, dw_two)
    rim_width = 1
    wide_input = extended(density, (("own", 1), ("space", 2)), rim_width)
    first = depthwise(wide_input, taps_one, extent_x, extent_y, 1).astype(jnp.bfloat16)
    pre = pointwise(weight_one, first)
    act = jax.nn.silu(pre).astype(jnp.bfloat16)
    act_padded = extended(act, (("own", 1), ("space", 2)), 1)
    second = depthwise(act_padded, taps_two, extent_x, extent_y, 1).astype(jnp.bfloat16)
    grad_second = backmap(weight_two, cotangent).astype(jnp.bfloat16)
    second_padded = extended(grad_second, (("own", 1), ("space", 2)), 1)
    sigma = jax.nn.sigmoid(pre)
    grad_pre = (
        depthwise(second_padded, taps_two, extent_x, extent_y, -1)
        * (sigma * (1.0 + pre * (1.0 - sigma)))
    ).astype(jnp.bfloat16)
    grad_first = backmap(weight_one, grad_pre).astype(jnp.bfloat16)
    first_padded = extended(grad_first, (("own", 1), ("space", 2)), 1)
    grad_input = (
        cotangent.astype(jnp.float32) + depthwise(first_padded, taps_one, extent_x, extent_y, -1)
    ).astype(jnp.bfloat16)
    total_cells = extent_x * extent_y * extent_z * lax.axis_size("own") * lax.axis_size("space")
    grad_scale = 1.0 / math.sqrt(float(total_cells))
    local_pw_one = contract_cells(first, grad_pre) * grad_scale
    local_pw_two = contract_cells(second, cotangent) * grad_scale
    local_dw_one = tap_sums(wide_input, grad_first) * grad_scale
    local_dw_two = tap_sums(act_padded, grad_second) * grad_scale
    partials = (local_pw_one, local_pw_two, local_dw_one, local_dw_two)
    scatter, _ = reduce_plan(lax.axis_size("space"))
    blocks = 1
    for stage in scatter[1:]:
        blocks *= stage[2]
    packed, _ = pack_halves(partials, blocks)
    result = unpack_half(tree_reduce(packed), partials)
    return (grad_input, result[0], result[1], result[2], result[3])


def solution(mesh):
    in_specs = (
        P(None, "own", "space", None),
        P(None, "own", "space", None),
        P("own", None),
        P("own", None),
        P(None, "own"),
        P(None, "own"),
    )
    out_specs = (
        P(None, "own", "space", None),
        P("own", None),
        P("own", None),
        P(None, "own"),
        P(None, "own"),
    )
    return jax.shard_map(shards, mesh=mesh, in_specs=in_specs, out_specs=out_specs, check_vma=False)
```

```python
import functools
import math

import jax
import jax.numpy as jnp
from jax import lax
from jax.experimental import pallas as pl
from jax.experimental.pallas import tpu as pltpu
from jax.sharding import PartitionSpec as P

MESH = pl.DeviceIdType.MESH
TILE = 8 * 128

TAP_LIST = [
    (9 * (a + 1) + 3 * (b + 1) + (d + 1), a, b, d)
    for a in (-1, 0, 1)
    for b in (-1, 0, 1)
    for d in (-1, 0, 1)
]


def extended(value, sides, width):
    for axis, dim in sides:
        size, length = (lax.axis_size(axis), value.shape[dim])
        up = [(i, (i + 1) % size) for i in range(size)]
        down = [(j, i) for i, j in up]
        last = lax.slice_in_dim(value, length - width, length, axis=dim)
        first = lax.slice_in_dim(value, 0, width, axis=dim)
        if size == 2:
            theirs = lax.ppermute(jnp.concatenate([first, last], axis=dim), axis, up)
            after = lax.slice_in_dim(theirs, 0, width, axis=dim)
            before = lax.slice_in_dim(theirs, width, 2 * width, axis=dim)
        else:
            before = lax.ppermute(last, axis, up)
            after = lax.ppermute(first, axis, down)
        value = jnp.concatenate([before, value, after], axis=dim)
    return value


def gather_weights(pw_one, pw_two, dw_one, dw_two):
    mine = jnp.concatenate([pw_one.reshape(-1), pw_two.reshape(-1), dw_one.reshape(-1), dw_two.reshape(-1)])
    theirs = lax.ppermute(mine, "own", [(0, 1), (1, 0)])
    first_half = lax.axis_index("own") == 0
    low = jnp.where(first_half, mine, theirs)
    high = jnp.where(first_half, theirs, mine)
    out, offset = [], 0
    for w, dim in ((pw_one, 0), (pw_two, 0), (dw_one, 1), (dw_two, 1)):
        count = w.size
        parts = [h[offset : offset + count].reshape(w.shape) for h in (low, high)]
        out.append(jnp.concatenate(parts, axis=dim))
        offset += count
    return out


def depthwise(padded, weights, extent_x, extent_y, direction):
    running = jnp.zeros((padded.shape[0], extent_x, extent_y, padded.shape[3]), jnp.float32)
    for k, a, b, d in TAP_LIST:
        start_x = 1 + direction * a
        start_y = 1 + direction * b
        shifted = padded[:, start_x : start_x + extent_x, start_y : start_y + extent_y, :]
        shifted = jnp.roll(shifted, -direction * d, axis=3).astype(jnp.float32)
        running = running + weights[k].astype(jnp.float32)[:, None, None, None] * shifted
    return running


def tap_sums(padded, gradient):
    extent_x = gradient.shape[1]
    extent_y = gradient.shape[2]
    grad_float = gradient.astype(jnp.float32)
    columns = []
    for k, a, b, d in TAP_LIST:
        shifted = padded[:, 1 + a : 1 + a + extent_x, 1 + b : 1 + b + extent_y, :]
        shifted = jnp.roll(shifted, -d, axis=3).astype(jnp.float32)
        columns.append(jnp.sum(shifted * grad_float, axis=(1, 2, 3)))
    return jnp.stack(columns, axis=0)


def pointwise(weights, source):
    layout = source.shape
    flattened = source.reshape(layout[0], -1)
    return jnp.dot(weights.T, flattened, preferred_element_type=jnp.float32).reshape(layout)


def backmap(weights, source):
    layout = source.shape
    flattened = source.reshape(layout[0], -1)
    return jnp.dot(weights, flattened, preferred_element_type=jnp.float32).reshape(layout)


def contract_cells(left, right):
    channels = left.shape[0]
    return lax.dot_general(
        left.reshape(channels, -1),
        right.reshape(channels, -1),
        (((1,), (1,)), ((), ())),
        preferred_element_type=jnp.float32,
    )


def reduce_plan(space_size):
    if space_size == 128:
        scatter = ((("own", 0, 2), ("space", 1, 2)), (("space", 2, 2), ("space", 4, 4)))
        return scatter, (("space", 16, 8),)
    factors, stride, rest = [], 1, space_size
    while rest > 2:
        factors.append(("space", stride, 2))
        stride, rest = stride * 2, rest // 2
    scatter = ((("own", 0, 2),) + tuple(factors[:1]),) + tuple((f,) for f in factors[1:])
    return scatter, (("space", stride, rest),)


def group_size(group):
    return math.prod(f[2] for f in group)


def reduce_kernel(plan, x_ref, o_ref, *refs):
    scatter, last = plan
    count = len(scatter)
    bufs = refs[:count]
    recvs = refs[count : 2 * count]
    recv_last, res, send_sem, recv_sem = refs[2 * count :]
    own = lax.axis_index("own")
    space = lax.axis_index("space")

    def coord(factor):
        axis, stride, size = factor
        return own if axis == "own" else (space // stride) % size

    def member(group):
        index = 0
        for factor in group:
            index = index * factor[2] + coord(factor)
        return index

    def device(group, target):
        new_own, new_space = own, space
        for factor in reversed(group):
            axis, stride, size = factor
            value = target % size
            target = target // size
            if axis == "own":
                new_own = value
            else:
                new_space = new_space + (value - coord(factor)) * stride
        return (new_own, new_space)

    barrier = pltpu.get_barrier_semaphore()
    partners = 0
    for group in scatter + (last,):
        size, me = group_size(group), member(group)
        for d in range(1, size):
            pl.semaphore_signal(
                barrier, 1, device_id=device(group, (me + d) % size), device_id_type=MESH
            )
            partners += 1
    pl.semaphore_wait(barrier, partners)

    def exchange(group, base, source_of, dest_of):
        size, me = group_size(group), member(group)
        sends = []
        for d in range(1, size):
            target = (me + d) % size
            copy = pltpu.make_async_remote_copy(
                src_ref=source_of(target),
                dst_ref=dest_of(me),
                send_sem=send_sem.at[base + target],
                recv_sem=recv_sem.at[base + me],
                device_id=device(group, target),
                device_id_type=MESH,
            )
            copy.start()
            sends.append(copy)
        return sends

    def finish(group, base, source_of, dest_of, sends):
        size, me = group_size(group), member(group)
        for d in range(1, size):
            sender = (me + d) % size
            pltpu.make_async_remote_copy(
                src_ref=source_of(sender),
                dst_ref=dest_of(sender),
                send_sem=send_sem.at[base + sender],
                recv_sem=recv_sem.at[base + sender],
                device_id=device(group, sender),
                device_id_type=MESH,
            ).wait_recv()
        for copy in sends:
            copy.wait_send()

    base = 0
    source = x_ref
    for i, group in enumerate(scatter):
        size, me = group_size(group), member(group)
        piece = source.shape[0] // size
        src_of = lambda t, s=source, n=piece: s.at[pl.ds(t * n, n)]
        dst_of = lambda t, r=recvs[i]: r.at[t]
        sends = exchange(group, base, src_of, dst_of)
        finish(group, base, src_of, dst_of, sends)
        total = source[pl.ds(me * piece, piece)]
        for d in range(1, size):
            total = total + recvs[i][(me + d) % size]
        bufs[i][...] = total
        source = bufs[i]
        base += size

    size, me = group_size(last), member(last)
    piece = source.shape[0]
    src_of = lambda t, s=source: s
    dst_of = lambda t: recv_last.at[t]
    sends = exchange(last, base, src_of, dst_of)
    recv_last[me] = source[...]
    finish(last, base, src_of, dst_of, sends)
    total = recv_last[0]
    for k in range(1, size):
        total = total + recv_last[k]
    space_factors = [f for group in scatter for f in group if f[0] != "own"]
    block = 0
    for factor in space_factors:
        block = block * factor[2] + coord(factor)
    res[pl.ds(block * piece, piece)] = total
    base += size

    span = piece
    gathers = [tuple(f for f in group if f[0] != "own") for group in scatter]
    for j in range(len(gathers) - 1, -1, -1):
        group = gathers[j]
        if not group:
            continue
        size, me = group_size(group), member(group)
        prefix = 0
        for earlier in gathers[:j]:
            prefix = prefix * group_size(earlier) + member(earlier)
        start = prefix * size * span
        src_of = lambda t, a=start, n=span: res.at[pl.ds(a + t * n, n)]
        sends = []
        for d in range(1, size):
            target = (me + d) % size
            copy = pltpu.make_async_remote_copy(
                src_ref=src_of(me),
                dst_ref=src_of(me),
                send_sem=send_sem.at[base + target],
                recv_sem=recv_sem.at[base + me],
                device_id=device(group, target),
                device_id_type=MESH,
            )
            copy.start()
            sends.append(copy)
        finish(group, base, src_of, src_of, sends)
        span *= size
        base += size
    o_ref[...] = res[...]


def tree_reduce(packed):
    plan = reduce_plan(lax.axis_size("space"))
    scatter, last = plan
    half = packed.shape[0] // 2
    shapes, length = [], packed.shape[0]
    for group in scatter:
        length //= group_size(group)
        shapes.append((group_size(group), length))
    semaphores = sum(group_size(group) for group in scatter) * 2 + group_size(last)
    scratch = [pltpu.VMEM((n, 8, 128), jnp.float32) for _, n in shapes]
    scratch += [pltpu.VMEM((size, n, 8, 128), jnp.float32) for size, n in shapes]
    scratch += [
        pltpu.VMEM((group_size(last), length, 8, 128), jnp.float32),
        pltpu.VMEM((half, 8, 128), jnp.float32),
        pltpu.SemaphoreType.DMA((semaphores,)),
        pltpu.SemaphoreType.DMA((semaphores,)),
    ]
    return pl.pallas_call(
        functools.partial(reduce_kernel, plan),
        out_shape=jax.ShapeDtypeStruct((half, 8, 128), jnp.float32),
        in_specs=[pl.BlockSpec(memory_space=pltpu.VMEM)],
        out_specs=pl.BlockSpec(memory_space=pltpu.VMEM),
        scratch_shapes=scratch,
        compiler_params=pltpu.CompilerParams(collective_id=0, has_side_effects=True),
        cost_estimate=pl.CostEstimate(
            flops=0, transcendentals=0, bytes_accessed=64 * packed.size * 4
        ),
    )(packed)


def pack_halves(parts, blocks):
    halves = []
    for h in range(2):
        pieces = []
        for p in parts[:2]:
            rows = p.shape[0] // 2
            pieces.append(p[h * rows : (h + 1) * rows].reshape(-1))
        for p in parts[2:]:
            cols = p.shape[1] // 2
            pieces.append(p[:, h * cols : (h + 1) * cols].reshape(-1))
        halves.append(jnp.concatenate(pieces))
    real = halves[0].shape[0]
    tiles = -(-real // (TILE * blocks)) * blocks
    flat = jnp.stack(halves)
    flat = jnp.pad(flat, ((0, 0), (0, tiles * TILE - real)))
    return flat.reshape(2 * tiles, 8, 128), real


def unpack_half(reduced, parts):
    flat = reduced.reshape(-1)
    out, offset = [], 0
    for p in parts[:2]:
        shape = (p.shape[0] // 2, p.shape[1])
        out.append(flat[offset : offset + shape[0] * shape[1]].reshape(shape))
        offset += shape[0] * shape[1]
    for p in parts[2:]:
        shape = (p.shape[0], p.shape[1] // 2)
        out.append(flat[offset : offset + shape[0] * shape[1]].reshape(shape))
        offset += shape[0] * shape[1]
    return out


def shards(density, cotangent, pw_one, pw_two, dw_one, dw_two):
    channels, extent_x, extent_y, extent_z = density.shape
    assert lax.axis_size("own") == 2
    weight_one, weight_two, taps_one, taps_two = gather_weights(pw_one, pw_two, dw_one, dw_two)
    rim_width = 1
    wide_input = extended(density, (("own", 1), ("space", 2)), rim_width)
    first = depthwise(wide_input, taps_one, extent_x, extent_y, 1).astype(jnp.bfloat16)
    pre = pointwise(weight_one, first)
    act = jax.nn.silu(pre).astype(jnp.bfloat16)
    act_padded = extended(act, (("own", 1), ("space", 2)), 1)
    second = depthwise(act_padded, taps_two, extent_x, extent_y, 1).astype(jnp.bfloat16)
    grad_second = backmap(weight_two, cotangent).astype(jnp.bfloat16)
    second_padded = extended(grad_second, (("own", 1), ("space", 2)), 1)
    sigma = jax.nn.sigmoid(pre)
    grad_pre = (
        depthwise(second_padded, taps_two, extent_x, extent_y, -1)
        * (sigma * (1.0 + pre * (1.0 - sigma)))
    ).astype(jnp.bfloat16)
    grad_first = backmap(weight_one, grad_pre).astype(jnp.bfloat16)
    first_padded = extended(grad_first, (("own", 1), ("space", 2)), 1)
    grad_input = (
        cotangent.astype(jnp.float32) + depthwise(first_padded, taps_one, extent_x, extent_y, -1)
    ).astype(jnp.bfloat16)
    total_cells = extent_x * extent_y * extent_z * lax.axis_size("own") * lax.axis_size("space")
    grad_scale = 1.0 / math.sqrt(float(total_cells))
    local_pw_one = contract_cells(first, grad_pre) * grad_scale
    local_pw_two = contract_cells(second, cotangent) * grad_scale
    local_dw_one = tap_sums(wide_input, grad_first) * grad_scale
    local_dw_two = tap_sums(act_padded, grad_second) * grad_scale
    partials = (local_pw_one, local_pw_two, local_dw_one, local_dw_two)
    scatter, _ = reduce_plan(lax.axis_size("space"))
    blocks = math.prod(f[2] for group in scatter for f in group if f[0] != "own")
    packed, _ = pack_halves(partials, blocks)
    result = unpack_half(tree_reduce(packed), partials)
    return (grad_input, result[0], result[1], result[2], result[3])


def solution(mesh):
    in_specs = (
        P(None, "own", "space", None),
        P(None, "own", "space", None),
        P("own", None),
        P("own", None),
        P(None, "own"),
        P(None, "own"),
    )
    out_specs = (
        P(None, "own", "space", None),
        P("own", None),
        P("own", None),
        P(None, "own"),
        P(None, "own"),
    )
    return jax.shard_map(shards, mesh=mesh, in_specs=in_specs, out_specs=out_specs, check_vma=False)
```

```python
import functools
import math

import jax
import jax.numpy as jnp
from jax import lax
from jax.experimental import pallas as pl
from jax.experimental.pallas import tpu as pltpu
from jax.sharding import PartitionSpec as P

MESH = pl.DeviceIdType.MESH
TILE = 8 * 128

TAP_LIST = [
    (9 * (a + 1) + 3 * (b + 1) + (d + 1), a, b, d)
    for a in (-1, 0, 1)
    for b in (-1, 0, 1)
    for d in (-1, 0, 1)
]


def extended(value):
    count = lax.axis_size("space")
    swap = [(0, 1), (1, 0)]
    up = [(i, (i + 1) % count) for i in range(count)]
    down = [(j, i) for i, j in up]
    cross_up = [(o * count + i, (1 - o) * count + j) for o in range(2) for i, j in up]
    cross_down = [(o * count + i, (1 - o) * count + j) for o in range(2) for i, j in down]
    first = value[:, :, :1]
    last = value[:, :, -1:]
    partner = lax.ppermute(value, "own", swap)
    below = lax.ppermute(last, "space", up)
    above = lax.ppermute(first, "space", down)
    corner_below = lax.ppermute(last, ("own", "space"), cross_up)
    corner_above = lax.ppermute(first, ("own", "space"), cross_down)

    def row(theirs, mine):
        return jnp.concatenate([theirs[:, -1:], mine, theirs[:, :1]], axis=1)

    return jnp.concatenate(
        [row(corner_below, below), row(partner, value), row(corner_above, above)], axis=2
    )


def gather_weights(pw_one, pw_two, dw_one, dw_two):
    mine = jnp.concatenate([pw_one.reshape(-1), pw_two.reshape(-1), dw_one.reshape(-1), dw_two.reshape(-1)])
    theirs = lax.ppermute(mine, "own", [(0, 1), (1, 0)])
    first_half = lax.axis_index("own") == 0
    low = jnp.where(first_half, mine, theirs)
    high = jnp.where(first_half, theirs, mine)
    out, offset = [], 0
    for w, dim in ((pw_one, 0), (pw_two, 0), (dw_one, 1), (dw_two, 1)):
        count = w.size
        parts = [h[offset : offset + count].reshape(w.shape) for h in (low, high)]
        out.append(jnp.concatenate(parts, axis=dim))
        offset += count
    return out


def depthwise(padded, weights, extent_x, extent_y, direction):
    running = jnp.zeros((padded.shape[0], extent_x, extent_y, padded.shape[3]), jnp.float32)
    for k, a, b, d in TAP_LIST:
        start_x = 1 + direction * a
        start_y = 1 + direction * b
        shifted = padded[:, start_x : start_x + extent_x, start_y : start_y + extent_y, :]
        shifted = jnp.roll(shifted, -direction * d, axis=3).astype(jnp.float32)
        running = running + weights[k].astype(jnp.float32)[:, None, None, None] * shifted
    return running


def tap_sums(padded, gradient):
    extent_x = gradient.shape[1]
    extent_y = gradient.shape[2]
    grad_float = gradient.astype(jnp.float32)
    columns = []
    for k, a, b, d in TAP_LIST:
        shifted = padded[:, 1 + a : 1 + a + extent_x, 1 + b : 1 + b + extent_y, :]
        shifted = jnp.roll(shifted, -d, axis=3).astype(jnp.float32)
        columns.append(jnp.sum(shifted * grad_float, axis=(1, 2, 3)))
    return jnp.stack(columns, axis=0)


def pointwise(weights, source):
    layout = source.shape
    flattened = source.reshape(layout[0], -1)
    return jnp.dot(weights.T, flattened, preferred_element_type=jnp.float32).reshape(layout)


def backmap(weights, source):
    layout = source.shape
    flattened = source.reshape(layout[0], -1)
    return jnp.dot(weights, flattened, preferred_element_type=jnp.float32).reshape(layout)


def contract_cells(left, right):
    channels = left.shape[0]
    return lax.dot_general(
        left.reshape(channels, -1),
        right.reshape(channels, -1),
        (((1,), (1,)), ((), ())),
        preferred_element_type=jnp.float32,
    )


def reduce_plan(space_size):
    if space_size == 128:
        scatter = ((("own", 0, 2), ("space", 1, 2)), (("space", 2, 2), ("space", 4, 4)))
        return scatter, (("space", 16, 8),)
    factors, stride, rest = [], 1, space_size
    while rest > 2:
        factors.append(("space", stride, 2))
        stride, rest = stride * 2, rest // 2
    scatter = ((("own", 0, 2),) + tuple(factors[:1]),) + tuple((f,) for f in factors[1:])
    return scatter, (("space", stride, rest),)


def group_size(group):
    return math.prod(f[2] for f in group)


def reduce_kernel(plan, x_ref, o_ref, *refs):
    scatter, last = plan
    count = len(scatter)
    bufs = refs[:count]
    recvs = refs[count : 2 * count]
    recv_last, res, send_sem, recv_sem = refs[2 * count :]
    own = lax.axis_index("own")
    space = lax.axis_index("space")

    def coord(factor):
        axis, stride, size = factor
        return own if axis == "own" else (space // stride) % size

    def member(group):
        index = 0
        for factor in group:
            index = index * factor[2] + coord(factor)
        return index

    def device(group, target):
        new_own, new_space = own, space
        for factor in reversed(group):
            axis, stride, size = factor
            value = target % size
            target = target // size
            if axis == "own":
                new_own = value
            else:
                new_space = new_space + (value - coord(factor)) * stride
        return (new_own, new_space)

    barrier = pltpu.get_barrier_semaphore()
    partners = 0
    for group in scatter + (last,):
        size, me = group_size(group), member(group)
        for d in range(1, size):
            pl.semaphore_signal(
                barrier, 1, device_id=device(group, (me + d) % size), device_id_type=MESH
            )
            partners += 1
    pl.semaphore_wait(barrier, partners)

    def exchange(group, base, source_of, dest_of):
        size, me = group_size(group), member(group)
        sends = []
        for d in range(1, size):
            target = (me + d) % size
            copy = pltpu.make_async_remote_copy(
                src_ref=source_of(target),
                dst_ref=dest_of(me),
                send_sem=send_sem.at[base + target],
                recv_sem=recv_sem.at[base + me],
                device_id=device(group, target),
                device_id_type=MESH,
            )
            copy.start()
            sends.append(copy)
        return sends

    def finish(group, base, source_of, dest_of, sends):
        size, me = group_size(group), member(group)
        for d in range(1, size):
            sender = (me + d) % size
            pltpu.make_async_remote_copy(
                src_ref=source_of(sender),
                dst_ref=dest_of(sender),
                send_sem=send_sem.at[base + sender],
                recv_sem=recv_sem.at[base + sender],
                device_id=device(group, sender),
                device_id_type=MESH,
            ).wait_recv()
        for copy in sends:
            copy.wait_send()

    base = 0
    source = x_ref
    for i, group in enumerate(scatter):
        size, me = group_size(group), member(group)
        piece = source.shape[0] // size
        src_of = lambda t, s=source, n=piece: s.at[pl.ds(t * n, n)]
        dst_of = lambda t, r=recvs[i]: r.at[t]
        sends = exchange(group, base, src_of, dst_of)
        finish(group, base, src_of, dst_of, sends)
        total = source[pl.ds(me * piece, piece)]
        for d in range(1, size):
            total = total + recvs[i][(me + d) % size]
        bufs[i][...] = total
        source = bufs[i]
        base += size

    size, me = group_size(last), member(last)
    piece = source.shape[0]
    src_of = lambda t, s=source: s
    dst_of = lambda t: recv_last.at[t]
    sends = exchange(last, base, src_of, dst_of)
    recv_last[me] = source[...]
    finish(last, base, src_of, dst_of, sends)
    total = recv_last[0]
    for k in range(1, size):
        total = total + recv_last[k]
    space_factors = [f for group in scatter for f in group if f[0] != "own"]
    block = 0
    for factor in space_factors:
        block = block * factor[2] + coord(factor)
    res[pl.ds(block * piece, piece)] = total
    base += size

    span = piece
    gathers = [tuple(f for f in group if f[0] != "own") for group in scatter]
    for j in range(len(gathers) - 1, -1, -1):
        group = gathers[j]
        if not group:
            continue
        size, me = group_size(group), member(group)
        prefix = 0
        for earlier in gathers[:j]:
            prefix = prefix * group_size(earlier) + member(earlier)
        start = prefix * size * span
        src_of = lambda t, a=start, n=span: res.at[pl.ds(a + t * n, n)]
        sends = []
        for d in range(1, size):
            target = (me + d) % size
            copy = pltpu.make_async_remote_copy(
                src_ref=src_of(me),
                dst_ref=src_of(me),
                send_sem=send_sem.at[base + target],
                recv_sem=recv_sem.at[base + me],
                device_id=device(group, target),
                device_id_type=MESH,
            )
            copy.start()
            sends.append(copy)
        finish(group, base, src_of, src_of, sends)
        span *= size
        base += size
    o_ref[...] = res[...]


def tree_reduce(packed):
    plan = reduce_plan(lax.axis_size("space"))
    scatter, last = plan
    half = packed.shape[0] // 2
    shapes, length = [], packed.shape[0]
    for group in scatter:
        length //= group_size(group)
        shapes.append((group_size(group), length))
    semaphores = sum(group_size(group) for group in scatter) * 2 + group_size(last)
    scratch = [pltpu.VMEM((n, 8, 128), jnp.float32) for _, n in shapes]
    scratch += [pltpu.VMEM((size, n, 8, 128), jnp.float32) for size, n in shapes]
    scratch += [
        pltpu.VMEM((group_size(last), length, 8, 128), jnp.float32),
        pltpu.VMEM((half, 8, 128), jnp.float32),
        pltpu.SemaphoreType.DMA((semaphores,)),
        pltpu.SemaphoreType.DMA((semaphores,)),
    ]
    return pl.pallas_call(
        functools.partial(reduce_kernel, plan),
        out_shape=jax.ShapeDtypeStruct((half, 8, 128), jnp.float32),
        in_specs=[pl.BlockSpec(memory_space=pltpu.VMEM)],
        out_specs=pl.BlockSpec(memory_space=pltpu.VMEM),
        scratch_shapes=scratch,
        compiler_params=pltpu.CompilerParams(collective_id=0, has_side_effects=True),
        cost_estimate=pl.CostEstimate(
            flops=0, transcendentals=0, bytes_accessed=64 * packed.size * 4
        ),
    )(packed)


def pack_halves(parts, blocks):
    halves = []
    for h in range(2):
        pieces = []
        for p in parts[:2]:
            rows = p.shape[0] // 2
            pieces.append(p[h * rows : (h + 1) * rows].reshape(-1))
        for p in parts[2:]:
            cols = p.shape[1] // 2
            pieces.append(p[:, h * cols : (h + 1) * cols].reshape(-1))
        halves.append(jnp.concatenate(pieces))
    real = halves[0].shape[0]
    tiles = -(-real // (TILE * blocks)) * blocks
    flat = jnp.stack(halves)
    flat = jnp.pad(flat, ((0, 0), (0, tiles * TILE - real)))
    return flat.reshape(2 * tiles, 8, 128), real


def unpack_half(reduced, parts):
    flat = reduced.reshape(-1)
    out, offset = [], 0
    for p in parts[:2]:
        shape = (p.shape[0] // 2, p.shape[1])
        out.append(flat[offset : offset + shape[0] * shape[1]].reshape(shape))
        offset += shape[0] * shape[1]
    for p in parts[2:]:
        shape = (p.shape[0], p.shape[1] // 2)
        out.append(flat[offset : offset + shape[0] * shape[1]].reshape(shape))
        offset += shape[0] * shape[1]
    return out


def shards(density, cotangent, pw_one, pw_two, dw_one, dw_two):
    channels, extent_x, extent_y, extent_z = density.shape
    assert lax.axis_size("own") == 2
    weight_one, weight_two, taps_one, taps_two = gather_weights(pw_one, pw_two, dw_one, dw_two)
    rim_width = 1
    wide_input = extended(density)
    first = depthwise(wide_input, taps_one, extent_x, extent_y, 1).astype(jnp.bfloat16)
    pre = pointwise(weight_one, first)
    act = jax.nn.silu(pre).astype(jnp.bfloat16)
    act_padded = extended(act)
    second = depthwise(act_padded, taps_two, extent_x, extent_y, 1).astype(jnp.bfloat16)
    grad_second = backmap(weight_two, cotangent).astype(jnp.bfloat16)
    second_padded = extended(grad_second)
    sigma = jax.nn.sigmoid(pre)
    grad_pre = (
        depthwise(second_padded, taps_two, extent_x, extent_y, -1)
        * (sigma * (1.0 + pre * (1.0 - sigma)))
    ).astype(jnp.bfloat16)
    grad_first = backmap(weight_one, grad_pre).astype(jnp.bfloat16)
    first_padded = extended(grad_first)
    grad_input = (
        cotangent.astype(jnp.float32) + depthwise(first_padded, taps_one, extent_x, extent_y, -1)
    ).astype(jnp.bfloat16)
    total_cells = extent_x * extent_y * extent_z * lax.axis_size("own") * lax.axis_size("space")
    grad_scale = 1.0 / math.sqrt(float(total_cells))
    local_pw_one = contract_cells(first, grad_pre) * grad_scale
    local_pw_two = contract_cells(second, cotangent) * grad_scale
    local_dw_one = tap_sums(wide_input, grad_first) * grad_scale
    local_dw_two = tap_sums(act_padded, grad_second) * grad_scale
    partials = (local_pw_one, local_pw_two, local_dw_one, local_dw_two)
    scatter, _ = reduce_plan(lax.axis_size("space"))
    blocks = math.prod(f[2] for group in scatter for f in group if f[0] != "own")
    packed, _ = pack_halves(partials, blocks)
    result = unpack_half(tree_reduce(packed), partials)
    return (grad_input, result[0], result[1], result[2], result[3])


def solution(mesh):
    in_specs = (
        P(None, "own", "space", None),
        P(None, "own", "space", None),
        P("own", None),
        P("own", None),
        P(None, "own"),
        P(None, "own"),
    )
    out_specs = (
        P(None, "own", "space", None),
        P("own", None),
        P("own", None),
        P(None, "own"),
        P(None, "own"),
    )
    return jax.shard_map(shards, mesh=mesh, in_specs=in_specs, out_specs=out_specs, check_vma=False)
```

```python
import functools
import math

import jax
import jax.numpy as jnp
from jax import lax
from jax.experimental import pallas as pl
from jax.experimental.pallas import tpu as pltpu
from jax.sharding import PartitionSpec as P

MESH = pl.DeviceIdType.MESH
TILE = 8 * 128

TAP_LIST = [
    (9 * (a + 1) + 3 * (b + 1) + (d + 1), a, b, d)
    for a in (-1, 0, 1)
    for b in (-1, 0, 1)
    for d in (-1, 0, 1)
]


def extended(value, extra=None):
    swap = [(0, 1), (1, 0)]
    if extra is None:
        partner = lax.ppermute(value, "own", swap)
    else:
        partner, theirs = lax.ppermute((value, extra), "own", swap)
    value = jnp.concatenate([partner[:, -1:], value, partner[:, :1]], axis=1)
    count, length = lax.axis_size("space"), value.shape[2]
    up = [(i, (i + 1) % count) for i in range(count)]
    down = [(j, i) for i, j in up]
    before = lax.ppermute(value[:, :, length - 1 :], "space", up)
    after = lax.ppermute(value[:, :, :1], "space", down)
    value = jnp.concatenate([before, value, after], axis=2)
    return value if extra is None else (value, theirs)


def gather_weights(weights, theirs):
    mine = jnp.concatenate([w.reshape(-1) for w in weights])
    first_half = lax.axis_index("own") == 0
    low = jnp.where(first_half, mine, theirs)
    high = jnp.where(first_half, theirs, mine)
    out, offset = [], 0
    for w, dim in zip(weights, (0, 0, 1, 1)):
        count = w.size
        parts = [h[offset : offset + count].reshape(w.shape) for h in (low, high)]
        out.append(jnp.concatenate(parts, axis=dim))
        offset += count
    return out


def depthwise(padded, weights, extent_x, extent_y, direction):
    running = jnp.zeros((padded.shape[0], extent_x, extent_y, padded.shape[3]), jnp.float32)
    for k, a, b, d in TAP_LIST:
        start_x = 1 + direction * a
        start_y = 1 + direction * b
        shifted = padded[:, start_x : start_x + extent_x, start_y : start_y + extent_y, :]
        shifted = jnp.roll(shifted, -direction * d, axis=3).astype(jnp.float32)
        running = running + weights[k].astype(jnp.float32)[:, None, None, None] * shifted
    return running


def tap_sums(padded, gradient):
    extent_x = gradient.shape[1]
    extent_y = gradient.shape[2]
    grad_float = gradient.astype(jnp.float32)
    columns = []
    for k, a, b, d in TAP_LIST:
        shifted = padded[:, 1 + a : 1 + a + extent_x, 1 + b : 1 + b + extent_y, :]
        shifted = jnp.roll(shifted, -d, axis=3).astype(jnp.float32)
        columns.append(jnp.sum(shifted * grad_float, axis=(1, 2, 3)))
    return jnp.stack(columns, axis=0)


def pointwise(weights, source):
    layout = source.shape
    flattened = source.reshape(layout[0], -1)
    return jnp.dot(weights.T, flattened, preferred_element_type=jnp.float32).reshape(layout)


def backmap(weights, source):
    layout = source.shape
    flattened = source.reshape(layout[0], -1)
    return jnp.dot(weights, flattened, preferred_element_type=jnp.float32).reshape(layout)


def contract_cells(left, right):
    channels = left.shape[0]
    return lax.dot_general(
        left.reshape(channels, -1),
        right.reshape(channels, -1),
        (((1,), (1,)), ((), ())),
        preferred_element_type=jnp.float32,
    )


def reduce_plan(space_size):
    if space_size == 128:
        scatter = ((("own", 0, 2), ("space", 1, 2)), (("space", 2, 2), ("space", 4, 4)))
        return scatter, (("space", 16, 8),)
    factors, stride, rest = [], 1, space_size
    while rest > 2:
        factors.append(("space", stride, 2))
        stride, rest = stride * 2, rest // 2
    scatter = ((("own", 0, 2),) + tuple(factors[:1]),) + tuple((f,) for f in factors[1:])
    return scatter, (("space", stride, rest),)


def group_size(group):
    return math.prod(f[2] for f in group)


def reduce_kernel(plan, x_ref, o_ref, *refs):
    scatter, last = plan
    count = len(scatter)
    bufs = refs[:count]
    recvs = refs[count : 2 * count]
    recv_last, res, send_sem, recv_sem = refs[2 * count :]
    own = lax.axis_index("own")
    space = lax.axis_index("space")

    def coord(factor):
        axis, stride, size = factor
        return own if axis == "own" else (space // stride) % size

    def member(group):
        index = 0
        for factor in group:
            index = index * factor[2] + coord(factor)
        return index

    def device(group, target):
        new_own, new_space = own, space
        for factor in reversed(group):
            axis, stride, size = factor
            value = target % size
            target = target // size
            if axis == "own":
                new_own = value
            else:
                new_space = new_space + (value - coord(factor)) * stride
        return (new_own, new_space)

    barrier = pltpu.get_barrier_semaphore()
    partners = 0
    for group in scatter + (last,):
        size, me = group_size(group), member(group)
        for d in range(1, size):
            pl.semaphore_signal(
                barrier, 1, device_id=device(group, (me + d) % size), device_id_type=MESH
            )
            partners += 1
    pl.semaphore_wait(barrier, partners)

    def exchange(group, base, source_of, dest_of):
        size, me = group_size(group), member(group)
        sends = []
        for d in range(1, size):
            target = (me + d) % size
            copy = pltpu.make_async_remote_copy(
                src_ref=source_of(target),
                dst_ref=dest_of(me),
                send_sem=send_sem.at[base + target],
                recv_sem=recv_sem.at[base + me],
                device_id=device(group, target),
                device_id_type=MESH,
            )
            copy.start()
            sends.append(copy)
        return sends

    def finish(group, base, source_of, dest_of, sends):
        size, me = group_size(group), member(group)
        for d in range(1, size):
            sender = (me + d) % size
            pltpu.make_async_remote_copy(
                src_ref=source_of(sender),
                dst_ref=dest_of(sender),
                send_sem=send_sem.at[base + sender],
                recv_sem=recv_sem.at[base + sender],
                device_id=device(group, sender),
                device_id_type=MESH,
            ).wait_recv()
        for copy in sends:
            copy.wait_send()

    base = 0
    source = x_ref
    for i, group in enumerate(scatter):
        size, me = group_size(group), member(group)
        piece = source.shape[0] // size
        src_of = lambda t, s=source, n=piece: s.at[pl.ds(t * n, n)]
        dst_of = lambda t, r=recvs[i]: r.at[t]
        sends = exchange(group, base, src_of, dst_of)
        finish(group, base, src_of, dst_of, sends)
        total = source[pl.ds(me * piece, piece)]
        for d in range(1, size):
            total = total + recvs[i][(me + d) % size]
        bufs[i][...] = total
        source = bufs[i]
        base += size

    size, me = group_size(last), member(last)
    piece = source.shape[0]
    src_of = lambda t, s=source: s
    dst_of = lambda t: recv_last.at[t]
    sends = exchange(last, base, src_of, dst_of)
    recv_last[me] = source[...]
    finish(last, base, src_of, dst_of, sends)
    total = recv_last[0]
    for k in range(1, size):
        total = total + recv_last[k]
    space_factors = [f for group in scatter for f in group if f[0] != "own"]
    block = 0
    for factor in space_factors:
        block = block * factor[2] + coord(factor)
    res[pl.ds(block * piece, piece)] = total
    base += size

    span = piece
    gathers = [tuple(f for f in group if f[0] != "own") for group in scatter]
    for j in range(len(gathers) - 1, -1, -1):
        group = gathers[j]
        if not group:
            continue
        size, me = group_size(group), member(group)
        prefix = 0
        for earlier in gathers[:j]:
            prefix = prefix * group_size(earlier) + member(earlier)
        start = prefix * size * span
        src_of = lambda t, a=start, n=span: res.at[pl.ds(a + t * n, n)]
        sends = []
        for d in range(1, size):
            target = (me + d) % size
            copy = pltpu.make_async_remote_copy(
                src_ref=src_of(me),
                dst_ref=src_of(me),
                send_sem=send_sem.at[base + target],
                recv_sem=recv_sem.at[base + me],
                device_id=device(group, target),
                device_id_type=MESH,
            )
            copy.start()
            sends.append(copy)
        finish(group, base, src_of, src_of, sends)
        span *= size
        base += size
    o_ref[...] = res[...]


def tree_reduce(packed):
    plan = reduce_plan(lax.axis_size("space"))
    scatter, last = plan
    half = packed.shape[0] // 2
    shapes, length = [], packed.shape[0]
    for group in scatter:
        length //= group_size(group)
        shapes.append((group_size(group), length))
    semaphores = sum(group_size(group) for group in scatter) * 2 + group_size(last)
    scratch = [pltpu.VMEM((n, 8, 128), jnp.float32) for _, n in shapes]
    scratch += [pltpu.VMEM((size, n, 8, 128), jnp.float32) for size, n in shapes]
    scratch += [
        pltpu.VMEM((group_size(last), length, 8, 128), jnp.float32),
        pltpu.VMEM((half, 8, 128), jnp.float32),
        pltpu.SemaphoreType.DMA((semaphores,)),
        pltpu.SemaphoreType.DMA((semaphores,)),
    ]
    return pl.pallas_call(
        functools.partial(reduce_kernel, plan),
        out_shape=jax.ShapeDtypeStruct((half, 8, 128), jnp.float32),
        in_specs=[pl.BlockSpec(memory_space=pltpu.VMEM)],
        out_specs=pl.BlockSpec(memory_space=pltpu.VMEM),
        scratch_shapes=scratch,
        compiler_params=pltpu.CompilerParams(collective_id=0, has_side_effects=True),
        cost_estimate=pl.CostEstimate(
            flops=0, transcendentals=0, bytes_accessed=64 * packed.size * 4
        ),
    )(packed)


def pack_halves(parts, blocks):
    halves = []
    for h in range(2):
        pieces = []
        for p in parts[:2]:
            rows = p.shape[0] // 2
            pieces.append(p[h * rows : (h + 1) * rows].reshape(-1))
        for p in parts[2:]:
            cols = p.shape[1] // 2
            pieces.append(p[:, h * cols : (h + 1) * cols].reshape(-1))
        halves.append(jnp.concatenate(pieces))
    real = halves[0].shape[0]
    tiles = -(-real // (TILE * blocks)) * blocks
    flat = jnp.stack(halves)
    flat = jnp.pad(flat, ((0, 0), (0, tiles * TILE - real)))
    return flat.reshape(2 * tiles, 8, 128), real


def unpack_half(reduced, parts):
    flat = reduced.reshape(-1)
    out, offset = [], 0
    for p in parts[:2]:
        shape = (p.shape[0] // 2, p.shape[1])
        out.append(flat[offset : offset + shape[0] * shape[1]].reshape(shape))
        offset += shape[0] * shape[1]
    for p in parts[2:]:
        shape = (p.shape[0], p.shape[1] // 2)
        out.append(flat[offset : offset + shape[0] * shape[1]].reshape(shape))
        offset += shape[0] * shape[1]
    return out


def shards(density, cotangent, pw_one, pw_two, dw_one, dw_two):
    channels, extent_x, extent_y, extent_z = density.shape
    assert lax.axis_size("own") == 2
    weights = (pw_one, pw_two, dw_one, dw_two)
    wide_input, theirs = extended(density, jnp.concatenate([w.reshape(-1) for w in weights]))
    weight_one, weight_two, taps_one, taps_two = gather_weights(weights, theirs)
    first = depthwise(wide_input, taps_one, extent_x, extent_y, 1).astype(jnp.bfloat16)
    pre = pointwise(weight_one, first)
    act = jax.nn.silu(pre).astype(jnp.bfloat16)
    grad_second = backmap(weight_two, cotangent).astype(jnp.bfloat16)
    both_padded = extended(jnp.concatenate([act, grad_second], axis=0))
    act_padded, second_padded = both_padded[:channels], both_padded[channels:]
    second = depthwise(act_padded, taps_two, extent_x, extent_y, 1).astype(jnp.bfloat16)
    sigma = jax.nn.sigmoid(pre)
    grad_pre = (
        depthwise(second_padded, taps_two, extent_x, extent_y, -1)
        * (sigma * (1.0 + pre * (1.0 - sigma)))
    ).astype(jnp.bfloat16)
    grad_first = backmap(weight_one, grad_pre).astype(jnp.bfloat16)
    first_padded = extended(grad_first)
    grad_input = (
        cotangent.astype(jnp.float32) + depthwise(first_padded, taps_one, extent_x, extent_y, -1)
    ).astype(jnp.bfloat16)
    total_cells = extent_x * extent_y * extent_z * lax.axis_size("own") * lax.axis_size("space")
    grad_scale = 1.0 / math.sqrt(float(total_cells))
    local_pw_one = contract_cells(first, grad_pre) * grad_scale
    local_pw_two = contract_cells(second, cotangent) * grad_scale
    local_dw_one = tap_sums(wide_input, grad_first) * grad_scale
    local_dw_two = tap_sums(act_padded, grad_second) * grad_scale
    partials = (local_pw_one, local_pw_two, local_dw_one, local_dw_two)
    scatter, _ = reduce_plan(lax.axis_size("space"))
    blocks = math.prod(f[2] for group in scatter for f in group if f[0] != "own")
    packed, _ = pack_halves(partials, blocks)
    result = unpack_half(tree_reduce(packed), partials)
    return (grad_input, result[0], result[1], result[2], result[3])


def solution(mesh):
    in_specs = (
        P(None, "own", "space", None),
        P(None, "own", "space", None),
        P("own", None),
        P("own", None),
        P(None, "own"),
        P(None, "own"),
    )
    out_specs = (
        P(None, "own", "space", None),
        P("own", None),
        P("own", None),
        P(None, "own"),
        P(None, "own"),
    )
    return jax.shard_map(shards, mesh=mesh, in_specs=in_specs, out_specs=out_specs, check_vma=False)
```

```python
import functools
import math

import jax
import jax.numpy as jnp
from jax import lax
from jax.experimental import pallas as pl
from jax.experimental.pallas import tpu as pltpu
from jax.sharding import PartitionSpec as P

MESH = pl.DeviceIdType.MESH
TILE = 8 * 128

TAP_LIST = [
    (9 * (a + 1) + 3 * (b + 1) + (d + 1), a, b, d)
    for a in (-1, 0, 1)
    for b in (-1, 0, 1)
    for d in (-1, 0, 1)
]


def extended(value, sides, width):
    for axis, dim in sides:
        size, length = (lax.axis_size(axis), value.shape[dim])
        up = [(i, (i + 1) % size) for i in range(size)]
        down = [(j, i) for i, j in up]
        last = lax.slice_in_dim(value, length - width, length, axis=dim)
        first = lax.slice_in_dim(value, 0, width, axis=dim)
        if size == 2:
            theirs = lax.ppermute(jnp.concatenate([first, last], axis=dim), axis, up)
            after = lax.slice_in_dim(theirs, 0, width, axis=dim)
            before = lax.slice_in_dim(theirs, width, 2 * width, axis=dim)
        else:
            before = lax.ppermute(last, axis, up)
            after = lax.ppermute(first, axis, down)
        value = jnp.concatenate([before, value, after], axis=dim)
    return value


def gather_weights(pw_one, pw_two, dw_one, dw_two):
    mine = jnp.concatenate([pw_one.reshape(-1), pw_two.reshape(-1), dw_one.reshape(-1), dw_two.reshape(-1)])
    theirs = lax.ppermute(mine, "own", [(0, 1), (1, 0)])
    first_half = lax.axis_index("own") == 0
    low = jnp.where(first_half, mine, theirs)
    high = jnp.where(first_half, theirs, mine)
    out, offset = [], 0
    for w, dim in ((pw_one, 0), (pw_two, 0), (dw_one, 1), (dw_two, 1)):
        count = w.size
        parts = [h[offset : offset + count].reshape(w.shape) for h in (low, high)]
        out.append(jnp.concatenate(parts, axis=dim))
        offset += count
    return out


def depthwise(padded, weights, extent_x, extent_y, direction):
    running = jnp.zeros((padded.shape[0], extent_x, extent_y, padded.shape[3]), jnp.float32)
    for k, a, b, d in TAP_LIST:
        start_x = 1 + direction * a
        start_y = 1 + direction * b
        shifted = padded[:, start_x : start_x + extent_x, start_y : start_y + extent_y, :]
        shifted = jnp.roll(shifted, -direction * d, axis=3).astype(jnp.float32)
        running = running + weights[k].astype(jnp.float32)[:, None, None, None] * shifted
    return running


def tap_sums(padded, gradient):
    extent_x = gradient.shape[1]
    extent_y = gradient.shape[2]
    grad_float = gradient.astype(jnp.float32)
    columns = []
    for k, a, b, d in TAP_LIST:
        shifted = padded[:, 1 + a : 1 + a + extent_x, 1 + b : 1 + b + extent_y, :]
        shifted = jnp.roll(shifted, -d, axis=3).astype(jnp.float32)
        columns.append(jnp.sum(shifted * grad_float, axis=(1, 2, 3)))
    return jnp.stack(columns, axis=0)


def pointwise(weights, source):
    layout = source.shape
    flattened = source.reshape(layout[0], -1)
    return jnp.dot(weights.T, flattened, preferred_element_type=jnp.float32).reshape(layout)


def backmap(weights, source):
    layout = source.shape
    flattened = source.reshape(layout[0], -1)
    return jnp.dot(weights, flattened, preferred_element_type=jnp.float32).reshape(layout)


def contract_cells(left, right):
    channels = left.shape[0]
    return lax.dot_general(
        left.reshape(channels, -1),
        right.reshape(channels, -1),
        (((1,), (1,)), ((), ())),
        preferred_element_type=jnp.float32,
    )


def reduce_plan(space_size):
    if space_size == 128:
        scatter = ((("space", 1, 2), ("space", 2, 2)), (("own", 0, 2), ("space", 4, 4)))
        return scatter, (("space", 16, 8),)
    factors, stride, rest = [], 1, space_size
    while rest > 2:
        factors.append(("space", stride, 2))
        stride, rest = stride * 2, rest // 2
    scatter = ((("own", 0, 2),) + tuple(factors[:1]),) + tuple((f,) for f in factors[1:])
    return scatter, (("space", stride, rest),)


def group_size(group):
    return math.prod(f[2] for f in group)


def reduce_kernel(plan, x_ref, o_ref, *refs):
    scatter, last = plan
    count = len(scatter)
    bufs = refs[:count]
    recvs = refs[count : 2 * count]
    recv_last, res, send_sem, recv_sem = refs[2 * count :]
    own = lax.axis_index("own")
    space = lax.axis_index("space")

    def coord(factor):
        axis, stride, size = factor
        return own if axis == "own" else (space // stride) % size

    def member(group):
        index = 0
        for factor in group:
            index = index * factor[2] + coord(factor)
        return index

    def device(group, target):
        new_own, new_space = own, space
        for factor in reversed(group):
            axis, stride, size = factor
            value = target % size
            target = target // size
            if axis == "own":
                new_own = value
            else:
                new_space = new_space + (value - coord(factor)) * stride
        return (new_own, new_space)

    barrier = pltpu.get_barrier_semaphore()
    partners = 0
    for group in scatter + (last,):
        size, me = group_size(group), member(group)
        for d in range(1, size):
            pl.semaphore_signal(
                barrier, 1, device_id=device(group, (me + d) % size), device_id_type=MESH
            )
            partners += 1
    pl.semaphore_wait(barrier, partners)

    def exchange(group, base, source_of, dest_of):
        size, me = group_size(group), member(group)
        sends = []
        for d in range(1, size):
            target = (me + d) % size
            copy = pltpu.make_async_remote_copy(
                src_ref=source_of(target),
                dst_ref=dest_of(me),
                send_sem=send_sem.at[base + target],
                recv_sem=recv_sem.at[base + me],
                device_id=device(group, target),
                device_id_type=MESH,
            )
            copy.start()
            sends.append(copy)
        return sends

    def finish(group, base, source_of, dest_of, sends):
        size, me = group_size(group), member(group)
        for d in range(1, size):
            sender = (me + d) % size
            pltpu.make_async_remote_copy(
                src_ref=source_of(sender),
                dst_ref=dest_of(sender),
                send_sem=send_sem.at[base + sender],
                recv_sem=recv_sem.at[base + sender],
                device_id=device(group, sender),
                device_id_type=MESH,
            ).wait_recv()
        for copy in sends:
            copy.wait_send()

    base = 0
    source = x_ref
    for i, group in enumerate(scatter):
        size, me = group_size(group), member(group)
        piece = source.shape[0] // size
        src_of = lambda t, s=source, n=piece: s.at[pl.ds(t * n, n)]
        dst_of = lambda t, r=recvs[i]: r.at[t]
        sends = exchange(group, base, src_of, dst_of)
        finish(group, base, src_of, dst_of, sends)
        total = source[pl.ds(me * piece, piece)]
        for d in range(1, size):
            total = total + recvs[i][(me + d) % size]
        bufs[i][...] = total
        source = bufs[i]
        base += size

    size, me = group_size(last), member(last)
    piece = source.shape[0]
    src_of = lambda t, s=source: s
    dst_of = lambda t: recv_last.at[t]
    sends = exchange(last, base, src_of, dst_of)
    recv_last[me] = source[...]
    finish(last, base, src_of, dst_of, sends)
    total = recv_last[0]
    for k in range(1, size):
        total = total + recv_last[k]
    space_factors = [f for group in scatter for f in group if f[0] != "own"]
    block = 0
    for factor in space_factors:
        block = block * factor[2] + coord(factor)
    res[pl.ds(block * piece, piece)] = total
    base += size

    span = piece
    gathers = [tuple(f for f in group if f[0] != "own") for group in scatter]
    for j in range(len(gathers) - 1, -1, -1):
        group = gathers[j]
        if not group:
            continue
        size, me = group_size(group), member(group)
        prefix = 0
        for earlier in gathers[:j]:
            prefix = prefix * group_size(earlier) + member(earlier)
        start = prefix * size * span
        src_of = lambda t, a=start, n=span: res.at[pl.ds(a + t * n, n)]
        sends = []
        for d in range(1, size):
            target = (me + d) % size
            copy = pltpu.make_async_remote_copy(
                src_ref=src_of(me),
                dst_ref=src_of(me),
                send_sem=send_sem.at[base + target],
                recv_sem=recv_sem.at[base + me],
                device_id=device(group, target),
                device_id_type=MESH,
            )
            copy.start()
            sends.append(copy)
        finish(group, base, src_of, src_of, sends)
        span *= size
        base += size
    o_ref[...] = res[...]


def tree_reduce(packed):
    plan = reduce_plan(lax.axis_size("space"))
    scatter, last = plan
    half = packed.shape[0] // 2
    shapes, length = [], packed.shape[0]
    for group in scatter:
        length //= group_size(group)
        shapes.append((group_size(group), length))
    semaphores = sum(group_size(group) for group in scatter) * 2 + group_size(last)
    scratch = [pltpu.VMEM((n, 8, 128), jnp.float32) for _, n in shapes]
    scratch += [pltpu.VMEM((size, n, 8, 128), jnp.float32) for size, n in shapes]
    scratch += [
        pltpu.VMEM((group_size(last), length, 8, 128), jnp.float32),
        pltpu.VMEM((half, 8, 128), jnp.float32),
        pltpu.SemaphoreType.DMA((semaphores,)),
        pltpu.SemaphoreType.DMA((semaphores,)),
    ]
    return pl.pallas_call(
        functools.partial(reduce_kernel, plan),
        out_shape=jax.ShapeDtypeStruct((half, 8, 128), jnp.float32),
        in_specs=[pl.BlockSpec(memory_space=pltpu.VMEM)],
        out_specs=pl.BlockSpec(memory_space=pltpu.VMEM),
        scratch_shapes=scratch,
        compiler_params=pltpu.CompilerParams(collective_id=0, has_side_effects=True),
        cost_estimate=pl.CostEstimate(
            flops=0, transcendentals=0, bytes_accessed=64 * packed.size * 4
        ),
    )(packed)


def pack_halves(parts, plan):
    scatter, _ = plan
    blocks = math.prod(f[2] for group in scatter for f in group if f[0] != "own")
    halves = []
    for h in range(2):
        pieces = []
        for p in parts[:2]:
            rows = p.shape[0] // 2
            pieces.append(p[h * rows : (h + 1) * rows].reshape(-1))
        for p in parts[2:]:
            cols = p.shape[1] // 2
            pieces.append(p[:, h * cols : (h + 1) * cols].reshape(-1))
        halves.append(jnp.concatenate(pieces))
    real = halves[0].shape[0]
    tiles = -(-real // (TILE * blocks)) * blocks
    flat = jnp.pad(jnp.stack(halves), ((0, 0), (0, tiles * TILE - real)))
    factors = [f for group in scatter for f in group]
    sizes = [f[2] for f in factors if f[0] != "own"]
    flat = flat.reshape([2] + sizes + [tiles * TILE // blocks])
    place = [i for i, f in enumerate(factors) if f[0] == "own"][0]
    order = list(range(1, place + 1)) + [0] + list(range(place + 1, len(factors) + 1))
    return flat.transpose(order).reshape(2 * tiles, 8, 128), real


def unpack_half(reduced, parts):
    flat = reduced.reshape(-1)
    out, offset = [], 0
    for p in parts[:2]:
        shape = (p.shape[0] // 2, p.shape[1])
        out.append(flat[offset : offset + shape[0] * shape[1]].reshape(shape))
        offset += shape[0] * shape[1]
    for p in parts[2:]:
        shape = (p.shape[0], p.shape[1] // 2)
        out.append(flat[offset : offset + shape[0] * shape[1]].reshape(shape))
        offset += shape[0] * shape[1]
    return out


def shards(density, cotangent, pw_one, pw_two, dw_one, dw_two):
    channels, extent_x, extent_y, extent_z = density.shape
    assert lax.axis_size("own") == 2
    weight_one, weight_two, taps_one, taps_two = gather_weights(pw_one, pw_two, dw_one, dw_two)
    rim_width = 1
    wide_input = extended(density, (("own", 1), ("space", 2)), rim_width)
    first = depthwise(wide_input, taps_one, extent_x, extent_y, 1).astype(jnp.bfloat16)
    pre = pointwise(weight_one, first)
    act = jax.nn.silu(pre).astype(jnp.bfloat16)
    act_padded = extended(act, (("own", 1), ("space", 2)), 1)
    second = depthwise(act_padded, taps_two, extent_x, extent_y, 1).astype(jnp.bfloat16)
    grad_second = backmap(weight_two, cotangent).astype(jnp.bfloat16)
    second_padded = extended(grad_second, (("own", 1), ("space", 2)), 1)
    sigma = jax.nn.sigmoid(pre)
    grad_pre = (
        depthwise(second_padded, taps_two, extent_x, extent_y, -1)
        * (sigma * (1.0 + pre * (1.0 - sigma)))
    ).astype(jnp.bfloat16)
    grad_first = backmap(weight_one, grad_pre).astype(jnp.bfloat16)
    first_padded = extended(grad_first, (("own", 1), ("space", 2)), 1)
    grad_input = (
        cotangent.astype(jnp.float32) + depthwise(first_padded, taps_one, extent_x, extent_y, -1)
    ).astype(jnp.bfloat16)
    total_cells = extent_x * extent_y * extent_z * lax.axis_size("own") * lax.axis_size("space")
    grad_scale = 1.0 / math.sqrt(float(total_cells))
    local_pw_one = contract_cells(first, grad_pre) * grad_scale
    local_pw_two = contract_cells(second, cotangent) * grad_scale
    local_dw_one = tap_sums(wide_input, grad_first) * grad_scale
    local_dw_two = tap_sums(act_padded, grad_second) * grad_scale
    partials = (local_pw_one, local_pw_two, local_dw_one, local_dw_two)
    packed, _ = pack_halves(partials, reduce_plan(lax.axis_size("space")))
    result = unpack_half(tree_reduce(packed), partials)
    return (grad_input, result[0], result[1], result[2], result[3])


def solution(mesh):
    in_specs = (
        P(None, "own", "space", None),
        P(None, "own", "space", None),
        P("own", None),
        P("own", None),
        P(None, "own"),
        P(None, "own"),
    )
    out_specs = (
        P(None, "own", "space", None),
        P("own", None),
        P("own", None),
        P(None, "own"),
        P(None, "own"),
    )
    return jax.shard_map(shards, mesh=mesh, in_specs=in_specs, out_specs=out_specs, check_vma=False)
```

```python
import functools
import math

import jax
import jax.numpy as jnp
from jax import lax
from jax.experimental import pallas as pl
from jax.experimental.pallas import tpu as pltpu
from jax.sharding import PartitionSpec as P

MESH = pl.DeviceIdType.MESH
TILE = 8 * 128

TAP_LIST = [
    (9 * (a + 1) + 3 * (b + 1) + (d + 1), a, b, d)
    for a in (-1, 0, 1)
    for b in (-1, 0, 1)
    for d in (-1, 0, 1)
]


def extended(value, sides, width):
    for axis, dim in sides:
        size, length = (lax.axis_size(axis), value.shape[dim])
        up = [(i, (i + 1) % size) for i in range(size)]
        down = [(j, i) for i, j in up]
        last = lax.slice_in_dim(value, length - width, length, axis=dim)
        first = lax.slice_in_dim(value, 0, width, axis=dim)
        if size == 2:
            theirs = lax.ppermute(jnp.concatenate([first, last], axis=dim), axis, up)
            after = lax.slice_in_dim(theirs, 0, width, axis=dim)
            before = lax.slice_in_dim(theirs, width, 2 * width, axis=dim)
        else:
            before = lax.ppermute(last, axis, up)
            after = lax.ppermute(first, axis, down)
        value = jnp.concatenate([before, value, after], axis=dim)
    return value


def gather_weights(pw_one, pw_two, dw_one, dw_two):
    mine = jnp.concatenate([pw_one.reshape(-1), pw_two.reshape(-1), dw_one.reshape(-1), dw_two.reshape(-1)])
    theirs = lax.ppermute(mine, "own", [(0, 1), (1, 0)])
    first_half = lax.axis_index("own") == 0
    low = jnp.where(first_half, mine, theirs)
    high = jnp.where(first_half, theirs, mine)
    out, offset = [], 0
    for w, dim in ((pw_one, 0), (pw_two, 0), (dw_one, 1), (dw_two, 1)):
        count = w.size
        parts = [h[offset : offset + count].reshape(w.shape) for h in (low, high)]
        out.append(jnp.concatenate(parts, axis=dim))
        offset += count
    return out


def ring_z(padded):
    return jnp.concatenate([padded[..., -1:], padded, padded[..., :1]], axis=3)


def depthwise(padded, weights, extent_x, extent_y, direction):
    extent_z = padded.shape[3]
    wide = ring_z(padded)
    running = jnp.zeros((padded.shape[0], extent_x, extent_y, extent_z), jnp.float32)
    for k, a, b, d in TAP_LIST:
        start_x = 1 + direction * a
        start_y = 1 + direction * b
        start_z = 1 + direction * d
        shifted = wide[:, start_x : start_x + extent_x, start_y : start_y + extent_y, start_z : start_z + extent_z]
        running = running + weights[k].astype(jnp.float32)[:, None, None, None] * shifted.astype(jnp.float32)
    return running


def tap_sums(padded, gradient):
    extent_x, extent_y, extent_z = gradient.shape[1:]
    wide = ring_z(padded)
    grad_float = gradient.astype(jnp.float32)
    columns = []
    for k, a, b, d in TAP_LIST:
        shifted = wide[:, 1 + a : 1 + a + extent_x, 1 + b : 1 + b + extent_y, 1 + d : 1 + d + extent_z]
        columns.append(jnp.sum(shifted.astype(jnp.float32) * grad_float, axis=(1, 2, 3)))
    return jnp.stack(columns, axis=0)


def pointwise(weights, source):
    layout = source.shape
    flattened = source.reshape(layout[0], -1)
    return jnp.dot(weights.T, flattened, preferred_element_type=jnp.float32).reshape(layout)


def backmap(weights, source):
    layout = source.shape
    flattened = source.reshape(layout[0], -1)
    return jnp.dot(weights, flattened, preferred_element_type=jnp.float32).reshape(layout)


def contract_cells(left, right):
    channels = left.shape[0]
    return lax.dot_general(
        left.reshape(channels, -1),
        right.reshape(channels, -1),
        (((1,), (1,)), ((), ())),
        preferred_element_type=jnp.float32,
    )


def reduce_plan(space_size):
    if space_size == 128:
        scatter = ((("own", 0, 2), ("space", 1, 2)), (("space", 2, 2), ("space", 4, 4)))
        return scatter, (("space", 16, 8),)
    factors, stride, rest = [], 1, space_size
    while rest > 2:
        factors.append(("space", stride, 2))
        stride, rest = stride * 2, rest // 2
    scatter = ((("own", 0, 2),) + tuple(factors[:1]),) + tuple((f,) for f in factors[1:])
    return scatter, (("space", stride, rest),)


def group_size(group):
    return math.prod(f[2] for f in group)


def reduce_kernel(plan, x_ref, o_ref, *refs):
    scatter, last = plan
    count = len(scatter)
    bufs = refs[:count]
    recvs = refs[count : 2 * count]
    recv_last, res, send_sem, recv_sem = refs[2 * count :]
    own = lax.axis_index("own")
    space = lax.axis_index("space")

    def coord(factor):
        axis, stride, size = factor
        return own if axis == "own" else (space // stride) % size

    def member(group):
        index = 0
        for factor in group:
            index = index * factor[2] + coord(factor)
        return index

    def device(group, target):
        new_own, new_space = own, space
        for factor in reversed(group):
            axis, stride, size = factor
            value = target % size
            target = target // size
            if axis == "own":
                new_own = value
            else:
                new_space = new_space + (value - coord(factor)) * stride
        return (new_own, new_space)

    barrier = pltpu.get_barrier_semaphore()
    partners = 0
    for group in scatter + (last,):
        size, me = group_size(group), member(group)
        for d in range(1, size):
            pl.semaphore_signal(
                barrier, 1, device_id=device(group, (me + d) % size), device_id_type=MESH
            )
            partners += 1
    pl.semaphore_wait(barrier, partners)

    def exchange(group, base, source_of, dest_of):
        size, me = group_size(group), member(group)
        sends = []
        for d in range(1, size):
            target = (me + d) % size
            copy = pltpu.make_async_remote_copy(
                src_ref=source_of(target),
                dst_ref=dest_of(me),
                send_sem=send_sem.at[base + target],
                recv_sem=recv_sem.at[base + me],
                device_id=device(group, target),
                device_id_type=MESH,
            )
            copy.start()
            sends.append(copy)
        return sends

    def finish(group, base, source_of, dest_of, sends):
        size, me = group_size(group), member(group)
        for d in range(1, size):
            sender = (me + d) % size
            pltpu.make_async_remote_copy(
                src_ref=source_of(sender),
                dst_ref=dest_of(sender),
                send_sem=send_sem.at[base + sender],
                recv_sem=recv_sem.at[base + sender],
                device_id=device(group, sender),
                device_id_type=MESH,
            ).wait_recv()
        for copy in sends:
            copy.wait_send()

    base = 0
    source = x_ref
    for i, group in enumerate(scatter):
        size, me = group_size(group), member(group)
        piece = source.shape[0] // size
        src_of = lambda t, s=source, n=piece: s.at[pl.ds(t * n, n)]
        dst_of = lambda t, r=recvs[i]: r.at[t]
        sends = exchange(group, base, src_of, dst_of)
        finish(group, base, src_of, dst_of, sends)
        total = source[pl.ds(me * piece, piece)]
        for d in range(1, size):
            total = total + recvs[i][(me + d) % size]
        bufs[i][...] = total
        source = bufs[i]
        base += size

    size, me = group_size(last), member(last)
    piece = source.shape[0]
    src_of = lambda t, s=source: s
    dst_of = lambda t: recv_last.at[t]
    sends = exchange(last, base, src_of, dst_of)
    recv_last[me] = source[...]
    finish(last, base, src_of, dst_of, sends)
    total = recv_last[0]
    for k in range(1, size):
        total = total + recv_last[k]
    space_factors = [f for group in scatter for f in group if f[0] != "own"]
    block = 0
    for factor in space_factors:
        block = block * factor[2] + coord(factor)
    res[pl.ds(block * piece, piece)] = total
    base += size

    span = piece
    gathers = [tuple(f for f in group if f[0] != "own") for group in scatter]
    for j in range(len(gathers) - 1, -1, -1):
        group = gathers[j]
        if not group:
            continue
        size, me = group_size(group), member(group)
        prefix = 0
        for earlier in gathers[:j]:
            prefix = prefix * group_size(earlier) + member(earlier)
        start = prefix * size * span
        src_of = lambda t, a=start, n=span: res.at[pl.ds(a + t * n, n)]
        sends = []
        for d in range(1, size):
            target = (me + d) % size
            copy = pltpu.make_async_remote_copy(
                src_ref=src_of(me),
                dst_ref=src_of(me),
                send_sem=send_sem.at[base + target],
                recv_sem=recv_sem.at[base + me],
                device_id=device(group, target),
                device_id_type=MESH,
            )
            copy.start()
            sends.append(copy)
        finish(group, base, src_of, src_of, sends)
        span *= size
        base += size
    o_ref[...] = res[...]


def tree_reduce(packed):
    plan = reduce_plan(lax.axis_size("space"))
    scatter, last = plan
    half = packed.shape[0] // 2
    shapes, length = [], packed.shape[0]
    for group in scatter:
        length //= group_size(group)
        shapes.append((group_size(group), length))
    semaphores = sum(group_size(group) for group in scatter) * 2 + group_size(last)
    scratch = [pltpu.VMEM((n, 8, 128), jnp.float32) for _, n in shapes]
    scratch += [pltpu.VMEM((size, n, 8, 128), jnp.float32) for size, n in shapes]
    scratch += [
        pltpu.VMEM((group_size(last), length, 8, 128), jnp.float32),
        pltpu.VMEM((half, 8, 128), jnp.float32),
        pltpu.SemaphoreType.DMA((semaphores,)),
        pltpu.SemaphoreType.DMA((semaphores,)),
    ]
    return pl.pallas_call(
        functools.partial(reduce_kernel, plan),
        out_shape=jax.ShapeDtypeStruct((half, 8, 128), jnp.float32),
        in_specs=[pl.BlockSpec(memory_space=pltpu.VMEM)],
        out_specs=pl.BlockSpec(memory_space=pltpu.VMEM),
        scratch_shapes=scratch,
        compiler_params=pltpu.CompilerParams(collective_id=0, has_side_effects=True),
        cost_estimate=pl.CostEstimate(
            flops=0, transcendentals=0, bytes_accessed=64 * packed.size * 4
        ),
    )(packed)


def pack_halves(parts, blocks):
    halves = []
    for h in range(2):
        pieces = []
        for p in parts[:2]:
            rows = p.shape[0] // 2
            pieces.append(p[h * rows : (h + 1) * rows].reshape(-1))
        for p in parts[2:]:
            cols = p.shape[1] // 2
            pieces.append(p[:, h * cols : (h + 1) * cols].reshape(-1))
        halves.append(jnp.concatenate(pieces))
    real = halves[0].shape[0]
    tiles = -(-real // (TILE * blocks)) * blocks
    flat = jnp.stack(halves)
    flat = jnp.pad(flat, ((0, 0), (0, tiles * TILE - real)))
    return flat.reshape(2 * tiles, 8, 128), real


def unpack_half(reduced, parts):
    flat = reduced.reshape(-1)
    out, offset = [], 0
    for p in parts[:2]:
        shape = (p.shape[0] // 2, p.shape[1])
        out.append(flat[offset : offset + shape[0] * shape[1]].reshape(shape))
        offset += shape[0] * shape[1]
    for p in parts[2:]:
        shape = (p.shape[0], p.shape[1] // 2)
        out.append(flat[offset : offset + shape[0] * shape[1]].reshape(shape))
        offset += shape[0] * shape[1]
    return out


def shards(density, cotangent, pw_one, pw_two, dw_one, dw_two):
    channels, extent_x, extent_y, extent_z = density.shape
    assert lax.axis_size("own") == 2
    weight_one, weight_two, taps_one, taps_two = gather_weights(pw_one, pw_two, dw_one, dw_two)
    rim_width = 1
    wide_input = extended(density, (("own", 1), ("space", 2)), rim_width)
    first = depthwise(wide_input, taps_one, extent_x, extent_y, 1).astype(jnp.bfloat16)
    pre = pointwise(weight_one, first)
    act = jax.nn.silu(pre).astype(jnp.bfloat16)
    act_padded = extended(act, (("own", 1), ("space", 2)), 1)
    second = depthwise(act_padded, taps_two, extent_x, extent_y, 1).astype(jnp.bfloat16)
    grad_second = backmap(weight_two, cotangent).astype(jnp.bfloat16)
    second_padded = extended(grad_second, (("own", 1), ("space", 2)), 1)
    sigma = jax.nn.sigmoid(pre)
    grad_pre = (
        depthwise(second_padded, taps_two, extent_x, extent_y, -1)
        * (sigma * (1.0 + pre * (1.0 - sigma)))
    ).astype(jnp.bfloat16)
    grad_first = backmap(weight_one, grad_pre).astype(jnp.bfloat16)
    first_padded = extended(grad_first, (("own", 1), ("space", 2)), 1)
    grad_input = (
        cotangent.astype(jnp.float32) + depthwise(first_padded, taps_one, extent_x, extent_y, -1)
    ).astype(jnp.bfloat16)
    total_cells = extent_x * extent_y * extent_z * lax.axis_size("own") * lax.axis_size("space")
    grad_scale = 1.0 / math.sqrt(float(total_cells))
    local_pw_one = contract_cells(first, grad_pre) * grad_scale
    local_pw_two = contract_cells(second, cotangent) * grad_scale
    local_dw_one = tap_sums(wide_input, grad_first) * grad_scale
    local_dw_two = tap_sums(act_padded, grad_second) * grad_scale
    partials = (local_pw_one, local_pw_two, local_dw_one, local_dw_two)
    scatter, _ = reduce_plan(lax.axis_size("space"))
    blocks = math.prod(f[2] for group in scatter for f in group if f[0] != "own")
    packed, _ = pack_halves(partials, blocks)
    result = unpack_half(tree_reduce(packed), partials)
    return (grad_input, result[0], result[1], result[2], result[3])


def solution(mesh):
    in_specs = (
        P(None, "own", "space", None),
        P(None, "own", "space", None),
        P("own", None),
        P("own", None),
        P(None, "own"),
        P(None, "own"),
    )
    out_specs = (
        P(None, "own", "space", None),
        P("own", None),
        P("own", None),
        P(None, "own"),
        P(None, "own"),
    )
    return jax.shard_map(shards, mesh=mesh, in_specs=in_specs, out_specs=out_specs, check_vma=False)
```

```python
import functools
import math

import jax
import jax.numpy as jnp
from jax import lax
from jax.experimental import pallas as pl
from jax.experimental.pallas import tpu as pltpu
from jax.sharding import PartitionSpec as P

MESH = pl.DeviceIdType.MESH
TILE = 8 * 128

TAP_LIST = [
    (9 * (a + 1) + 3 * (b + 1) + (d + 1), a, b, d)
    for a in (-1, 0, 1)
    for b in (-1, 0, 1)
    for d in (-1, 0, 1)
]


def extended(value, width=1, wrap_x=False):
    swap = [(0, 1), (1, 0)]
    partner = lax.ppermute(value, "own", swap)
    count, length = lax.axis_size("space"), value.shape[2]
    up = [(i, (i + 1) % count) for i in range(count)]
    down = [(j, i) for i, j in up]
    if wrap_x:
        unique = jnp.concatenate([value, partner], axis=1)
        before = lax.ppermute(unique[:, :, length - width :], "space", up)
        after = lax.ppermute(unique[:, :, :width], "space", down)
        extent = value.shape[1]

        def wrap(v):
            return jnp.concatenate([v[:, extent:], v], axis=1)

        return jnp.concatenate([wrap(before), wrap(unique), wrap(after)], axis=2)
    value = jnp.concatenate([partner[:, -1:], value, partner[:, :1]], axis=1)
    before = lax.ppermute(value[:, :, length - width :], "space", up)
    after = lax.ppermute(value[:, :, :width], "space", down)
    return jnp.concatenate([before, value, after], axis=2)


def gather_weights(pw_one, pw_two, dw_one, dw_two):
    mine = jnp.concatenate([pw_one.reshape(-1), pw_two.reshape(-1), dw_one.reshape(-1), dw_two.reshape(-1)])
    theirs = lax.ppermute(mine, "own", [(0, 1), (1, 0)])
    first_half = lax.axis_index("own") == 0
    low = jnp.where(first_half, mine, theirs)
    high = jnp.where(first_half, theirs, mine)
    out, offset = [], 0
    for w, dim in ((pw_one, 0), (pw_two, 0), (dw_one, 1), (dw_two, 1)):
        count = w.size
        parts = [h[offset : offset + count].reshape(w.shape) for h in (low, high)]
        out.append(jnp.concatenate(parts, axis=dim))
        offset += count
    return out


def ring_z(padded):
    return jnp.concatenate([padded[..., -1:], padded, padded[..., :1]], axis=3)


def depthwise(padded, weights, extent_x, extent_y, direction):
    extent_z = padded.shape[3]
    wide = ring_z(padded)
    running = jnp.zeros((padded.shape[0], extent_x, extent_y, extent_z), jnp.float32)
    for k, a, b, d in TAP_LIST:
        start_x = 1 + direction * a
        start_y = 1 + direction * b
        start_z = 1 + direction * d
        shifted = wide[:, start_x : start_x + extent_x, start_y : start_y + extent_y, start_z : start_z + extent_z]
        running = running + weights[k].astype(jnp.float32)[:, None, None, None] * shifted.astype(jnp.float32)
    return running


def tap_sums(padded, gradient):
    extent_x, extent_y, extent_z = gradient.shape[1:]
    wide = ring_z(padded)
    grad_float = gradient.astype(jnp.float32)
    columns = []
    for k, a, b, d in TAP_LIST:
        shifted = wide[:, 1 + a : 1 + a + extent_x, 1 + b : 1 + b + extent_y, 1 + d : 1 + d + extent_z]
        columns.append(jnp.sum(shifted.astype(jnp.float32) * grad_float, axis=(1, 2, 3)))
    return jnp.stack(columns, axis=0)


def pointwise(weights, source):
    layout = source.shape
    flattened = source.reshape(layout[0], -1)
    return jnp.dot(weights.T, flattened, preferred_element_type=jnp.float32).reshape(layout)


def backmap(weights, source):
    layout = source.shape
    flattened = source.reshape(layout[0], -1)
    return jnp.dot(weights, flattened, preferred_element_type=jnp.float32).reshape(layout)


def contract_cells(left, right):
    channels = left.shape[0]
    return lax.dot_general(
        left.reshape(channels, -1),
        right.reshape(channels, -1),
        (((1,), (1,)), ((), ())),
        preferred_element_type=jnp.float32,
    )


def reduce_plan(space_size):
    if space_size == 128:
        scatter = ((("own", 0, 2), ("space", 1, 2)), (("space", 2, 2), ("space", 4, 4)))
        return scatter, (("space", 16, 8),)
    factors, stride, rest = [], 1, space_size
    while rest > 2:
        factors.append(("space", stride, 2))
        stride, rest = stride * 2, rest // 2
    scatter = ((("own", 0, 2),) + tuple(factors[:1]),) + tuple((f,) for f in factors[1:])
    return scatter, (("space", stride, rest),)


def group_size(group):
    return math.prod(f[2] for f in group)


def reduce_kernel(plan, x_ref, o_ref, *refs):
    scatter, last = plan
    count = len(scatter)
    bufs = refs[:count]
    recvs = refs[count : 2 * count]
    recv_last, res, send_sem, recv_sem = refs[2 * count :]
    own = lax.axis_index("own")
    space = lax.axis_index("space")

    def coord(factor):
        axis, stride, size = factor
        return own if axis == "own" else (space // stride) % size

    def member(group):
        index = 0
        for factor in group:
            index = index * factor[2] + coord(factor)
        return index

    def device(group, target):
        new_own, new_space = own, space
        for factor in reversed(group):
            axis, stride, size = factor
            value = target % size
            target = target // size
            if axis == "own":
                new_own = value
            else:
                new_space = new_space + (value - coord(factor)) * stride
        return (new_own, new_space)

    barrier = pltpu.get_barrier_semaphore()
    partners = 0
    for group in scatter + (last,):
        size, me = group_size(group), member(group)
        for d in range(1, size):
            pl.semaphore_signal(
                barrier, 1, device_id=device(group, (me + d) % size), device_id_type=MESH
            )
            partners += 1
    pl.semaphore_wait(barrier, partners)

    def exchange(group, base, source_of, dest_of):
        size, me = group_size(group), member(group)
        sends = []
        for d in range(1, size):
            target = (me + d) % size
            copy = pltpu.make_async_remote_copy(
                src_ref=source_of(target),
                dst_ref=dest_of(me),
                send_sem=send_sem.at[base + target],
                recv_sem=recv_sem.at[base + me],
                device_id=device(group, target),
                device_id_type=MESH,
            )
            copy.start()
            sends.append(copy)
        return sends

    def finish(group, base, source_of, dest_of, sends):
        size, me = group_size(group), member(group)
        for d in range(1, size):
            sender = (me + d) % size
            pltpu.make_async_remote_copy(
                src_ref=source_of(sender),
                dst_ref=dest_of(sender),
                send_sem=send_sem.at[base + sender],
                recv_sem=recv_sem.at[base + sender],
                device_id=device(group, sender),
                device_id_type=MESH,
            ).wait_recv()
        for copy in sends:
            copy.wait_send()

    base = 0
    source = x_ref
    for i, group in enumerate(scatter):
        size, me = group_size(group), member(group)
        piece = source.shape[0] // size
        src_of = lambda t, s=source, n=piece: s.at[pl.ds(t * n, n)]
        dst_of = lambda t, r=recvs[i]: r.at[t]
        sends = exchange(group, base, src_of, dst_of)
        finish(group, base, src_of, dst_of, sends)
        total = source[pl.ds(me * piece, piece)]
        for d in range(1, size):
            total = total + recvs[i][(me + d) % size]
        bufs[i][...] = total
        source = bufs[i]
        base += size

    size, me = group_size(last), member(last)
    piece = source.shape[0]
    src_of = lambda t, s=source: s
    dst_of = lambda t: recv_last.at[t]
    sends = exchange(last, base, src_of, dst_of)
    recv_last[me] = source[...]
    finish(last, base, src_of, dst_of, sends)
    total = recv_last[0]
    for k in range(1, size):
        total = total + recv_last[k]
    space_factors = [f for group in scatter for f in group if f[0] != "own"]
    block = 0
    for factor in space_factors:
        block = block * factor[2] + coord(factor)
    res[pl.ds(block * piece, piece)] = total
    base += size

    span = piece
    gathers = [tuple(f for f in group if f[0] != "own") for group in scatter]
    for j in range(len(gathers) - 1, -1, -1):
        group = gathers[j]
        if not group:
            continue
        size, me = group_size(group), member(group)
        prefix = 0
        for earlier in gathers[:j]:
            prefix = prefix * group_size(earlier) + member(earlier)
        start = prefix * size * span
        src_of = lambda t, a=start, n=span: res.at[pl.ds(a + t * n, n)]
        sends = []
        for d in range(1, size):
            target = (me + d) % size
            copy = pltpu.make_async_remote_copy(
                src_ref=src_of(me),
                dst_ref=src_of(me),
                send_sem=send_sem.at[base + target],
                recv_sem=recv_sem.at[base + me],
                device_id=device(group, target),
                device_id_type=MESH,
            )
            copy.start()
            sends.append(copy)
        finish(group, base, src_of, src_of, sends)
        span *= size
        base += size
    o_ref[...] = res[...]


def tree_reduce(packed):
    plan = reduce_plan(lax.axis_size("space"))
    scatter, last = plan
    half = packed.shape[0] // 2
    shapes, length = [], packed.shape[0]
    for group in scatter:
        length //= group_size(group)
        shapes.append((group_size(group), length))
    semaphores = sum(group_size(group) for group in scatter) * 2 + group_size(last)
    scratch = [pltpu.VMEM((n, 8, 128), jnp.float32) for _, n in shapes]
    scratch += [pltpu.VMEM((size, n, 8, 128), jnp.float32) for size, n in shapes]
    scratch += [
        pltpu.VMEM((group_size(last), length, 8, 128), jnp.float32),
        pltpu.VMEM((half, 8, 128), jnp.float32),
        pltpu.SemaphoreType.DMA((semaphores,)),
        pltpu.SemaphoreType.DMA((semaphores,)),
    ]
    return pl.pallas_call(
        functools.partial(reduce_kernel, plan),
        out_shape=jax.ShapeDtypeStruct((half, 8, 128), jnp.float32),
        in_specs=[pl.BlockSpec(memory_space=pltpu.VMEM)],
        out_specs=pl.BlockSpec(memory_space=pltpu.VMEM),
        scratch_shapes=scratch,
        compiler_params=pltpu.CompilerParams(collective_id=0, has_side_effects=True),
        cost_estimate=pl.CostEstimate(
            flops=0, transcendentals=0, bytes_accessed=64 * packed.size * 4
        ),
    )(packed)


def pack_halves(parts, blocks):
    halves = []
    for h in range(2):
        pieces = []
        for p in parts[:2]:
            rows = p.shape[0] // 2
            pieces.append(p[h * rows : (h + 1) * rows].reshape(-1))
        for p in parts[2:]:
            cols = p.shape[1] // 2
            pieces.append(p[:, h * cols : (h + 1) * cols].reshape(-1))
        halves.append(jnp.concatenate(pieces))
    real = halves[0].shape[0]
    tiles = -(-real // (TILE * blocks)) * blocks
    flat = jnp.stack(halves)
    flat = jnp.pad(flat, ((0, 0), (0, tiles * TILE - real)))
    return flat.reshape(2 * tiles, 8, 128), real


def unpack_half(reduced, parts):
    flat = reduced.reshape(-1)
    out, offset = [], 0
    for p in parts[:2]:
        shape = (p.shape[0] // 2, p.shape[1])
        out.append(flat[offset : offset + shape[0] * shape[1]].reshape(shape))
        offset += shape[0] * shape[1]
    for p in parts[2:]:
        shape = (p.shape[0], p.shape[1] // 2)
        out.append(flat[offset : offset + shape[0] * shape[1]].reshape(shape))
        offset += shape[0] * shape[1]
    return out


def shards(density, cotangent, pw_one, pw_two, dw_one, dw_two):
    channels, extent_x, extent_y, extent_z = density.shape
    assert lax.axis_size("own") == 2
    weight_one, weight_two, taps_one, taps_two = gather_weights(pw_one, pw_two, dw_one, dw_two)
    widest = extended(density, width=2, wrap_x=True)
    wide_input = widest[:, 1 : 3 + extent_x, 1 : 3 + extent_y]
    first_wide = depthwise(widest, taps_one, 2 + extent_x, 2 + extent_y, 1).astype(jnp.bfloat16)
    pre_wide = pointwise(weight_one, first_wide)
    act_padded = jax.nn.silu(pre_wide).astype(jnp.bfloat16)
    core = (slice(None), slice(1, 1 + extent_x), slice(1, 1 + extent_y))
    first, pre = first_wide[core], pre_wide[core]
    second = depthwise(act_padded, taps_two, extent_x, extent_y, 1).astype(jnp.bfloat16)
    grad_second = backmap(weight_two, cotangent).astype(jnp.bfloat16)
    second_padded = extended(grad_second)
    sigma = jax.nn.sigmoid(pre)
    grad_pre = (
        depthwise(second_padded, taps_two, extent_x, extent_y, -1)
        * (sigma * (1.0 + pre * (1.0 - sigma)))
    ).astype(jnp.bfloat16)
    grad_first = backmap(weight_one, grad_pre).astype(jnp.bfloat16)
    first_padded = extended(grad_first)
    grad_input = (
        cotangent.astype(jnp.float32) + depthwise(first_padded, taps_one, extent_x, extent_y, -1)
    ).astype(jnp.bfloat16)
    total_cells = extent_x * extent_y * extent_z * lax.axis_size("own") * lax.axis_size("space")
    grad_scale = 1.0 / math.sqrt(float(total_cells))
    local_pw_one = contract_cells(first, grad_pre) * grad_scale
    local_pw_two = contract_cells(second, cotangent) * grad_scale
    local_dw_one = tap_sums(wide_input, grad_first) * grad_scale
    local_dw_two = tap_sums(act_padded, grad_second) * grad_scale
    partials = (local_pw_one, local_pw_two, local_dw_one, local_dw_two)
    scatter, _ = reduce_plan(lax.axis_size("space"))
    blocks = math.prod(f[2] for group in scatter for f in group if f[0] != "own")
    packed, _ = pack_halves(partials, blocks)
    result = unpack_half(tree_reduce(packed), partials)
    return (grad_input, result[0], result[1], result[2], result[3])


def solution(mesh):
    in_specs = (
        P(None, "own", "space", None),
        P(None, "own", "space", None),
        P("own", None),
        P("own", None),
        P(None, "own"),
        P(None, "own"),
    )
    out_specs = (
        P(None, "own", "space", None),
        P("own", None),
        P("own", None),
        P(None, "own"),
        P(None, "own"),
    )
    return jax.shard_map(shards, mesh=mesh, in_specs=in_specs, out_specs=out_specs, check_vma=False)
```

```python
import functools
import math

import jax
import jax.numpy as jnp
from jax import lax
from jax.experimental import pallas as pl
from jax.experimental.pallas import tpu as pltpu
from jax.sharding import PartitionSpec as P

MESH = pl.DeviceIdType.MESH
TILE = 8 * 128

TAP_LIST = [
    (9 * (a + 1) + 3 * (b + 1) + (d + 1), a, b, d)
    for a in (-1, 0, 1)
    for b in (-1, 0, 1)
    for d in (-1, 0, 1)
]


def extended(value, sides, width):
    for axis, dim in sides:
        size, length = (lax.axis_size(axis), value.shape[dim])
        up = [(i, (i + 1) % size) for i in range(size)]
        down = [(j, i) for i, j in up]
        last = lax.slice_in_dim(value, length - width, length, axis=dim)
        first = lax.slice_in_dim(value, 0, width, axis=dim)
        if size == 2:
            theirs = lax.ppermute(jnp.concatenate([first, last], axis=dim), axis, up)
            after = lax.slice_in_dim(theirs, 0, width, axis=dim)
            before = lax.slice_in_dim(theirs, width, 2 * width, axis=dim)
        else:
            before = lax.ppermute(last, axis, up)
            after = lax.ppermute(first, axis, down)
        value = jnp.concatenate([before, value, after], axis=dim)
    return value


def extended_at_once(value):
    count = lax.axis_size("space")
    up = [(i, (i + 1) % count) for i in range(count)]
    down = [(j, i) for i, j in up]
    cross_up = [(o * count + i, (1 - o) * count + j) for o in range(2) for i, j in up]
    cross_down = [(o * count + i, (1 - o) * count + j) for o in range(2) for i, j in down]
    first = value[:, :, :1]
    last = value[:, :, -1:]
    partner = lax.ppermute(value, "own", [(0, 1), (1, 0)])
    below = lax.ppermute(last, "space", up)
    above = lax.ppermute(first, "space", down)
    corner_below = lax.ppermute(last, ("own", "space"), cross_up)
    corner_above = lax.ppermute(first, ("own", "space"), cross_down)

    def row(theirs, mine):
        return jnp.concatenate([theirs[:, -1:], mine, theirs[:, :1]], axis=1)

    return jnp.concatenate(
        [row(corner_below, below), row(partner, value), row(corner_above, above)], axis=2
    )


def gather_weights(pw_one, pw_two, dw_one, dw_two):
    mine = jnp.concatenate([pw_one.reshape(-1), pw_two.reshape(-1), dw_one.reshape(-1), dw_two.reshape(-1)])
    theirs = lax.ppermute(mine, "own", [(0, 1), (1, 0)])
    first_half = lax.axis_index("own") == 0
    low = jnp.where(first_half, mine, theirs)
    high = jnp.where(first_half, theirs, mine)
    out, offset = [], 0
    for w, dim in ((pw_one, 0), (pw_two, 0), (dw_one, 1), (dw_two, 1)):
        count = w.size
        parts = [h[offset : offset + count].reshape(w.shape) for h in (low, high)]
        out.append(jnp.concatenate(parts, axis=dim))
        offset += count
    return out


def ring_z(padded):
    return jnp.concatenate([padded[..., -1:], padded, padded[..., :1]], axis=3)


def depthwise(padded, weights, extent_x, extent_y, direction):
    extent_z = padded.shape[3]
    wide = ring_z(padded)
    running = jnp.zeros((padded.shape[0], extent_x, extent_y, extent_z), jnp.float32)
    for k, a, b, d in TAP_LIST:
        start_x = 1 + direction * a
        start_y = 1 + direction * b
        start_z = 1 + direction * d
        shifted = wide[:, start_x : start_x + extent_x, start_y : start_y + extent_y, start_z : start_z + extent_z]
        running = running + weights[k].astype(jnp.float32)[:, None, None, None] * shifted.astype(jnp.float32)
    return running


def tap_sums(padded, gradient):
    extent_x, extent_y, extent_z = gradient.shape[1:]
    wide = ring_z(padded)
    grad_float = gradient.astype(jnp.float32)
    columns = []
    for k, a, b, d in TAP_LIST:
        shifted = wide[:, 1 + a : 1 + a + extent_x, 1 + b : 1 + b + extent_y, 1 + d : 1 + d + extent_z]
        columns.append(jnp.sum(shifted.astype(jnp.float32) * grad_float, axis=(1, 2, 3)))
    return jnp.stack(columns, axis=0)


def pointwise(weights, source):
    layout = source.shape
    flattened = source.reshape(layout[0], -1)
    return jnp.dot(weights.T, flattened, preferred_element_type=jnp.float32).reshape(layout)


def backmap(weights, source):
    layout = source.shape
    flattened = source.reshape(layout[0], -1)
    return jnp.dot(weights, flattened, preferred_element_type=jnp.float32).reshape(layout)


def contract_cells(left, right):
    channels = left.shape[0]
    return lax.dot_general(
        left.reshape(channels, -1),
        right.reshape(channels, -1),
        (((1,), (1,)), ((), ())),
        preferred_element_type=jnp.float32,
    )


def reduce_plan(space_size):
    if space_size == 128:
        scatter = ((("own", 0, 2), ("space", 1, 2)), (("space", 2, 2), ("space", 4, 4)))
        return scatter, (("space", 16, 8),)
    factors, stride, rest = [], 1, space_size
    while rest > 2:
        factors.append(("space", stride, 2))
        stride, rest = stride * 2, rest // 2
    scatter = ((("own", 0, 2),) + tuple(factors[:1]),) + tuple((f,) for f in factors[1:])
    return scatter, (("space", stride, rest),)


def group_size(group):
    return math.prod(f[2] for f in group)


def reduce_kernel(plan, x_ref, o_ref, *refs):
    scatter, last = plan
    count = len(scatter)
    bufs = refs[:count]
    recvs = refs[count : 2 * count]
    recv_last, res, send_sem, recv_sem = refs[2 * count :]
    own = lax.axis_index("own")
    space = lax.axis_index("space")

    def coord(factor):
        axis, stride, size = factor
        return own if axis == "own" else (space // stride) % size

    def member(group):
        index = 0
        for factor in group:
            index = index * factor[2] + coord(factor)
        return index

    def device(group, target):
        new_own, new_space = own, space
        for factor in reversed(group):
            axis, stride, size = factor
            value = target % size
            target = target // size
            if axis == "own":
                new_own = value
            else:
                new_space = new_space + (value - coord(factor)) * stride
        return (new_own, new_space)

    barrier = pltpu.get_barrier_semaphore()
    partners = 0
    for group in scatter + (last,):
        size, me = group_size(group), member(group)
        for d in range(1, size):
            pl.semaphore_signal(
                barrier, 1, device_id=device(group, (me + d) % size), device_id_type=MESH
            )
            partners += 1
    pl.semaphore_wait(barrier, partners)

    def exchange(group, base, source_of, dest_of):
        size, me = group_size(group), member(group)
        sends = []
        for d in range(1, size):
            target = (me + d) % size
            copy = pltpu.make_async_remote_copy(
                src_ref=source_of(target),
                dst_ref=dest_of(me),
                send_sem=send_sem.at[base + target],
                recv_sem=recv_sem.at[base + me],
                device_id=device(group, target),
                device_id_type=MESH,
            )
            copy.start()
            sends.append(copy)
        return sends

    def finish(group, base, source_of, dest_of, sends):
        size, me = group_size(group), member(group)
        for d in range(1, size):
            sender = (me + d) % size
            pltpu.make_async_remote_copy(
                src_ref=source_of(sender),
                dst_ref=dest_of(sender),
                send_sem=send_sem.at[base + sender],
                recv_sem=recv_sem.at[base + sender],
                device_id=device(group, sender),
                device_id_type=MESH,
            ).wait_recv()
        for copy in sends:
            copy.wait_send()

    base = 0
    source = x_ref
    for i, group in enumerate(scatter):
        size, me = group_size(group), member(group)
        piece = source.shape[0] // size
        src_of = lambda t, s=source, n=piece: s.at[pl.ds(t * n, n)]
        dst_of = lambda t, r=recvs[i]: r.at[t]
        sends = exchange(group, base, src_of, dst_of)
        finish(group, base, src_of, dst_of, sends)
        total = source[pl.ds(me * piece, piece)]
        for d in range(1, size):
            total = total + recvs[i][(me + d) % size]
        bufs[i][...] = total
        source = bufs[i]
        base += size

    size, me = group_size(last), member(last)
    piece = source.shape[0]
    src_of = lambda t, s=source: s
    dst_of = lambda t: recv_last.at[t]
    sends = exchange(last, base, src_of, dst_of)
    recv_last[me] = source[...]
    finish(last, base, src_of, dst_of, sends)
    total = recv_last[0]
    for k in range(1, size):
        total = total + recv_last[k]
    space_factors = [f for group in scatter for f in group if f[0] != "own"]
    block = 0
    for factor in space_factors:
        block = block * factor[2] + coord(factor)
    res[pl.ds(block * piece, piece)] = total
    base += size

    span = piece
    gathers = [tuple(f for f in group if f[0] != "own") for group in scatter]
    for j in range(len(gathers) - 1, -1, -1):
        group = gathers[j]
        if not group:
            continue
        size, me = group_size(group), member(group)
        prefix = 0
        for earlier in gathers[:j]:
            prefix = prefix * group_size(earlier) + member(earlier)
        start = prefix * size * span
        src_of = lambda t, a=start, n=span: res.at[pl.ds(a + t * n, n)]
        sends = []
        for d in range(1, size):
            target = (me + d) % size
            copy = pltpu.make_async_remote_copy(
                src_ref=src_of(me),
                dst_ref=src_of(me),
                send_sem=send_sem.at[base + target],
                recv_sem=recv_sem.at[base + me],
                device_id=device(group, target),
                device_id_type=MESH,
            )
            copy.start()
            sends.append(copy)
        finish(group, base, src_of, src_of, sends)
        span *= size
        base += size
    o_ref[...] = res[...]


def tree_reduce(packed):
    plan = reduce_plan(lax.axis_size("space"))
    scatter, last = plan
    half = packed.shape[0] // 2
    shapes, length = [], packed.shape[0]
    for group in scatter:
        length //= group_size(group)
        shapes.append((group_size(group), length))
    semaphores = sum(group_size(group) for group in scatter) * 2 + group_size(last)
    scratch = [pltpu.VMEM((n, 8, 128), jnp.float32) for _, n in shapes]
    scratch += [pltpu.VMEM((size, n, 8, 128), jnp.float32) for size, n in shapes]
    scratch += [
        pltpu.VMEM((group_size(last), length, 8, 128), jnp.float32),
        pltpu.VMEM((half, 8, 128), jnp.float32),
        pltpu.SemaphoreType.DMA((semaphores,)),
        pltpu.SemaphoreType.DMA((semaphores,)),
    ]
    return pl.pallas_call(
        functools.partial(reduce_kernel, plan),
        out_shape=jax.ShapeDtypeStruct((half, 8, 128), jnp.float32),
        in_specs=[pl.BlockSpec(memory_space=pltpu.VMEM)],
        out_specs=pl.BlockSpec(memory_space=pltpu.VMEM),
        scratch_shapes=scratch,
        compiler_params=pltpu.CompilerParams(collective_id=0, has_side_effects=True),
        cost_estimate=pl.CostEstimate(
            flops=0, transcendentals=0, bytes_accessed=64 * packed.size * 4
        ),
    )(packed)


def pack_halves(parts, blocks):
    halves = []
    for h in range(2):
        pieces = []
        for p in parts[:2]:
            rows = p.shape[0] // 2
            pieces.append(p[h * rows : (h + 1) * rows].reshape(-1))
        for p in parts[2:]:
            cols = p.shape[1] // 2
            pieces.append(p[:, h * cols : (h + 1) * cols].reshape(-1))
        halves.append(jnp.concatenate(pieces))
    real = halves[0].shape[0]
    tiles = -(-real // (TILE * blocks)) * blocks
    flat = jnp.stack(halves)
    flat = jnp.pad(flat, ((0, 0), (0, tiles * TILE - real)))
    return flat.reshape(2 * tiles, 8, 128), real


def unpack_half(reduced, parts):
    flat = reduced.reshape(-1)
    out, offset = [], 0
    for p in parts[:2]:
        shape = (p.shape[0] // 2, p.shape[1])
        out.append(flat[offset : offset + shape[0] * shape[1]].reshape(shape))
        offset += shape[0] * shape[1]
    for p in parts[2:]:
        shape = (p.shape[0], p.shape[1] // 2)
        out.append(flat[offset : offset + shape[0] * shape[1]].reshape(shape))
        offset += shape[0] * shape[1]
    return out


def shards(density, cotangent, pw_one, pw_two, dw_one, dw_two):
    channels, extent_x, extent_y, extent_z = density.shape
    assert lax.axis_size("own") == 2
    weight_one, weight_two, taps_one, taps_two = gather_weights(pw_one, pw_two, dw_one, dw_two)
    rim_width = 1
    wide_input = extended(density, (("own", 1), ("space", 2)), rim_width)
    first = depthwise(wide_input, taps_one, extent_x, extent_y, 1).astype(jnp.bfloat16)
    pre = pointwise(weight_one, first)
    act = jax.nn.silu(pre).astype(jnp.bfloat16)
    act_padded = extended(act, (("own", 1), ("space", 2)), 1)
    second = depthwise(act_padded, taps_two, extent_x, extent_y, 1).astype(jnp.bfloat16)
    grad_second = backmap(weight_two, cotangent).astype(jnp.bfloat16)
    second_padded = extended(grad_second, (("own", 1), ("space", 2)), 1)
    sigma = jax.nn.sigmoid(pre)
    grad_pre = (
        depthwise(second_padded, taps_two, extent_x, extent_y, -1)
        * (sigma * (1.0 + pre * (1.0 - sigma)))
    ).astype(jnp.bfloat16)
    grad_first = backmap(weight_one, grad_pre).astype(jnp.bfloat16)
    first_padded = extended_at_once(grad_first)
    grad_input = (
        cotangent.astype(jnp.float32) + depthwise(first_padded, taps_one, extent_x, extent_y, -1)
    ).astype(jnp.bfloat16)
    total_cells = extent_x * extent_y * extent_z * lax.axis_size("own") * lax.axis_size("space")
    grad_scale = 1.0 / math.sqrt(float(total_cells))
    local_pw_one = contract_cells(first, grad_pre) * grad_scale
    local_pw_two = contract_cells(second, cotangent) * grad_scale
    local_dw_one = tap_sums(wide_input, grad_first) * grad_scale
    local_dw_two = tap_sums(act_padded, grad_second) * grad_scale
    partials = (local_pw_one, local_pw_two, local_dw_one, local_dw_two)
    scatter, _ = reduce_plan(lax.axis_size("space"))
    blocks = math.prod(f[2] for group in scatter for f in group if f[0] != "own")
    packed, _ = pack_halves(partials, blocks)
    result = unpack_half(tree_reduce(packed), partials)
    return (grad_input, result[0], result[1], result[2], result[3])


def solution(mesh):
    in_specs = (
        P(None, "own", "space", None),
        P(None, "own", "space", None),
        P("own", None),
        P("own", None),
        P(None, "own"),
        P(None, "own"),
    )
    out_specs = (
        P(None, "own", "space", None),
        P("own", None),
        P("own", None),
        P(None, "own"),
        P(None, "own"),
    )
    return jax.shard_map(shards, mesh=mesh, in_specs=in_specs, out_specs=out_specs, check_vma=False)
```

```python
import functools
import math

import jax
import jax.numpy as jnp
from jax import lax
from jax.experimental import pallas as pl
from jax.experimental.pallas import tpu as pltpu
from jax.sharding import PartitionSpec as P

MESH = pl.DeviceIdType.MESH
TILE = 8 * 128

TAP_LIST = [
    (9 * (a + 1) + 3 * (b + 1) + (d + 1), a, b, d)
    for a in (-1, 0, 1)
    for b in (-1, 0, 1)
    for d in (-1, 0, 1)
]


def extended(value, sides, width):
    for axis, dim in sides:
        size, length = (lax.axis_size(axis), value.shape[dim])
        up = [(i, (i + 1) % size) for i in range(size)]
        down = [(j, i) for i, j in up]
        last = lax.slice_in_dim(value, length - width, length, axis=dim)
        first = lax.slice_in_dim(value, 0, width, axis=dim)
        if size == 2:
            theirs = lax.ppermute(jnp.concatenate([first, last], axis=dim), axis, up)
            after = lax.slice_in_dim(theirs, 0, width, axis=dim)
            before = lax.slice_in_dim(theirs, width, 2 * width, axis=dim)
        else:
            before = lax.ppermute(last, axis, up)
            after = lax.ppermute(first, axis, down)
        value = jnp.concatenate([before, value, after], axis=dim)
    return value


def gather_weights(pw_one, pw_two, dw_one, dw_two):
    mine = jnp.concatenate([pw_one.reshape(-1), pw_two.reshape(-1), dw_one.reshape(-1), dw_two.reshape(-1)])
    theirs = lax.ppermute(mine, "own", [(0, 1), (1, 0)])
    first_half = lax.axis_index("own") == 0
    low = jnp.where(first_half, mine, theirs)
    high = jnp.where(first_half, theirs, mine)
    out, offset = [], 0
    for w, dim in ((pw_one, 0), (pw_two, 0), (dw_one, 1), (dw_two, 1)):
        count = w.size
        parts = [h[offset : offset + count].reshape(w.shape) for h in (low, high)]
        out.append(jnp.concatenate(parts, axis=dim))
        offset += count
    return out


def ring_z(padded):
    return jnp.concatenate([padded[..., -1:], padded, padded[..., :1]], axis=3)


def depthwise(padded, weights, extent_x, extent_y, direction):
    extent_z = padded.shape[3]
    wide = ring_z(padded)
    running = jnp.zeros((padded.shape[0], extent_x, extent_y, extent_z), jnp.float32)
    for k, a, b, d in TAP_LIST:
        start_x = 1 + direction * a
        start_y = 1 + direction * b
        start_z = 1 + direction * d
        shifted = wide[:, start_x : start_x + extent_x, start_y : start_y + extent_y, start_z : start_z + extent_z]
        running = running + weights[k].astype(jnp.float32)[:, None, None, None] * shifted.astype(jnp.float32)
    return running


def tap_sums(padded, gradient):
    extent_x, extent_y, extent_z = gradient.shape[1:]
    wide = ring_z(padded)
    grad_float = gradient.astype(jnp.float32)
    columns = []
    for k, a, b, d in TAP_LIST:
        shifted = wide[:, 1 + a : 1 + a + extent_x, 1 + b : 1 + b + extent_y, 1 + d : 1 + d + extent_z]
        columns.append(jnp.sum(shifted.astype(jnp.float32) * grad_float, axis=(1, 2, 3)))
    return jnp.stack(columns, axis=0)


def pointwise(weights, source):
    layout = source.shape
    flattened = source.reshape(layout[0], -1)
    return jnp.dot(weights.T, flattened, preferred_element_type=jnp.float32).reshape(layout)


def backmap(weights, source):
    layout = source.shape
    flattened = source.reshape(layout[0], -1)
    return jnp.dot(weights, flattened, preferred_element_type=jnp.float32).reshape(layout)


def contract_cells(left, right):
    channels = left.shape[0]
    return lax.dot_general(
        left.reshape(channels, -1),
        right.reshape(channels, -1),
        (((1,), (1,)), ((), ())),
        preferred_element_type=jnp.float32,
    )


def reduce_plan(space_size):
    if space_size == 128:
        scatter = ((("own", 0, 2), ("space", 1, 2)), (("space", 2, 2), ("space", 4, 4)))
        return scatter, (("space", 16, 8),)
    factors, stride, rest = [], 1, space_size
    while rest > 2:
        factors.append(("space", stride, 2))
        stride, rest = stride * 2, rest // 2
    scatter = ((("own", 0, 2),) + tuple(factors[:1]),) + tuple((f,) for f in factors[1:])
    return scatter, (("space", stride, rest),)


def group_size(group):
    return math.prod(f[2] for f in group)


def reduce_kernel(plan, x_ref, o_ref, *refs):
    scatter, last = plan
    count = len(scatter)
    bufs = refs[:count]
    recvs = refs[count : 2 * count]
    recv_last, res, send_sem, recv_sem = refs[2 * count :]
    own = lax.axis_index("own")
    space = lax.axis_index("space")

    def coord(factor):
        axis, stride, size = factor
        return own if axis == "own" else (space // stride) % size

    def member(group):
        index = 0
        for factor in group:
            index = index * factor[2] + coord(factor)
        return index

    def device(group, target):
        new_own, new_space = own, space
        for factor in reversed(group):
            axis, stride, size = factor
            value = target % size
            target = target // size
            if axis == "own":
                new_own = value
            else:
                new_space = new_space + (value - coord(factor)) * stride
        return (new_own, new_space)

    barrier = pltpu.get_barrier_semaphore()
    partners = 0
    for group in scatter + (last,):
        size, me = group_size(group), member(group)
        for d in range(1, size):
            pl.semaphore_signal(
                barrier, 1, device_id=device(group, (me + d) % size), device_id_type=MESH
            )
            partners += 1
    pl.semaphore_wait(barrier, partners)

    def exchange(group, base, source_of, dest_of):
        size, me = group_size(group), member(group)
        sends = []
        for d in range(1, size):
            target = (me + d) % size
            copy = pltpu.make_async_remote_copy(
                src_ref=source_of(target),
                dst_ref=dest_of(me),
                send_sem=send_sem.at[base + target],
                recv_sem=recv_sem.at[base + me],
                device_id=device(group, target),
                device_id_type=MESH,
            )
            copy.start()
            sends.append(copy)
        return sends

    def finish(group, base, source_of, dest_of, sends):
        size, me = group_size(group), member(group)
        for d in range(1, size):
            sender = (me + d) % size
            pltpu.make_async_remote_copy(
                src_ref=source_of(sender),
                dst_ref=dest_of(sender),
                send_sem=send_sem.at[base + sender],
                recv_sem=recv_sem.at[base + sender],
                device_id=device(group, sender),
                device_id_type=MESH,
            ).wait_recv()
        for copy in sends:
            copy.wait_send()

    base = 0
    source = x_ref
    for i, group in enumerate(scatter):
        size, me = group_size(group), member(group)
        piece = source.shape[0] // size
        src_of = lambda t, s=source, n=piece: s.at[pl.ds(t * n, n)]
        dst_of = lambda t, r=recvs[i]: r.at[t]
        sends = exchange(group, base, src_of, dst_of)
        finish(group, base, src_of, dst_of, sends)
        total = source[pl.ds(me * piece, piece)]
        for d in range(1, size):
            total = total + recvs[i][(me + d) % size]
        bufs[i][...] = total
        source = bufs[i]
        base += size

    size, me = group_size(last), member(last)
    piece = source.shape[0]
    src_of = lambda t, s=source: s
    dst_of = lambda t: recv_last.at[t]
    sends = exchange(last, base, src_of, dst_of)
    recv_last[me] = source[...]
    finish(last, base, src_of, dst_of, sends)
    total = recv_last[0]
    for k in range(1, size):
        total = total + recv_last[k]
    space_factors = [f for group in scatter for f in group if f[0] != "own"]
    block = 0
    for factor in space_factors:
        block = block * factor[2] + coord(factor)
    res[pl.ds(block * piece, piece)] = total
    base += size

    span = piece
    gathers = [tuple(f for group in scatter for f in group if f[0] != "own")]
    for j in range(len(gathers) - 1, -1, -1):
        group = gathers[j]
        if not group:
            continue
        size, me = group_size(group), member(group)
        prefix = 0
        for earlier in gathers[:j]:
            prefix = prefix * group_size(earlier) + member(earlier)
        start = prefix * size * span
        src_of = lambda t, a=start, n=span: res.at[pl.ds(a + t * n, n)]
        sends = []
        for d in range(1, size):
            target = (me + d) % size
            copy = pltpu.make_async_remote_copy(
                src_ref=src_of(me),
                dst_ref=src_of(me),
                send_sem=send_sem.at[base + target],
                recv_sem=recv_sem.at[base + me],
                device_id=device(group, target),
                device_id_type=MESH,
            )
            copy.start()
            sends.append(copy)
        finish(group, base, src_of, src_of, sends)
        span *= size
        base += size
    o_ref[...] = res[...]


def tree_reduce(packed):
    plan = reduce_plan(lax.axis_size("space"))
    scatter, last = plan
    half = packed.shape[0] // 2
    shapes, length = [], packed.shape[0]
    for group in scatter:
        length //= group_size(group)
        shapes.append((group_size(group), length))
    semaphores = sum(group_size(group) for group in scatter) + group_size(last) + math.prod(
        f[2] for group in scatter for f in group if f[0] != "own"
    )
    scratch = [pltpu.VMEM((n, 8, 128), jnp.float32) for _, n in shapes]
    scratch += [pltpu.VMEM((size, n, 8, 128), jnp.float32) for size, n in shapes]
    scratch += [
        pltpu.VMEM((group_size(last), length, 8, 128), jnp.float32),
        pltpu.VMEM((half, 8, 128), jnp.float32),
        pltpu.SemaphoreType.DMA((semaphores,)),
        pltpu.SemaphoreType.DMA((semaphores,)),
    ]
    return pl.pallas_call(
        functools.partial(reduce_kernel, plan),
        out_shape=jax.ShapeDtypeStruct((half, 8, 128), jnp.float32),
        in_specs=[pl.BlockSpec(memory_space=pltpu.VMEM)],
        out_specs=pl.BlockSpec(memory_space=pltpu.VMEM),
        scratch_shapes=scratch,
        compiler_params=pltpu.CompilerParams(collective_id=0, has_side_effects=True),
        cost_estimate=pl.CostEstimate(
            flops=0, transcendentals=0, bytes_accessed=64 * packed.size * 4
        ),
    )(packed)


def pack_halves(parts, blocks):
    halves = []
    for h in range(2):
        pieces = []
        for p in parts[:2]:
            rows = p.shape[0] // 2
            pieces.append(p[h * rows : (h + 1) * rows].reshape(-1))
        for p in parts[2:]:
            cols = p.shape[1] // 2
            pieces.append(p[:, h * cols : (h + 1) * cols].reshape(-1))
        halves.append(jnp.concatenate(pieces))
    real = halves[0].shape[0]
    tiles = -(-real // (TILE * blocks)) * blocks
    flat = jnp.stack(halves)
    flat = jnp.pad(flat, ((0, 0), (0, tiles * TILE - real)))
    return flat.reshape(2 * tiles, 8, 128), real


def unpack_half(reduced, parts):
    flat = reduced.reshape(-1)
    out, offset = [], 0
    for p in parts[:2]:
        shape = (p.shape[0] // 2, p.shape[1])
        out.append(flat[offset : offset + shape[0] * shape[1]].reshape(shape))
        offset += shape[0] * shape[1]
    for p in parts[2:]:
        shape = (p.shape[0], p.shape[1] // 2)
        out.append(flat[offset : offset + shape[0] * shape[1]].reshape(shape))
        offset += shape[0] * shape[1]
    return out


def shards(density, cotangent, pw_one, pw_two, dw_one, dw_two):
    channels, extent_x, extent_y, extent_z = density.shape
    assert lax.axis_size("own") == 2
    weight_one, weight_two, taps_one, taps_two = gather_weights(pw_one, pw_two, dw_one, dw_two)
    rim_width = 1
    wide_input = extended(density, (("own", 1), ("space", 2)), rim_width)
    first = depthwise(wide_input, taps_one, extent_x, extent_y, 1).astype(jnp.bfloat16)
    pre = pointwise(weight_one, first)
    act = jax.nn.silu(pre).astype(jnp.bfloat16)
    act_padded = extended(act, (("own", 1), ("space", 2)), 1)
    second = depthwise(act_padded, taps_two, extent_x, extent_y, 1).astype(jnp.bfloat16)
    grad_second = backmap(weight_two, cotangent).astype(jnp.bfloat16)
    second_padded = extended(grad_second, (("own", 1), ("space", 2)), 1)
    sigma = jax.nn.sigmoid(pre)
    grad_pre = (
        depthwise(second_padded, taps_two, extent_x, extent_y, -1)
        * (sigma * (1.0 + pre * (1.0 - sigma)))
    ).astype(jnp.bfloat16)
    grad_first = backmap(weight_one, grad_pre).astype(jnp.bfloat16)
    first_padded = extended(grad_first, (("own", 1), ("space", 2)), 1)
    grad_input = (
        cotangent.astype(jnp.float32) + depthwise(first_padded, taps_one, extent_x, extent_y, -1)
    ).astype(jnp.bfloat16)
    total_cells = extent_x * extent_y * extent_z * lax.axis_size("own") * lax.axis_size("space")
    grad_scale = 1.0 / math.sqrt(float(total_cells))
    local_pw_one = contract_cells(first, grad_pre) * grad_scale
    local_pw_two = contract_cells(second, cotangent) * grad_scale
    local_dw_one = tap_sums(wide_input, grad_first) * grad_scale
    local_dw_two = tap_sums(act_padded, grad_second) * grad_scale
    partials = (local_pw_one, local_pw_two, local_dw_one, local_dw_two)
    scatter, _ = reduce_plan(lax.axis_size("space"))
    blocks = math.prod(f[2] for group in scatter for f in group if f[0] != "own")
    packed, _ = pack_halves(partials, blocks)
    result = unpack_half(tree_reduce(packed), partials)
    return (grad_input, result[0], result[1], result[2], result[3])


def solution(mesh):
    in_specs = (
        P(None, "own", "space", None),
        P(None, "own", "space", None),
        P("own", None),
        P("own", None),
        P(None, "own"),
        P(None, "own"),
    )
    out_specs = (
        P(None, "own", "space", None),
        P("own", None),
        P("own", None),
        P(None, "own"),
        P(None, "own"),
    )
    return jax.shard_map(shards, mesh=mesh, in_specs=in_specs, out_specs=out_specs, check_vma=False)
```

```python
import functools
import math

import jax
import jax.numpy as jnp
from jax import lax
from jax.experimental import pallas as pl
from jax.experimental.pallas import tpu as pltpu
from jax.sharding import PartitionSpec as P

MESH = pl.DeviceIdType.MESH
TILE = 8 * 128

TAP_LIST = [
    (9 * (a + 1) + 3 * (b + 1) + (d + 1), a, b, d)
    for a in (-1, 0, 1)
    for b in (-1, 0, 1)
    for d in (-1, 0, 1)
]


def extended(value, sides, width):
    for axis, dim in sides:
        size, length = (lax.axis_size(axis), value.shape[dim])
        up = [(i, (i + 1) % size) for i in range(size)]
        down = [(j, i) for i, j in up]
        last = lax.slice_in_dim(value, length - width, length, axis=dim)
        first = lax.slice_in_dim(value, 0, width, axis=dim)
        if size == 2:
            theirs = lax.ppermute(jnp.concatenate([first, last], axis=dim), axis, up)
            after = lax.slice_in_dim(theirs, 0, width, axis=dim)
            before = lax.slice_in_dim(theirs, width, 2 * width, axis=dim)
        else:
            before = lax.ppermute(last, axis, up)
            after = lax.ppermute(first, axis, down)
        value = jnp.concatenate([before, value, after], axis=dim)
    return value


def gather_weights(pw_one, pw_two, dw_one, dw_two):
    mine = jnp.concatenate([pw_one.reshape(-1), pw_two.reshape(-1), dw_one.reshape(-1), dw_two.reshape(-1)])
    theirs = lax.ppermute(mine, "own", [(0, 1), (1, 0)])
    first_half = lax.axis_index("own") == 0
    low = jnp.where(first_half, mine, theirs)
    high = jnp.where(first_half, theirs, mine)
    out, offset = [], 0
    for w, dim in ((pw_one, 0), (pw_two, 0), (dw_one, 1), (dw_two, 1)):
        count = w.size
        parts = [h[offset : offset + count].reshape(w.shape) for h in (low, high)]
        out.append(jnp.concatenate(parts, axis=dim))
        offset += count
    return out


def ring_z(padded):
    return jnp.concatenate([padded[..., -1:], padded, padded[..., :1]], axis=3)


def depthwise(padded, weights, extent_x, extent_y, direction):
    extent_z = padded.shape[3]
    wide = ring_z(padded)
    running = jnp.zeros((padded.shape[0], extent_x, extent_y, extent_z), jnp.float32)
    for k, a, b, d in TAP_LIST:
        start_x = 1 + direction * a
        start_y = 1 + direction * b
        start_z = 1 + direction * d
        shifted = wide[:, start_x : start_x + extent_x, start_y : start_y + extent_y, start_z : start_z + extent_z]
        running = running + weights[k].astype(jnp.float32)[:, None, None, None] * shifted.astype(jnp.float32)
    return running


def tap_sums(padded, gradient):
    extent_x, extent_y, extent_z = gradient.shape[1:]
    wide = ring_z(padded)
    grad_float = gradient.astype(jnp.float32)
    columns = []
    for k, a, b, d in TAP_LIST:
        shifted = wide[:, 1 + a : 1 + a + extent_x, 1 + b : 1 + b + extent_y, 1 + d : 1 + d + extent_z]
        columns.append(jnp.sum(shifted.astype(jnp.float32) * grad_float, axis=(1, 2, 3)))
    return columns


def pointwise(weights, source):
    layout = source.shape
    flattened = source.reshape(layout[0], -1)
    return jnp.dot(weights.T, flattened, preferred_element_type=jnp.float32).reshape(layout)


def backmap(weights, source):
    layout = source.shape
    flattened = source.reshape(layout[0], -1)
    return jnp.dot(weights, flattened, preferred_element_type=jnp.float32).reshape(layout)


def contract_cells(left, right):
    channels = left.shape[0]
    return lax.dot_general(
        left.reshape(channels, -1),
        right.reshape(channels, -1),
        (((1,), (1,)), ((), ())),
        preferred_element_type=jnp.float32,
    )


def reduce_plan(space_size):
    if space_size == 128:
        scatter = ((("own", 0, 2), ("space", 1, 2)), (("space", 2, 2), ("space", 4, 4)))
        return scatter, (("space", 16, 8),)
    factors, stride, rest = [], 1, space_size
    while rest > 2:
        factors.append(("space", stride, 2))
        stride, rest = stride * 2, rest // 2
    scatter = ((("own", 0, 2),) + tuple(factors[:1]),) + tuple((f,) for f in factors[1:])
    return scatter, (("space", stride, rest),)


def group_size(group):
    return math.prod(f[2] for f in group)


def reduce_kernel(plan, x_ref, o_ref, *refs):
    scatter, last = plan
    count = len(scatter)
    bufs = refs[:count]
    recvs = refs[count : 2 * count]
    recv_last, res, send_sem, recv_sem = refs[2 * count :]
    own = lax.axis_index("own")
    space = lax.axis_index("space")

    def coord(factor):
        axis, stride, size = factor
        return own if axis == "own" else (space // stride) % size

    def member(group):
        index = 0
        for factor in group:
            index = index * factor[2] + coord(factor)
        return index

    def device(group, target):
        new_own, new_space = own, space
        for factor in reversed(group):
            axis, stride, size = factor
            value = target % size
            target = target // size
            if axis == "own":
                new_own = value
            else:
                new_space = new_space + (value - coord(factor)) * stride
        return (new_own, new_space)

    barrier = pltpu.get_barrier_semaphore()
    partners = 0
    for group in scatter + (last,):
        size, me = group_size(group), member(group)
        for d in range(1, size):
            pl.semaphore_signal(
                barrier, 1, device_id=device(group, (me + d) % size), device_id_type=MESH
            )
            partners += 1
    pl.semaphore_wait(barrier, partners)

    def exchange(group, base, source_of, dest_of):
        size, me = group_size(group), member(group)
        sends = []
        for d in range(1, size):
            target = (me + d) % size
            copy = pltpu.make_async_remote_copy(
                src_ref=source_of(target),
                dst_ref=dest_of(me),
                send_sem=send_sem.at[base + target],
                recv_sem=recv_sem.at[base + me],
                device_id=device(group, target),
                device_id_type=MESH,
            )
            copy.start()
            sends.append(copy)
        return sends

    def finish(group, base, source_of, dest_of, sends):
        size, me = group_size(group), member(group)
        for d in range(1, size):
            sender = (me + d) % size
            pltpu.make_async_remote_copy(
                src_ref=source_of(sender),
                dst_ref=dest_of(sender),
                send_sem=send_sem.at[base + sender],
                recv_sem=recv_sem.at[base + sender],
                device_id=device(group, sender),
                device_id_type=MESH,
            ).wait_recv()
        for copy in sends:
            copy.wait_send()

    base = 0
    source = x_ref
    for i, group in enumerate(scatter):
        size, me = group_size(group), member(group)
        piece = source.shape[0] // size
        src_of = lambda t, s=source, n=piece: s.at[pl.ds(t * n, n)]
        dst_of = lambda t, r=recvs[i]: r.at[t]
        sends = exchange(group, base, src_of, dst_of)
        finish(group, base, src_of, dst_of, sends)
        total = source[pl.ds(me * piece, piece)]
        for d in range(1, size):
            total = total + recvs[i][(me + d) % size]
        bufs[i][...] = total
        source = bufs[i]
        base += size

    size, me = group_size(last), member(last)
    piece = source.shape[0]
    src_of = lambda t, s=source: s
    dst_of = lambda t: recv_last.at[t]
    sends = exchange(last, base, src_of, dst_of)
    recv_last[me] = source[...]
    finish(last, base, src_of, dst_of, sends)
    total = recv_last[0]
    for k in range(1, size):
        total = total + recv_last[k]
    space_factors = [f for group in scatter for f in group if f[0] != "own"]
    block = 0
    for factor in space_factors:
        block = block * factor[2] + coord(factor)
    res[pl.ds(block * piece, piece)] = total
    base += size

    span = piece
    gathers = [tuple(f for group in scatter for f in group if f[0] != "own")]
    for j in range(len(gathers) - 1, -1, -1):
        group = gathers[j]
        if not group:
            continue
        size, me = group_size(group), member(group)
        prefix = 0
        for earlier in gathers[:j]:
            prefix = prefix * group_size(earlier) + member(earlier)
        start = prefix * size * span
        src_of = lambda t, a=start, n=span: res.at[pl.ds(a + t * n, n)]
        sends = []
        for d in range(1, size):
            target = (me + d) % size
            copy = pltpu.make_async_remote_copy(
                src_ref=src_of(me),
                dst_ref=src_of(me),
                send_sem=send_sem.at[base + target],
                recv_sem=recv_sem.at[base + me],
                device_id=device(group, target),
                device_id_type=MESH,
            )
            copy.start()
            sends.append(copy)
        finish(group, base, src_of, src_of, sends)
        span *= size
        base += size
    o_ref[...] = res[...]


def tree_reduce(packed):
    plan = reduce_plan(lax.axis_size("space"))
    scatter, last = plan
    half = packed.shape[0] // 2
    shapes, length = [], packed.shape[0]
    for group in scatter:
        length //= group_size(group)
        shapes.append((group_size(group), length))
    semaphores = sum(group_size(group) for group in scatter) + group_size(last) + math.prod(
        f[2] for group in scatter for f in group if f[0] != "own"
    )
    scratch = [pltpu.VMEM((n, 8, 128), jnp.float32) for _, n in shapes]
    scratch += [pltpu.VMEM((size, n, 8, 128), jnp.float32) for size, n in shapes]
    scratch += [
        pltpu.VMEM((group_size(last), length, 8, 128), jnp.float32),
        pltpu.VMEM((half, 8, 128), jnp.float32),
        pltpu.SemaphoreType.DMA((semaphores,)),
        pltpu.SemaphoreType.DMA((semaphores,)),
    ]
    return pl.pallas_call(
        functools.partial(reduce_kernel, plan),
        out_shape=jax.ShapeDtypeStruct((half, 8, 128), jnp.float32),
        in_specs=[pl.BlockSpec(memory_space=pltpu.VMEM)],
        out_specs=pl.BlockSpec(memory_space=pltpu.VMEM),
        scratch_shapes=scratch,
        compiler_params=pltpu.CompilerParams(collective_id=0, has_side_effects=True),
        cost_estimate=pl.CostEstimate(
            flops=0, transcendentals=0, bytes_accessed=64 * packed.size * 4
        ),
    )(packed)


def pack_halves(parts, blocks):
    halves = []
    for h in range(2):
        pieces = []
        for p in parts[:2]:
            rows = p.shape[0] // 2
            pieces.append(p[h * rows : (h + 1) * rows].reshape(-1))
        for columns in parts[2:]:
            cols = columns[0].shape[0] // 2
            pieces.extend(column[h * cols : (h + 1) * cols] for column in columns)
        halves.append(jnp.concatenate(pieces))
    real = halves[0].shape[0]
    tiles = -(-real // (TILE * blocks)) * blocks
    flat = jnp.stack(halves)
    flat = jnp.pad(flat, ((0, 0), (0, tiles * TILE - real)))
    return flat.reshape(2 * tiles, 8, 128), real


def unpack_half(reduced, parts):
    flat = reduced.reshape(-1)
    out, offset = [], 0
    for p in parts[:2]:
        shape = (p.shape[0] // 2, p.shape[1])
        out.append(flat[offset : offset + shape[0] * shape[1]].reshape(shape))
        offset += shape[0] * shape[1]
    for columns in parts[2:]:
        shape = (len(columns), columns[0].shape[0] // 2)
        out.append(flat[offset : offset + shape[0] * shape[1]].reshape(shape))
        offset += shape[0] * shape[1]
    return out


def shards(density, cotangent, pw_one, pw_two, dw_one, dw_two):
    channels, extent_x, extent_y, extent_z = density.shape
    assert lax.axis_size("own") == 2
    weight_one, weight_two, taps_one, taps_two = gather_weights(pw_one, pw_two, dw_one, dw_two)
    rim_width = 1
    wide_input = extended(density, (("own", 1), ("space", 2)), rim_width)
    first = depthwise(wide_input, taps_one, extent_x, extent_y, 1).astype(jnp.bfloat16)
    pre = pointwise(weight_one, first)
    act = jax.nn.silu(pre).astype(jnp.bfloat16)
    act_padded = extended(act, (("own", 1), ("space", 2)), 1)
    second = depthwise(act_padded, taps_two, extent_x, extent_y, 1).astype(jnp.bfloat16)
    grad_second = backmap(weight_two, cotangent).astype(jnp.bfloat16)
    second_padded = extended(grad_second, (("own", 1), ("space", 2)), 1)
    sigma = jax.nn.sigmoid(pre)
    grad_pre = (
        depthwise(second_padded, taps_two, extent_x, extent_y, -1)
        * (sigma * (1.0 + pre * (1.0 - sigma)))
    ).astype(jnp.bfloat16)
    grad_first = backmap(weight_one, grad_pre).astype(jnp.bfloat16)
    first_padded = extended(grad_first, (("own", 1), ("space", 2)), 1)
    grad_input = (
        cotangent.astype(jnp.float32) + depthwise(first_padded, taps_one, extent_x, extent_y, -1)
    ).astype(jnp.bfloat16)
    total_cells = extent_x * extent_y * extent_z * lax.axis_size("own") * lax.axis_size("space")
    grad_scale = 1.0 / math.sqrt(float(total_cells))
    local_pw_one = contract_cells(first, grad_pre) * grad_scale
    local_pw_two = contract_cells(second, cotangent) * grad_scale
    local_dw_one = [column * grad_scale for column in tap_sums(wide_input, grad_first)]
    local_dw_two = [column * grad_scale for column in tap_sums(act_padded, grad_second)]
    partials = (local_pw_one, local_pw_two, local_dw_one, local_dw_two)
    scatter, _ = reduce_plan(lax.axis_size("space"))
    blocks = math.prod(f[2] for group in scatter for f in group if f[0] != "own")
    packed, _ = pack_halves(partials, blocks)
    result = unpack_half(tree_reduce(packed), partials)
    return (grad_input, result[0], result[1], result[2], result[3])


def solution(mesh):
    in_specs = (
        P(None, "own", "space", None),
        P(None, "own", "space", None),
        P("own", None),
        P("own", None),
        P(None, "own"),
        P(None, "own"),
    )
    out_specs = (
        P(None, "own", "space", None),
        P("own", None),
        P("own", None),
        P(None, "own"),
        P(None, "own"),
    )
    return jax.shard_map(shards, mesh=mesh, in_specs=in_specs, out_specs=out_specs, check_vma=False)
```

```python
import functools
import math

import jax
import jax.numpy as jnp
from jax import lax
from jax.experimental import pallas as pl
from jax.experimental.pallas import tpu as pltpu
from jax.sharding import PartitionSpec as P

MESH = pl.DeviceIdType.MESH
TILE = 8 * 128

TAP_LIST = [
    (9 * (a + 1) + 3 * (b + 1) + (d + 1), a, b, d)
    for a in (-1, 0, 1)
    for b in (-1, 0, 1)
    for d in (-1, 0, 1)
]


def extended(value, sides, width):
    for axis, dim in sides:
        size, length = (lax.axis_size(axis), value.shape[dim])
        up = [(i, (i + 1) % size) for i in range(size)]
        down = [(j, i) for i, j in up]
        last = lax.slice_in_dim(value, length - width, length, axis=dim)
        first = lax.slice_in_dim(value, 0, width, axis=dim)
        if size == 2:
            theirs = lax.ppermute(jnp.concatenate([first, last], axis=dim), axis, up)
            after = lax.slice_in_dim(theirs, 0, width, axis=dim)
            before = lax.slice_in_dim(theirs, width, 2 * width, axis=dim)
        else:
            before = lax.ppermute(last, axis, up)
            after = lax.ppermute(first, axis, down)
        value = jnp.concatenate([before, value, after], axis=dim)
    return value


def gather_weights(pw_one, pw_two, dw_one, dw_two):
    mine = jnp.concatenate([pw_one.reshape(-1), pw_two.reshape(-1), dw_one.reshape(-1), dw_two.reshape(-1)])
    theirs = lax.ppermute(mine, "own", [(0, 1), (1, 0)])
    first_half = lax.axis_index("own") == 0
    low = jnp.where(first_half, mine, theirs)
    high = jnp.where(first_half, theirs, mine)
    out, offset = [], 0
    for w, dim in ((pw_one, 0), (pw_two, 0), (dw_one, 1), (dw_two, 1)):
        count = w.size
        parts = [h[offset : offset + count].reshape(w.shape) for h in (low, high)]
        out.append(jnp.concatenate(parts, axis=dim))
        offset += count
    return out


def ring_z(padded):
    return jnp.concatenate([padded[..., -1:], padded, padded[..., :1]], axis=3)


def depthwise(padded, weights, extent_x, extent_y, direction):
    extent_z = padded.shape[3]
    wide = ring_z(padded)
    running = jnp.zeros((padded.shape[0], extent_x, extent_y, extent_z), jnp.float32)
    for k, a, b, d in TAP_LIST:
        start_x = 1 + direction * a
        start_y = 1 + direction * b
        start_z = 1 + direction * d
        shifted = wide[:, start_x : start_x + extent_x, start_y : start_y + extent_y, start_z : start_z + extent_z]
        running = running + weights[k].astype(jnp.float32)[:, None, None, None] * shifted.astype(jnp.float32)
    return running


def tap_sums(padded, gradient):
    extent_x, extent_y, extent_z = gradient.shape[1:]
    wide = ring_z(padded)
    grad_float = gradient.astype(jnp.float32)
    columns = []
    for k, a, b, d in TAP_LIST:
        shifted = wide[:, 1 + a : 1 + a + extent_x, 1 + b : 1 + b + extent_y, 1 + d : 1 + d + extent_z]
        columns.append(jnp.sum(shifted.astype(jnp.float32) * grad_float, axis=(1, 2, 3)))
    return columns


def pointwise(weights, source):
    layout = source.shape
    flattened = source.reshape(layout[0], -1)
    return jnp.dot(weights.T, flattened, preferred_element_type=jnp.float32).reshape(layout)


def backmap(weights, source):
    layout = source.shape
    flattened = source.reshape(layout[0], -1)
    return jnp.dot(weights, flattened, preferred_element_type=jnp.float32).reshape(layout)


def contract_cells(left, right):
    channels = left.shape[0]
    return lax.dot_general(
        left.reshape(channels, -1),
        right.reshape(channels, -1),
        (((1,), (1,)), ((), ())),
        preferred_element_type=jnp.float32,
    )


def reduce_plan(space_size):
    if space_size == 128:
        scatter = ((("own", 0, 2), ("space", 1, 2)), (("space", 2, 2), ("space", 4, 4)))
        return scatter, (("space", 16, 8),)
    factors, stride, rest = [], 1, space_size
    while rest > 2:
        factors.append(("space", stride, 2))
        stride, rest = stride * 2, rest // 2
    scatter = ((("own", 0, 2),) + tuple(factors[:1]),) + tuple((f,) for f in factors[1:])
    return scatter, (("space", stride, rest),)


def group_size(group):
    return math.prod(f[2] for f in group)


def reduce_kernel(plan, x_ref, o_ref, *refs):
    scatter, last = plan
    count = len(scatter)
    bufs = refs[:count]
    recvs = refs[count : 2 * count]
    recv_last, res, send_sem, recv_sem = refs[2 * count :]
    own = lax.axis_index("own")
    space = lax.axis_index("space")

    def coord(factor):
        axis, stride, size = factor
        return own if axis == "own" else (space // stride) % size

    def member(group):
        index = 0
        for factor in group:
            index = index * factor[2] + coord(factor)
        return index

    def device(group, target):
        new_own, new_space = own, space
        for factor in reversed(group):
            axis, stride, size = factor
            value = target % size
            target = target // size
            if axis == "own":
                new_own = value
            else:
                new_space = new_space + (value - coord(factor)) * stride
        return (new_own, new_space)

    barrier = pltpu.get_barrier_semaphore()
    partners = 0
    for group in scatter + (last,):
        size, me = group_size(group), member(group)
        for d in range(1, size):
            pl.semaphore_signal(
                barrier, 1, device_id=device(group, (me + d) % size), device_id_type=MESH
            )
            partners += 1
    pl.semaphore_wait(barrier, partners)

    def exchange(group, base, source_of, dest_of):
        size, me = group_size(group), member(group)
        sends = []
        for d in range(1, size):
            target = (me + d) % size
            copy = pltpu.make_async_remote_copy(
                src_ref=source_of(target),
                dst_ref=dest_of(me),
                send_sem=send_sem.at[base + target],
                recv_sem=recv_sem.at[base + me],
                device_id=device(group, target),
                device_id_type=MESH,
            )
            copy.start()
            sends.append(copy)
        return sends

    def finish(group, base, source_of, dest_of, sends):
        size, me = group_size(group), member(group)
        for d in range(1, size):
            sender = (me + d) % size
            pltpu.make_async_remote_copy(
                src_ref=source_of(sender),
                dst_ref=dest_of(sender),
                send_sem=send_sem.at[base + sender],
                recv_sem=recv_sem.at[base + sender],
                device_id=device(group, sender),
                device_id_type=MESH,
            ).wait_recv()
        for copy in sends:
            copy.wait_send()

    base = 0
    source = x_ref
    for i, group in enumerate(scatter):
        size, me = group_size(group), member(group)
        piece = source.shape[0] // size
        src_of = lambda t, s=source, n=piece: s.at[pl.ds(t * n, n)]
        dst_of = lambda t, r=recvs[i]: r.at[t]
        sends = exchange(group, base, src_of, dst_of)
        finish(group, base, src_of, dst_of, sends)
        total = source[pl.ds(me * piece, piece)]
        for d in range(1, size):
            total = total + recvs[i][(me + d) % size]
        bufs[i][...] = total
        source = bufs[i]
        base += size

    size, me = group_size(last), member(last)
    piece = source.shape[0]
    src_of = lambda t, s=source: s
    dst_of = lambda t: recv_last.at[t]
    sends = exchange(last, base, src_of, dst_of)
    recv_last[me] = source[...]
    finish(last, base, src_of, dst_of, sends)
    total = recv_last[0]
    for k in range(1, size):
        total = total + recv_last[k]
    space_factors = [f for group in scatter for f in group if f[0] != "own"]
    block = 0
    for factor in space_factors:
        block = block * factor[2] + coord(factor)
    res[pl.ds(block * piece, piece)] = total
    base += size

    span = piece
    gathers = [tuple(f for group in scatter for f in group if f[0] != "own")]
    for j in range(len(gathers) - 1, -1, -1):
        group = gathers[j]
        if not group:
            continue
        size, me = group_size(group), member(group)
        prefix = 0
        for earlier in gathers[:j]:
            prefix = prefix * group_size(earlier) + member(earlier)
        start = prefix * size * span
        src_of = lambda t, a=start, n=span: res.at[pl.ds(a + t * n, n)]
        sends = []
        for d in range(1, size):
            target = (me + d) % size
            copy = pltpu.make_async_remote_copy(
                src_ref=src_of(me),
                dst_ref=src_of(me),
                send_sem=send_sem.at[base + target],
                recv_sem=recv_sem.at[base + me],
                device_id=device(group, target),
                device_id_type=MESH,
            )
            copy.start()
            sends.append(copy)
        finish(group, base, src_of, src_of, sends)
        span *= size
        base += size
    o_ref[...] = res[...]


def tree_reduce(packed):
    plan = reduce_plan(lax.axis_size("space"))
    scatter, last = plan
    half = packed.shape[0] // 2
    shapes, length = [], packed.shape[0]
    for group in scatter:
        length //= group_size(group)
        shapes.append((group_size(group), length))
    semaphores = sum(group_size(group) for group in scatter) + group_size(last) + math.prod(
        f[2] for group in scatter for f in group if f[0] != "own"
    )
    scratch = [pltpu.VMEM((n, 8, 128), jnp.float32) for _, n in shapes]
    scratch += [pltpu.VMEM((size, n, 8, 128), jnp.float32) for size, n in shapes]
    scratch += [
        pltpu.VMEM((group_size(last), length, 8, 128), jnp.float32),
        pltpu.VMEM((half, 8, 128), jnp.float32),
        pltpu.SemaphoreType.DMA((semaphores,)),
        pltpu.SemaphoreType.DMA((semaphores,)),
    ]
    return pl.pallas_call(
        functools.partial(reduce_kernel, plan),
        out_shape=jax.ShapeDtypeStruct((half, 8, 128), jnp.float32),
        in_specs=[pl.BlockSpec(memory_space=pltpu.VMEM)],
        out_specs=pl.BlockSpec(memory_space=pltpu.VMEM),
        scratch_shapes=scratch,
        compiler_params=pltpu.CompilerParams(collective_id=0, has_side_effects=True),
        cost_estimate=pl.CostEstimate(
            flops=0, transcendentals=0, bytes_accessed=64 * packed.size * 4
        ),
    )(packed)


def tiled(block):
    rows, cols = block.shape
    return block.reshape(rows // 8, 8, cols // 128, 128).transpose(0, 2, 1, 3).reshape(-1, 8, 128)


def untiled(tiles, rows, cols):
    return tiles.reshape(rows // 8, cols // 128, 8, 128).transpose(0, 2, 1, 3).reshape(rows, cols)


def pack_halves(parts, blocks):
    halves = []
    for h in range(2):
        tiles = []
        for p in parts[:2]:
            rows = p.shape[0] // 2
            tiles.append(tiled(p[h * rows : (h + 1) * rows]))
        tail = []
        for columns in parts[2:]:
            cols = columns[0].shape[0] // 2
            tail.extend(column[h * cols : (h + 1) * cols] for column in columns)
        tail = jnp.concatenate(tail)
        head = sum(t.shape[0] for t in tiles)
        total = -(-(head + -(-tail.shape[0] // TILE)) // blocks) * blocks
        tail = jnp.pad(tail, (0, (total - head) * TILE - tail.shape[0]))
        halves.append(jnp.concatenate(tiles + [tail.reshape(-1, 8, 128)]))
    return jnp.concatenate(halves), None


def unpack_half(reduced, parts):
    out, offset = [], 0
    for p in parts[:2]:
        rows, cols = p.shape[0] // 2, p.shape[1]
        count = rows * cols // TILE
        out.append(untiled(reduced[offset : offset + count], rows, cols))
        offset += count
    flat = reduced[offset:].reshape(-1)
    offset = 0
    for columns in parts[2:]:
        shape = (len(columns), columns[0].shape[0] // 2)
        out.append(flat[offset : offset + shape[0] * shape[1]].reshape(shape))
        offset += shape[0] * shape[1]
    return out


def shards(density, cotangent, pw_one, pw_two, dw_one, dw_two):
    channels, extent_x, extent_y, extent_z = density.shape
    assert lax.axis_size("own") == 2
    weight_one, weight_two, taps_one, taps_two = gather_weights(pw_one, pw_two, dw_one, dw_two)
    rim_width = 1
    wide_input = extended(density, (("own", 1), ("space", 2)), rim_width)
    first = depthwise(wide_input, taps_one, extent_x, extent_y, 1).astype(jnp.bfloat16)
    pre = pointwise(weight_one, first)
    act = jax.nn.silu(pre).astype(jnp.bfloat16)
    act_padded = extended(act, (("own", 1), ("space", 2)), 1)
    second = depthwise(act_padded, taps_two, extent_x, extent_y, 1).astype(jnp.bfloat16)
    grad_second = backmap(weight_two, cotangent).astype(jnp.bfloat16)
    second_padded = extended(grad_second, (("own", 1), ("space", 2)), 1)
    sigma = jax.nn.sigmoid(pre)
    grad_pre = (
        depthwise(second_padded, taps_two, extent_x, extent_y, -1)
        * (sigma * (1.0 + pre * (1.0 - sigma)))
    ).astype(jnp.bfloat16)
    grad_first = backmap(weight_one, grad_pre).astype(jnp.bfloat16)
    first_padded = extended(grad_first, (("own", 1), ("space", 2)), 1)
    grad_input = (
        cotangent.astype(jnp.float32) + depthwise(first_padded, taps_one, extent_x, extent_y, -1)
    ).astype(jnp.bfloat16)
    total_cells = extent_x * extent_y * extent_z * lax.axis_size("own") * lax.axis_size("space")
    grad_scale = 1.0 / math.sqrt(float(total_cells))
    local_pw_one = contract_cells(first, grad_pre) * grad_scale
    local_pw_two = contract_cells(second, cotangent) * grad_scale
    local_dw_one = [column * grad_scale for column in tap_sums(wide_input, grad_first)]
    local_dw_two = [column * grad_scale for column in tap_sums(act_padded, grad_second)]
    partials = (local_pw_one, local_pw_two, local_dw_one, local_dw_two)
    scatter, _ = reduce_plan(lax.axis_size("space"))
    blocks = math.prod(f[2] for group in scatter for f in group if f[0] != "own")
    packed, _ = pack_halves(partials, blocks)
    result = unpack_half(tree_reduce(packed), partials)
    return (grad_input, result[0], result[1], result[2], result[3])


def solution(mesh):
    in_specs = (
        P(None, "own", "space", None),
        P(None, "own", "space", None),
        P("own", None),
        P("own", None),
        P(None, "own"),
        P(None, "own"),
    )
    out_specs = (
        P(None, "own", "space", None),
        P("own", None),
        P("own", None),
        P(None, "own"),
        P(None, "own"),
    )
    return jax.shard_map(shards, mesh=mesh, in_specs=in_specs, out_specs=out_specs, check_vma=False)
```

```python
import functools
import math

import jax
import jax.numpy as jnp
from jax import lax
from jax.experimental import pallas as pl
from jax.experimental.pallas import tpu as pltpu
from jax.sharding import PartitionSpec as P

MESH = pl.DeviceIdType.MESH
TILE = 8 * 128

TAP_LIST = [
    (9 * (a + 1) + 3 * (b + 1) + (d + 1), a, b, d)
    for a in (-1, 0, 1)
    for b in (-1, 0, 1)
    for d in (-1, 0, 1)
]


def extended(value, sides, width):
    for axis, dim in sides:
        size, length = (lax.axis_size(axis), value.shape[dim])
        up = [(i, (i + 1) % size) for i in range(size)]
        down = [(j, i) for i, j in up]
        last = lax.slice_in_dim(value, length - width, length, axis=dim)
        first = lax.slice_in_dim(value, 0, width, axis=dim)
        if size == 2:
            theirs = lax.ppermute(jnp.concatenate([first, last], axis=dim), axis, up)
            after = lax.slice_in_dim(theirs, 0, width, axis=dim)
            before = lax.slice_in_dim(theirs, width, 2 * width, axis=dim)
        else:
            before = lax.ppermute(last, axis, up)
            after = lax.ppermute(first, axis, down)
        value = jnp.concatenate([before, value, after], axis=dim)
    return value


def gather_weights(pw_one, pw_two, dw_one, dw_two):
    mine = jnp.concatenate([pw_one.reshape(-1), pw_two.reshape(-1), dw_one.reshape(-1), dw_two.reshape(-1)])
    theirs = lax.ppermute(mine, "own", [(0, 1), (1, 0)])
    first_half = lax.axis_index("own") == 0
    low = jnp.where(first_half, mine, theirs)
    high = jnp.where(first_half, theirs, mine)
    out, offset = [], 0
    for w, dim in ((pw_one, 0), (pw_two, 0), (dw_one, 1), (dw_two, 1)):
        count = w.size
        parts = [h[offset : offset + count].reshape(w.shape) for h in (low, high)]
        out.append(jnp.concatenate(parts, axis=dim))
        offset += count
    return out


def ring_z(padded):
    return jnp.concatenate([padded[..., -1:], padded, padded[..., :1]], axis=3)


def depthwise(padded, weights, extent_x, extent_y, direction):
    extent_z = padded.shape[3]
    wide = ring_z(padded)
    running = jnp.zeros((padded.shape[0], extent_x, extent_y, extent_z), jnp.float32)
    for k, a, b, d in TAP_LIST:
        start_x = 1 + direction * a
        start_y = 1 + direction * b
        start_z = 1 + direction * d
        shifted = wide[:, start_x : start_x + extent_x, start_y : start_y + extent_y, start_z : start_z + extent_z]
        running = running + weights[k].astype(jnp.float32)[:, None, None, None] * shifted.astype(jnp.float32)
    return running


def tap_sums(padded, gradient):
    extent_x, extent_y, extent_z = gradient.shape[1:]
    wide = ring_z(padded)
    grad_float = gradient.astype(jnp.float32)
    columns = []
    for k, a, b, d in TAP_LIST:
        shifted = wide[:, 1 + a : 1 + a + extent_x, 1 + b : 1 + b + extent_y, 1 + d : 1 + d + extent_z]
        columns.append(jnp.sum(shifted.astype(jnp.float32) * grad_float, axis=(1, 2, 3)))
    return columns


def pointwise(weights, source):
    layout = source.shape
    flattened = source.reshape(layout[0], -1)
    return jnp.dot(weights.T, flattened, preferred_element_type=jnp.float32).reshape(layout)


def backmap(weights, source):
    layout = source.shape
    flattened = source.reshape(layout[0], -1)
    return jnp.dot(weights, flattened, preferred_element_type=jnp.float32).reshape(layout)


def contract_cells(left, right):
    channels = left.shape[0]
    return lax.dot_general(
        left.reshape(channels, -1),
        right.reshape(channels, -1),
        (((1,), (1,)), ((), ())),
        preferred_element_type=jnp.float32,
    )


def reduce_plan(space_size):
    if space_size == 128:
        scatter = ((("own", 0, 2), ("space", 1, 2)), (("space", 2, 2), ("space", 4, 4)))
        return scatter, (("space", 16, 8),)
    factors, stride, rest = [], 1, space_size
    while rest > 2:
        factors.append(("space", stride, 2))
        stride, rest = stride * 2, rest // 2
    scatter = ((("own", 0, 2),) + tuple(factors[:1]),) + tuple((f,) for f in factors[1:])
    return scatter, (("space", stride, rest),)


def group_size(group):
    return math.prod(f[2] for f in group)


def reduce_kernel(plan, x_ref, o_ref, *refs):
    scatter, last = plan
    count = len(scatter)
    bufs = refs[:count]
    recvs = refs[count : 2 * count]
    recv_last, res, send_sem, recv_sem = refs[2 * count :]
    own = lax.axis_index("own")
    space = lax.axis_index("space")

    def coord(factor):
        axis, stride, size = factor
        return own if axis == "own" else (space // stride) % size

    def member(group):
        index = 0
        for factor in group:
            index = index * factor[2] + coord(factor)
        return index

    def device(group, target):
        new_own, new_space = own, space
        for factor in reversed(group):
            axis, stride, size = factor
            value = target % size
            target = target // size
            if axis == "own":
                new_own = value
            else:
                new_space = new_space + (value - coord(factor)) * stride
        return (new_own, new_space)

    barrier = pltpu.get_barrier_semaphore()
    partners = 0
    for group in scatter + (last,):
        size, me = group_size(group), member(group)
        for d in range(1, size):
            pl.semaphore_signal(
                barrier, 1, device_id=device(group, (me + d) % size), device_id_type=MESH
            )
            partners += 1
    pl.semaphore_wait(barrier, partners)

    def exchange(group, base, source_of, dest_of):
        size, me = group_size(group), member(group)
        sends = []
        for d in range(1, size):
            target = (me + d) % size
            copy = pltpu.make_async_remote_copy(
                src_ref=source_of(target),
                dst_ref=dest_of(me),
                send_sem=send_sem.at[base + target],
                recv_sem=recv_sem.at[base + me],
                device_id=device(group, target),
                device_id_type=MESH,
            )
            copy.start()
            sends.append(copy)
        return sends

    def finish(group, base, source_of, dest_of, sends):
        size, me = group_size(group), member(group)
        for d in range(1, size):
            sender = (me + d) % size
            pltpu.make_async_remote_copy(
                src_ref=source_of(sender),
                dst_ref=dest_of(sender),
                send_sem=send_sem.at[base + sender],
                recv_sem=recv_sem.at[base + sender],
                device_id=device(group, sender),
                device_id_type=MESH,
            ).wait_recv()
        for copy in sends:
            copy.wait_send()

    base = 0
    source = x_ref
    for i, group in enumerate(scatter):
        size, me = group_size(group), member(group)
        piece = source.shape[0] // size
        src_of = lambda t, s=source, n=piece: s.at[pl.ds(t * n, n)]
        dst_of = lambda t, r=recvs[i]: r.at[t]
        sends = exchange(group, base, src_of, dst_of)
        finish(group, base, src_of, dst_of, sends)
        total = source[pl.ds(me * piece, piece)]
        for d in range(1, size):
            total = total + recvs[i][(me + d) % size]
        bufs[i][...] = total
        source = bufs[i]
        base += size

    size, me = group_size(last), member(last)
    piece = source.shape[0]
    src_of = lambda t, s=source: s
    dst_of = lambda t: recv_last.at[t]
    sends = exchange(last, base, src_of, dst_of)
    recv_last[me] = source[...]
    finish(last, base, src_of, dst_of, sends)
    total = recv_last[0]
    for k in range(1, size):
        total = total + recv_last[k]
    space_factors = [f for group in scatter for f in group if f[0] != "own"]
    block = 0
    for factor in space_factors:
        block = block * factor[2] + coord(factor)
    res[pl.ds(block * piece, piece)] = total
    base += size

    span = piece
    gathers = [tuple(f for group in scatter for f in group if f[0] != "own")]
    for j in range(len(gathers) - 1, -1, -1):
        group = gathers[j]
        if not group:
            continue
        size, me = group_size(group), member(group)
        prefix = 0
        for earlier in gathers[:j]:
            prefix = prefix * group_size(earlier) + member(earlier)
        start = prefix * size * span
        src_of = lambda t, a=start, n=span: res.at[pl.ds(a + t * n, n)]
        sends = []
        for d in range(1, size):
            target = (me + d) % size
            copy = pltpu.make_async_remote_copy(
                src_ref=src_of(me),
                dst_ref=src_of(me),
                send_sem=send_sem.at[base + target],
                recv_sem=recv_sem.at[base + me],
                device_id=device(group, target),
                device_id_type=MESH,
            )
            copy.start()
            sends.append(copy)
        finish(group, base, src_of, src_of, sends)
        span *= size
        base += size
    o_ref[...] = res[...]


def tree_reduce(packed):
    plan = reduce_plan(lax.axis_size("space"))
    scatter, last = plan
    half = packed.shape[0] // 2
    shapes, length = [], packed.shape[0]
    for group in scatter:
        length //= group_size(group)
        shapes.append((group_size(group), length))
    semaphores = sum(group_size(group) for group in scatter) + group_size(last) + math.prod(
        f[2] for group in scatter for f in group if f[0] != "own"
    )
    scratch = [pltpu.VMEM((n, 8, 128), jnp.float32) for _, n in shapes]
    scratch += [pltpu.VMEM((size, n, 8, 128), jnp.float32) for size, n in shapes]
    scratch += [
        pltpu.VMEM((group_size(last), length, 8, 128), jnp.float32),
        pltpu.VMEM((half, 8, 128), jnp.float32),
        pltpu.SemaphoreType.DMA((semaphores,)),
        pltpu.SemaphoreType.DMA((semaphores,)),
    ]
    return pl.pallas_call(
        functools.partial(reduce_kernel, plan),
        out_shape=jax.ShapeDtypeStruct((half, 8, 128), jnp.float32),
        in_specs=[pl.BlockSpec(memory_space=pltpu.VMEM)],
        out_specs=pl.BlockSpec(memory_space=pltpu.VMEM),
        scratch_shapes=scratch,
        compiler_params=pltpu.CompilerParams(collective_id=0, has_side_effects=True),
        cost_estimate=pl.CostEstimate(
            flops=0, transcendentals=0, bytes_accessed=64 * packed.size * 4
        ),
    )(packed)


def tiled(block):
    rows, cols = block.shape
    return block.reshape(rows // 8, 8, cols // 128, 128).transpose(0, 2, 1, 3).reshape(-1, 8, 128)


def untiled(tiles, rows, cols):
    return tiles.reshape(rows // 8, cols // 128, 8, 128).transpose(0, 2, 1, 3).reshape(rows, cols)


def pack_halves(parts, blocks):
    halves = []
    for h in range(2):
        tiles = []
        for p in parts[:2]:
            rows = p.shape[0] // 2
            tiles.append(tiled(p[h * rows : (h + 1) * rows]))
        tail = []
        for columns in parts[2:]:
            cols = columns[0].shape[0] // 2
            tail.extend(column[h * cols : (h + 1) * cols] for column in columns)
        tail = jnp.concatenate(tail)
        head = sum(t.shape[0] for t in tiles)
        total = -(-(head + -(-tail.shape[0] // TILE)) // blocks) * blocks
        tail = jnp.pad(tail, (0, (total - head) * TILE - tail.shape[0]))
        halves.append(jnp.concatenate(tiles + [tail.reshape(-1, 8, 128)]))
    return jnp.concatenate(halves), None


def unpack_half(reduced, parts):
    out, offset = [], 0
    for p in parts[:2]:
        rows, cols = p.shape[0] // 2, p.shape[1]
        count = rows * cols // TILE
        out.append(untiled(reduced[offset : offset + count], rows, cols))
        offset += count
    flat = reduced[offset:].reshape(-1)
    offset = 0
    for columns in parts[2:]:
        shape = (len(columns), columns[0].shape[0] // 2)
        out.append(flat[offset : offset + shape[0] * shape[1]].reshape(shape))
        offset += shape[0] * shape[1]
    return out


def shards(density, cotangent, pw_one, pw_two, dw_one, dw_two):
    channels, extent_x, extent_y, extent_z = density.shape
    assert lax.axis_size("own") == 2
    weight_one, weight_two, taps_one, taps_two = gather_weights(pw_one, pw_two, dw_one, dw_two)
    rim_width = 1
    wide_input = extended(density, (("own", 1), ("space", 2)), rim_width)
    grad_second = backmap(weight_two, cotangent).astype(jnp.bfloat16)
    second_padded = extended(grad_second, (("own", 1), ("space", 2)), 1)
    first = depthwise(wide_input, taps_one, extent_x, extent_y, 1).astype(jnp.bfloat16)
    pre = pointwise(weight_one, first)
    second_padded, pre = lax.optimization_barrier((second_padded, pre))
    act = jax.nn.silu(pre).astype(jnp.bfloat16)
    act_padded = extended(act, (("own", 1), ("space", 2)), 1)
    second = depthwise(act_padded, taps_two, extent_x, extent_y, 1).astype(jnp.bfloat16)
    sigma = jax.nn.sigmoid(pre)
    grad_pre = (
        depthwise(second_padded, taps_two, extent_x, extent_y, -1)
        * (sigma * (1.0 + pre * (1.0 - sigma)))
    ).astype(jnp.bfloat16)
    grad_first = backmap(weight_one, grad_pre).astype(jnp.bfloat16)
    first_padded = extended(grad_first, (("own", 1), ("space", 2)), 1)
    grad_input = (
        cotangent.astype(jnp.float32) + depthwise(first_padded, taps_one, extent_x, extent_y, -1)
    ).astype(jnp.bfloat16)
    total_cells = extent_x * extent_y * extent_z * lax.axis_size("own") * lax.axis_size("space")
    grad_scale = 1.0 / math.sqrt(float(total_cells))
    local_pw_one = contract_cells(first, grad_pre) * grad_scale
    local_pw_two = contract_cells(second, cotangent) * grad_scale
    local_dw_one = [column * grad_scale for column in tap_sums(wide_input, grad_first)]
    local_dw_two = [column * grad_scale for column in tap_sums(act_padded, grad_second)]
    partials = (local_pw_one, local_pw_two, local_dw_one, local_dw_two)
    scatter, _ = reduce_plan(lax.axis_size("space"))
    blocks = math.prod(f[2] for group in scatter for f in group if f[0] != "own")
    packed, _ = pack_halves(partials, blocks)
    result = unpack_half(tree_reduce(packed), partials)
    return (grad_input, result[0], result[1], result[2], result[3])


def solution(mesh):
    in_specs = (
        P(None, "own", "space", None),
        P(None, "own", "space", None),
        P("own", None),
        P("own", None),
        P(None, "own"),
        P(None, "own"),
    )
    out_specs = (
        P(None, "own", "space", None),
        P("own", None),
        P("own", None),
        P(None, "own"),
        P(None, "own"),
    )
    return jax.shard_map(shards, mesh=mesh, in_specs=in_specs, out_specs=out_specs, check_vma=False)
```

```python
import functools
import math

import jax
import jax.numpy as jnp
from jax import lax
from jax.experimental import pallas as pl
from jax.experimental.pallas import tpu as pltpu
from jax.sharding import PartitionSpec as P

MESH = pl.DeviceIdType.MESH
TILE = 8 * 128

TAP_LIST = [
    (9 * (a + 1) + 3 * (b + 1) + (d + 1), a, b, d)
    for a in (-1, 0, 1)
    for b in (-1, 0, 1)
    for d in (-1, 0, 1)
]


def extended(value, sides, width):
    for axis, dim in sides:
        size, length = (lax.axis_size(axis), value.shape[dim])
        up = [(i, (i + 1) % size) for i in range(size)]
        down = [(j, i) for i, j in up]
        last = lax.slice_in_dim(value, length - width, length, axis=dim)
        first = lax.slice_in_dim(value, 0, width, axis=dim)
        if size == 2:
            theirs = lax.ppermute(jnp.concatenate([first, last], axis=dim), axis, up)
            after = lax.slice_in_dim(theirs, 0, width, axis=dim)
            before = lax.slice_in_dim(theirs, width, 2 * width, axis=dim)
        else:
            before = lax.ppermute(last, axis, up)
            after = lax.ppermute(first, axis, down)
        value = jnp.concatenate([before, value, after], axis=dim)
    return value


def gather_weights(pw_one, pw_two, dw_one, dw_two):
    mine = jnp.concatenate([pw_one.reshape(-1), pw_two.reshape(-1), dw_one.reshape(-1), dw_two.reshape(-1)])
    theirs = lax.ppermute(mine, "own", [(0, 1), (1, 0)])
    first_half = lax.axis_index("own") == 0
    low = jnp.where(first_half, mine, theirs)
    high = jnp.where(first_half, theirs, mine)
    out, offset = [], 0
    for w, dim in ((pw_one, 0), (pw_two, 0), (dw_one, 1), (dw_two, 1)):
        count = w.size
        parts = [h[offset : offset + count].reshape(w.shape) for h in (low, high)]
        out.append(jnp.concatenate(parts, axis=dim))
        offset += count
    return out


def ring_z(padded):
    return jnp.concatenate([padded[..., -1:], padded, padded[..., :1]], axis=3)


def depthwise(padded, weights, extent_x, extent_y, direction):
    extent_z = padded.shape[3]
    wide = ring_z(padded)
    running = jnp.zeros((padded.shape[0], extent_x, extent_y, extent_z), jnp.float32)
    for k, a, b, d in TAP_LIST:
        start_x = 1 + direction * a
        start_y = 1 + direction * b
        start_z = 1 + direction * d
        shifted = wide[:, start_x : start_x + extent_x, start_y : start_y + extent_y, start_z : start_z + extent_z]
        running = running + weights[k].astype(jnp.float32)[:, None, None, None] * shifted.astype(jnp.float32)
    return running


def tap_sums(padded, gradient):
    extent_x, extent_y, extent_z = gradient.shape[1:]
    wide = ring_z(padded)
    grad_float = gradient.astype(jnp.float32)
    columns = []
    for k, a, b, d in TAP_LIST:
        shifted = wide[:, 1 + a : 1 + a + extent_x, 1 + b : 1 + b + extent_y, 1 + d : 1 + d + extent_z]
        columns.append(jnp.sum(shifted.astype(jnp.float32) * grad_float, axis=(1, 2, 3)))
    return columns


def pointwise(weights, source):
    layout = source.shape
    flattened = source.reshape(layout[0], -1)
    return jnp.dot(weights.T, flattened, preferred_element_type=jnp.float32).reshape(layout)


def backmap(weights, source):
    layout = source.shape
    flattened = source.reshape(layout[0], -1)
    return jnp.dot(weights, flattened, preferred_element_type=jnp.float32).reshape(layout)


def contract_cells(left, right):
    channels = left.shape[0]
    return lax.dot_general(
        left.reshape(channels, -1),
        right.reshape(channels, -1),
        (((1,), (1,)), ((), ())),
        preferred_element_type=jnp.float32,
    )


def reduce_plan(space_size):
    if space_size == 128:
        scatter = ((("own", 0, 2), ("space", 1, 2)), (("space", 2, 2), ("space", 4, 4)))
        return scatter, (("space", 16, 8),)
    factors, stride, rest = [], 1, space_size
    while rest > 2:
        factors.append(("space", stride, 2))
        stride, rest = stride * 2, rest // 2
    scatter = ((("own", 0, 2),) + tuple(factors[:1]),) + tuple((f,) for f in factors[1:])
    return scatter, (("space", stride, rest),)


def group_size(group):
    return math.prod(f[2] for f in group)


def reduce_kernel(plan, x_ref, o_ref, *refs):
    scatter, last = plan
    count = len(scatter)
    bufs = refs[:count]
    recvs = refs[count : 2 * count]
    recv_last, res, send_sem, recv_sem = refs[2 * count :]
    own = lax.axis_index("own")
    space = lax.axis_index("space")

    def coord(factor):
        axis, stride, size = factor
        return own if axis == "own" else (space // stride) % size

    def member(group):
        index = 0
        for factor in group:
            index = index * factor[2] + coord(factor)
        return index

    def device(group, target):
        new_own, new_space = own, space
        for factor in reversed(group):
            axis, stride, size = factor
            value = target % size
            target = target // size
            if axis == "own":
                new_own = value
            else:
                new_space = new_space + (value - coord(factor)) * stride
        return (new_own, new_space)

    barrier = pltpu.get_barrier_semaphore()
    partners = 0
    for group in scatter + (last,):
        size, me = group_size(group), member(group)
        for d in range(1, size):
            pl.semaphore_signal(
                barrier, 1, device_id=device(group, (me + d) % size), device_id_type=MESH
            )
            partners += 1
    pl.semaphore_wait(barrier, partners)

    def exchange(group, base, source_of, dest_of):
        size, me = group_size(group), member(group)
        sends = []
        for d in range(1, size):
            target = (me + d) % size
            copy = pltpu.make_async_remote_copy(
                src_ref=source_of(target),
                dst_ref=dest_of(me),
                send_sem=send_sem.at[base + target],
                recv_sem=recv_sem.at[base + me],
                device_id=device(group, target),
                device_id_type=MESH,
            )
            copy.start()
            sends.append(copy)
        return sends

    def finish(group, base, source_of, dest_of, sends):
        size, me = group_size(group), member(group)
        for d in range(1, size):
            sender = (me + d) % size
            pltpu.make_async_remote_copy(
                src_ref=source_of(sender),
                dst_ref=dest_of(sender),
                send_sem=send_sem.at[base + sender],
                recv_sem=recv_sem.at[base + sender],
                device_id=device(group, sender),
                device_id_type=MESH,
            ).wait_recv()
        for copy in sends:
            copy.wait_send()

    base = 0
    source = x_ref
    for i, group in enumerate(scatter):
        size, me = group_size(group), member(group)
        piece = source.shape[0] // size
        src_of = lambda t, s=source, n=piece: s.at[pl.ds(t * n, n)]
        dst_of = lambda t, r=recvs[i]: r.at[t]
        sends = exchange(group, base, src_of, dst_of)
        finish(group, base, src_of, dst_of, sends)
        total = source[pl.ds(me * piece, piece)]
        for d in range(1, size):
            total = total + recvs[i][(me + d) % size]
        bufs[i][...] = total
        source = bufs[i]
        base += size

    size, me = group_size(last), member(last)
    piece = source.shape[0]
    src_of = lambda t, s=source: s
    dst_of = lambda t: recv_last.at[t]
    sends = exchange(last, base, src_of, dst_of)
    recv_last[me] = source[...]
    finish(last, base, src_of, dst_of, sends)
    total = recv_last[0]
    for k in range(1, size):
        total = total + recv_last[k]
    space_factors = [f for group in scatter for f in group if f[0] != "own"]
    block = 0
    for factor in space_factors:
        block = block * factor[2] + coord(factor)
    res[pl.ds(block * piece, piece)] = total
    base += size

    span = piece
    gathers = [tuple(f for group in scatter for f in group if f[0] != "own")]
    for j in range(len(gathers) - 1, -1, -1):
        group = gathers[j]
        if not group:
            continue
        size, me = group_size(group), member(group)
        prefix = 0
        for earlier in gathers[:j]:
            prefix = prefix * group_size(earlier) + member(earlier)
        start = prefix * size * span
        src_of = lambda t, a=start, n=span: res.at[pl.ds(a + t * n, n)]
        sends = []
        for d in range(1, size):
            target = (me + d) % size
            copy = pltpu.make_async_remote_copy(
                src_ref=src_of(me),
                dst_ref=src_of(me),
                send_sem=send_sem.at[base + target],
                recv_sem=recv_sem.at[base + me],
                device_id=device(group, target),
                device_id_type=MESH,
            )
            copy.start()
            sends.append(copy)
        finish(group, base, src_of, src_of, sends)
        span *= size
        base += size
    o_ref[...] = res[...]


def tree_reduce(packed):
    plan = reduce_plan(lax.axis_size("space"))
    scatter, last = plan
    half = packed.shape[0] // 2
    shapes, length = [], packed.shape[0]
    for group in scatter:
        length //= group_size(group)
        shapes.append((group_size(group), length))
    semaphores = sum(group_size(group) for group in scatter) + group_size(last) + math.prod(
        f[2] for group in scatter for f in group if f[0] != "own"
    )
    scratch = [pltpu.VMEM((n, 8, 128), jnp.float32) for _, n in shapes]
    scratch += [pltpu.VMEM((size, n, 8, 128), jnp.float32) for size, n in shapes]
    scratch += [
        pltpu.VMEM((group_size(last), length, 8, 128), jnp.float32),
        pltpu.VMEM((half, 8, 128), jnp.float32),
        pltpu.SemaphoreType.DMA((semaphores,)),
        pltpu.SemaphoreType.DMA((semaphores,)),
    ]
    return pl.pallas_call(
        functools.partial(reduce_kernel, plan),
        out_shape=jax.ShapeDtypeStruct((half, 8, 128), jnp.float32),
        in_specs=[pl.BlockSpec(memory_space=pltpu.VMEM)],
        out_specs=pl.BlockSpec(memory_space=pltpu.VMEM),
        scratch_shapes=scratch,
        compiler_params=pltpu.CompilerParams(collective_id=0, has_side_effects=True),
        cost_estimate=pl.CostEstimate(
            flops=0, transcendentals=0, bytes_accessed=64 * packed.size * 4
        ),
    )(packed)


def tiled(block):
    rows, cols = block.shape
    return block.reshape(rows // 8, 8, cols // 128, 128).transpose(0, 2, 1, 3).reshape(-1, 8, 128)


def untiled(tiles, rows, cols):
    return tiles.reshape(rows // 8, cols // 128, 8, 128).transpose(0, 2, 1, 3).reshape(rows, cols)


def pack_halves(parts, blocks):
    halves = []
    for h in range(2):
        tiles = []
        for p in parts[:2]:
            rows = p.shape[0] // 2
            tiles.append(tiled(p[h * rows : (h + 1) * rows]))
        tail = []
        for columns in parts[2:]:
            cols = columns[0].shape[0] // 2
            tail.extend(column[h * cols : (h + 1) * cols] for column in columns)
        tail = jnp.concatenate(tail)
        head = sum(t.shape[0] for t in tiles)
        total = -(-(head + -(-tail.shape[0] // TILE)) // blocks) * blocks
        tail = jnp.pad(tail, (0, (total - head) * TILE - tail.shape[0]))
        halves.append(jnp.concatenate(tiles + [tail.reshape(-1, 8, 128)]))
    return jnp.concatenate(halves), None


def unpack_half(reduced, parts):
    out, offset = [], 0
    for p in parts[:2]:
        rows, cols = p.shape[0] // 2, p.shape[1]
        count = rows * cols // TILE
        out.append(untiled(reduced[offset : offset + count], rows, cols))
        offset += count
    flat = reduced[offset:].reshape(-1)
    offset = 0
    for columns in parts[2:]:
        shape = (len(columns), columns[0].shape[0] // 2)
        out.append(flat[offset : offset + shape[0] * shape[1]].reshape(shape))
        offset += shape[0] * shape[1]
    return out


def shards(density, cotangent, pw_one, pw_two, dw_one, dw_two):
    channels, extent_x, extent_y, extent_z = density.shape
    assert lax.axis_size("own") == 2
    weight_one, weight_two, taps_one, taps_two = gather_weights(pw_one, pw_two, dw_one, dw_two)
    rim_width = 1
    wide_input = extended(density, (("own", 1), ("space", 2)), rim_width)
    grad_second = backmap(weight_two, cotangent).astype(jnp.bfloat16)
    grad_second, wide_input = lax.optimization_barrier((grad_second, wide_input))
    second_padded = extended(grad_second, (("own", 1), ("space", 2)), 1)
    first = depthwise(wide_input, taps_one, extent_x, extent_y, 1).astype(jnp.bfloat16)
    pre = pointwise(weight_one, first)
    second_padded, pre = lax.optimization_barrier((second_padded, pre))
    act = jax.nn.silu(pre).astype(jnp.bfloat16)
    act_padded = extended(act, (("own", 1), ("space", 2)), 1)
    second = depthwise(act_padded, taps_two, extent_x, extent_y, 1).astype(jnp.bfloat16)
    sigma = jax.nn.sigmoid(pre)
    grad_pre = (
        depthwise(second_padded, taps_two, extent_x, extent_y, -1)
        * (sigma * (1.0 + pre * (1.0 - sigma)))
    ).astype(jnp.bfloat16)
    grad_first = backmap(weight_one, grad_pre).astype(jnp.bfloat16)
    first_padded = extended(grad_first, (("own", 1), ("space", 2)), 1)
    grad_input = (
        cotangent.astype(jnp.float32) + depthwise(first_padded, taps_one, extent_x, extent_y, -1)
    ).astype(jnp.bfloat16)
    total_cells = extent_x * extent_y * extent_z * lax.axis_size("own") * lax.axis_size("space")
    grad_scale = 1.0 / math.sqrt(float(total_cells))
    local_pw_one = contract_cells(first, grad_pre) * grad_scale
    local_pw_two = contract_cells(second, cotangent) * grad_scale
    local_dw_one = [column * grad_scale for column in tap_sums(wide_input, grad_first)]
    local_dw_two = [column * grad_scale for column in tap_sums(act_padded, grad_second)]
    partials = (local_pw_one, local_pw_two, local_dw_one, local_dw_two)
    scatter, _ = reduce_plan(lax.axis_size("space"))
    blocks = math.prod(f[2] for group in scatter for f in group if f[0] != "own")
    packed, _ = pack_halves(partials, blocks)
    result = unpack_half(tree_reduce(packed), partials)
    return (grad_input, result[0], result[1], result[2], result[3])


def solution(mesh):
    in_specs = (
        P(None, "own", "space", None),
        P(None, "own", "space", None),
        P("own", None),
        P("own", None),
        P(None, "own"),
        P(None, "own"),
    )
    out_specs = (
        P(None, "own", "space", None),
        P("own", None),
        P("own", None),
        P(None, "own"),
        P(None, "own"),
    )
    return jax.shard_map(shards, mesh=mesh, in_specs=in_specs, out_specs=out_specs, check_vma=False)
```
